32 devices in a mesh: dp: 4 (over x, core), expert: 8 (over z, y).
Axes of the slice: x: 2, y: 2, z: 4, core: 2. Of those that a mesh axis runs over, the one named last changes fastest.
Arguments:
- tokens: bfloat16 [32768, 768], P(('dp', 'expert')), may hold values from -6 to 6
- routing: int32 [32768, 1], P(('dp', 'expert')), may hold values from 0 to 7; in each aligned block of 1024 rows (0 to 1023, 1024 to 2047, ...) at most 256 rows name the same one
- query_weight: bfloat16 [768, 768], replicated, may hold values from -0.3125 to 0.3125
- key_weight: bfloat16 [768, 768], replicated, may hold values from -0.3125 to 0.3125
- value_weight: bfloat16 [768, 768], replicated, may hold values from -0.21875 to 0.21875
- output_weight: bfloat16 [768, 768], replicated, may hold values from -0.625 to 0.625
- first_gain: float32 [768], replicated, may hold values from 0.25 to 1.75
- first_bias: float32 [768], replicated, may hold values from -1.2 to 1.2
- second_gain: float32 [768], replicated, may hold values from 0.25 to 1.75
- second_bias: float32 [768], replicated, may hold values from -1.2 to 1.2
- centroids: float32 [8, 768], replicated, may hold values from -0.18 to 0.18
- expert_up: bfloat16 [8, 768, 3072], P('expert'), may hold values from -0.21875 to 0.21875
- expert_down: bfloat16 [8, 3072, 768], P('expert'), may hold values from -0.3125 to 0.3125
- cotangent: bfloat16 [32768, 768], P(('dp', 'expert')), may hold values from -6 to 6
Outputs:
- layer_out: bfloat16 [32768, 768], P(('dp', 'expert'))
- grad_tokens: float32 [32768, 768], P(('dp', 'expert'))
- grad_query: float32 [768, 768], replicated
- grad_key: float32 [768, 768], replicated
- grad_value: float32 [768, 768], replicated
- grad_output: float32 [768, 768], replicated
- grad_first_gain: float32 [768], replicated
- grad_first_bias: float32 [768], replicated
- grad_second_gain: float32 [768], replicated
- grad_second_bias: float32 [768], replicated
- grad_up: float32 [8, 768, 3072], P('expert', None, 'dp')
- grad_down: float32 [8, 3072, 768], P('expert', 'dp')
The draws below stay inside these ranges and needn't reach their ends.
Inputs may be any that keep to these rules, and one draw needn't show every extreme that they name: `routing`: each token names one expert. Among the 1024 tokens of one device no expert is named more than 256 times, and in some device's tokens one expert is named exactly 256 times.
All inputs are finite; a program needn't handle non-finite values.
Results may differ from the reference program's by a relative error of at most 0.014.
The reference program's roundings to bfloat16 on the way count: a program that leaves them out, or rounds other values in their place, can miss the bound.
Values may be sent and summed in bfloat16 or wider, within the bound.
No kernel may reach another device: no remote copies, remote signals or barrier semaphores. Data moves between devices by JAX's collectives and lax.ppermute only.
A program may use at most 256 MiB of HBM per device.

```python
import math
import jax
import jax.numpy as jnp
import numpy as np
from jax import lax

D = 768
HEADS = 12
HEAD = 64
FF = 3072
TOK_DEV = 1024
EXPERTS = 8
TOKENS = 32768
CAP = 128
MOST = 256


def steps_of(rng, shape, shards, smallest, high):
    def one(dim, parts):
        draws = jax.random.uniform(jax.random.fold_in(jax.random.fold_in(rng, 6), dim), (parts,), jnp.float32, smallest / len(shards), high / len(shards))
        return jnp.repeat(jnp.exp(draws), shape[dim] // parts).reshape((-1,) + (1,) * (len(shape) - dim - 1))

    loudness = one(*shards[0])
    for cut in shards[1:]:
        loudness = loudness * one(*cut)
    return loudness


def deal_out(key, own, number, rows, amount, top, most, skew):
    ranking = jax.random.permutation(key, amount)
    heavy_load, usual = shares(amount, rows * top, most, skew, True), shares(amount, rows * top, most, skew, False)
    places = jnp.arange(amount)

    def named(tallies, offset_by):
        used = int((tallies > 0).sum())
        fixed = max(1, used // 4)
        moved = fixed + (places - fixed + offset_by * (used - fixed)) % max(1, amount - fixed)
        return jnp.zeros((amount,), jnp.int32).at[ranking[jnp.where(places < fixed, places, moved)]].set(jnp.asarray(tallies, jnp.int32))

    tallies = jnp.where(number % 4 == 0, named(heavy_load, number // 4), named(usual, number - number // 4 - 1))
    mixed = jax.random.permutation(jax.random.fold_in(own, 3), amount)
    donor, receiver = mixed[0:amount // 2 * 2:2], mixed[1:amount // 2 * 2:2]
    margin = jnp.minimum(tallies[donor] - 1, most - tallies[receiver]) // 2
    margin = jnp.where((donor == ranking[0]) | (receiver == ranking[0]) | (tallies[receiver] == 0), 0, jnp.maximum(margin, 0))
    moved = jax.random.randint(jax.random.fold_in(own, 4), (amount // 2,), 0, 1 << 20) % (margin + 1)
    tallies = tallies.at[donor].add(-moved).at[receiver].add(moved)
    members = jnp.searchsorted(jnp.cumsum(tallies), jnp.arange(rows * top), side="right").astype(jnp.int32)
    listing = members.reshape(top, rows).T
    listing = listing[jax.random.permutation(jax.random.fold_in(own, 1), rows)]
    offset_by = jax.random.randint(jax.random.fold_in(own, 2), (rows, 1), 0, top)
    return jnp.take_along_axis(listing, (jnp.arange(top)[None, :] + offset_by) % top, axis=1)


def shares(count, total, bound, lean, full):
    weights = [(1 << 20) // math.isqrt(grade ** lean) + 1 for grade in range(1, count + 1)]
    largest = bound if full else min(bound, max(-(-total // count), total * weights[0] // sum(weights)))
    least = 1 if total - largest >= count - 1 else 0
    holding, surplus = [largest] + [least] * (count - 1), total - largest - least * (count - 1)
    while surplus > 0:
        candidates = [i for i in range(1, count) if holding[i] < largest] or [i for i in range(1, count) if holding[i] < bound]
        pool, budget = sum([weights[i] for i in candidates]), surplus
        for i in candidates:
            addition = min(bound - holding[i], max(1, budget * weights[i] // pool), surplus)
            holding[i] = holding[i] + addition
            surplus = surplus - addition
    return np.array(holding)


def bell_draw(rng, extent, scale, reach, split=(), kind=jnp.bfloat16):
    array = scale * jax.random.normal(rng, extent, jnp.float32)
    if split:
        array = array * steps_of(rng, extent, split, -0.22, 0.18)
    return jnp.clip(array, -reach, reach).astype(kind)


def setup_inputs(seed: int = 0) -> dict:
    key_list = jax.random.split(jax.random.key(seed), 15)
    tokens = bell_draw(key_list[0], (TOKENS, D), 1.0, 6.0, ((0, 32),))
    routing_keys = jax.random.split(jax.random.fold_in(key_list[1], 1), TOKENS // TOK_DEV)
    routing_turns = jax.random.permutation(jax.random.fold_in(key_list[1], 3), TOKENS // TOK_DEV)
    routing = jax.vmap(lambda own, number: deal_out(jax.random.fold_in(key_list[1], 2), own, number, TOK_DEV, EXPERTS, 1, MOST, 2))(routing_keys, routing_turns).reshape((TOKENS, 1))
    query_weight = bell_draw(key_list[2], (D, D), (D // 2) ** -0.5, 0.3125)
    key_weight = bell_draw(key_list[3], (D, D), (D // 2) ** -0.5, 0.3125)
    value_weight = bell_draw(key_list[4], (D, D), D ** -0.5, 0.21875)
    output_weight = bell_draw(key_list[5], (D, D), (D // 8) ** -0.5, 0.625)
    first_gain = jnp.clip(1.0 + 0.15 * jax.random.normal(key_list[6], (D,), jnp.float32), 0.25, 1.75)
    first_bias = bell_draw(key_list[7], (D,), 0.3, 1.2, (), jnp.float32)
    second_gain = jnp.clip(1.0 + 0.15 * jax.random.normal(key_list[8], (D,), jnp.float32), 0.25, 1.75)
    second_bias = bell_draw(key_list[9], (D,), 0.3, 1.2, (), jnp.float32)
    centroids = bell_draw(key_list[10], (EXPERTS, D), 0.03, 0.18, (), jnp.float32)
    expert_up = bell_draw(key_list[11], (EXPERTS, D, FF), D ** -0.5, 0.21875, ((0, 8),))
    expert_down = bell_draw(key_list[12], (EXPERTS, FF, D), (FF // 9) ** -0.5, 0.3125, ((0, 8),))
    cotangent = bell_draw(key_list[13], (TOKENS, D), 1.0, 6.0, ((0, 32),))
    return {"tokens": tokens, "routing": routing, "query_weight": query_weight, "key_weight": key_weight, "value_weight": value_weight, "output_weight": output_weight, "first_gain": first_gain, "first_bias": first_bias, "second_gain": second_gain, "second_bias": second_bias, "centroids": centroids, "expert_up": expert_up, "expert_down": expert_down, "cotangent": cotangent}


highest = lax.Precision.HIGHEST

@jax.custom_vjp
def low(v):
    return lax.optimization_barrier(v.astype(jnp.bfloat16)).astype(jnp.float32)

@jax.custom_vjp
def low_back(v):
    return v

def low_keep(v):
    return (low(v), None)

def low_pass(kept, grad):
    return (grad,)

def back_keep(v):
    return (v, None)

def back_low(kept, grad):
    return (low(grad),)
low.defvjp(low_keep, low_pass)
low_back.defvjp(back_keep, back_low)

def normalize(values, gain, bias):
    centered = values - lax.optimization_barrier(jnp.mean(values, axis=-1, keepdims=True))
    variance = lax.optimization_barrier(jnp.mean(centered * centered, axis=-1, keepdims=True))
    return centered * lax.rsqrt(variance + 1e-05) * gain + bias

def attend(packed):
    queries, keys, values = packed
    scores = jnp.einsum('qhd,khd->hqk', queries, keys, precision=highest) * HEAD ** (-0.5)
    scores = low_back(scores)
    length = queries.shape[0]
    causal = jnp.arange(length)[:, None] >= jnp.arange(length)[None, :]
    scores = jnp.where(causal[None], scores, -1e+30)
    probs = low(jax.nn.softmax(scores, axis=-1))
    return jnp.einsum('hqk,khd->qhd', probs, values, precision=highest)

def expert_apply(packed):
    rows, up_matrix, down_matrix = packed
    pre_act = low_back(jnp.dot(rows, up_matrix, precision=highest))
    hidden = low(jax.nn.gelu(pre_act, approximate=False))
    return low_back(low(jnp.dot(hidden, down_matrix, precision=highest)))

def reference(tokens, routing, query_weight, key_weight, value_weight, output_weight, first_gain, first_bias, second_gain, second_bias, centroids, expert_up, expert_down, cotangent):
    groups = TOKENS // TOK_DEV
    chosen = routing[:, 0].reshape(groups, TOK_DEV)
    one_hot = (chosen[:, :, None] == jnp.arange(EXPERTS, dtype=jnp.int32)[None, None, :]).astype(jnp.int32)
    before = jnp.cumsum(one_hot, axis=1) - one_hot
    position = lax.optimization_barrier(jnp.sum(before * one_hot, axis=2))
    within = position < CAP
    group_index = jnp.arange(groups, dtype=jnp.int32)[:, None]
    slots = chosen * (groups * CAP) + group_index * CAP + position
    slots = jnp.where(within, slots, EXPERTS * groups * CAP).reshape(TOKENS).astype(jnp.int32)
    centroid_rows = centroids[routing[:, 0]]

    def forward(inputs_float, query_matrix, key_matrix, value_matrix, output_matrix, gain_one, bias_one, gain_two, bias_two, up_matrix, down_matrix):
        normed = low(normalize(inputs_float, gain_one, bias_one))
        queries = low_back(low(jnp.dot(normed, query_matrix, precision=highest)))
        keys = low_back(low(jnp.dot(normed, key_matrix, precision=highest)))
        values = low_back(low(jnp.dot(normed, value_matrix, precision=highest)))
        shaped = (queries.reshape(groups, TOK_DEV, HEADS, HEAD), keys.reshape(groups, TOK_DEV, HEADS, HEAD), values.reshape(groups, TOK_DEV, HEADS, HEAD))
        mixed = lax.map(jax.checkpoint(attend), shaped).reshape(TOKENS, D)
        mixed = low_back(low(mixed))
        branch = low_back(jnp.dot(mixed, output_matrix, precision=highest))
        resid = inputs_float + branch
        second = normalize(resid, gain_two, bias_two)
        gating = jax.nn.sigmoid(lax.optimization_barrier(jnp.sum(second * centroid_rows, axis=-1)))
        rows_low = low_back(low(second))
        buffer = jnp.zeros((EXPERTS * groups * CAP + 1, D), jnp.float32).at[slots].add(rows_low)
        buffer = buffer[:-1].reshape(EXPERTS, groups * CAP, D)
        results = lax.map(jax.checkpoint(expert_apply), (buffer, up_matrix, down_matrix))
        padded = jnp.concatenate([results.reshape(EXPERTS * groups * CAP, D), jnp.zeros((1, D), jnp.float32)], axis=0)
        returned = padded[slots]
        return resid + gating[:, None] * returned
    result, pullback = jax.vjp(forward, tokens.astype(jnp.float32), query_weight.astype(jnp.float32), key_weight.astype(jnp.float32), value_weight.astype(jnp.float32), output_weight.astype(jnp.float32), first_gain, first_bias, second_gain, second_bias, expert_up.astype(jnp.float32), expert_down.astype(jnp.float32))
    grads = pullback(cotangent.astype(jnp.float32))
    return (result.astype(jnp.bfloat16), grads[0], grads[1], grads[2], grads[3], grads[4], grads[5], grads[6], grads[7], grads[8], grads[9], grads[10])
```

```python
import functools

import jax
import jax.numpy as jnp
from jax import lax
from jax.experimental import pallas as pl
from jax.experimental.pallas import tpu as pltpu
from jax.sharding import PartitionSpec as P

HEADS = 12
HEAD = 64
LANES = 128
EPS = 1e-05
F32 = jnp.float32
BF16 = jnp.bfloat16


def contract(left, right, left_dim, right_dim):
    return lax.dot_general(
        left, right, (((left_dim,), (right_dim,)), ((), ())), preferred_element_type=F32
    )


def normalize(values, gain, bias):
    centered = values - jnp.mean(values, axis=-1, keepdims=True)
    variance = jnp.mean(centered * centered, axis=-1, keepdims=True)
    scale = lax.rsqrt(variance + EPS)
    xhat = centered * scale
    return xhat * gain + bias, xhat, scale


def normalize_back(grad, xhat, scale, gain):
    scaled = grad * gain
    first = jnp.mean(scaled, axis=-1, keepdims=True)
    cross = jnp.mean(scaled * xhat, axis=-1, keepdims=True)
    return scale * (scaled - first - xhat * cross)


def head_mask(parity, value):
    lane = lax.broadcasted_iota(jnp.int32, (1, LANES), 1)
    return jnp.where(lane // HEAD == parity, value, 0.0).astype(BF16)


def attention_kernel(q_ref, k_ref, v_ref, o_ref, lse_ref, *, block):
    parity = pl.program_id(1)
    length = q_ref.shape[0]
    queries = q_ref[...] * head_mask(parity, HEAD**-0.5)
    values = v_ref[...] * head_mask(parity, 1.0)
    row = lax.broadcasted_iota(jnp.int32, (block, block), 0)
    column = lax.broadcasted_iota(jnp.int32, (block, block), 1)
    outs = []
    for index in range(length // block):
        first, finish = index * block, (index + 1) * block
        scores = contract(queries[first:finish], k_ref[:finish, :], 1, 1)
        diagonal = jnp.where(row >= column, scores[:, first:], -1e30)
        if index:
            scores = jnp.concatenate([scores[:, :first], diagonal], axis=1)
        else:
            scores = diagonal
        top = jnp.max(scores, axis=1, keepdims=True)
        shifted = jnp.exp(scores - top)
        total = jnp.sum(shifted, axis=1, keepdims=True)
        probs = (shifted * (1.0 / total)).astype(BF16)
        outs.append(contract(probs, values[:finish], 1, 0).astype(BF16))
        lse = jnp.broadcast_to(top + jnp.log(total), (block, LANES))
        lse_ref[0, :, first:finish] = jnp.transpose(lse)[0:1, :]
    mixed = jnp.concatenate(outs, axis=0)

    @pl.when(parity == 0)
    def _():
        o_ref[...] = mixed

    @pl.when(parity == 1)
    def _():
        o_ref[...] = o_ref[...] + mixed


def attention(queries, keys, values):
    length, width = queries.shape
    pairs = width // LANES
    block = min(256, length)
    spec = pl.BlockSpec((length, LANES), lambda pair, parity: (0, pair))
    return pl.pallas_call(
        functools.partial(attention_kernel, block=block),
        grid=(pairs, 2),
        in_specs=[spec, spec, spec],
        out_specs=[
            spec,
            pl.BlockSpec((1, 1, length), lambda pair, parity: (pair * 2 + parity, 0, 0)),
        ],
        out_shape=[
            jax.ShapeDtypeStruct((length, width), BF16),
            jax.ShapeDtypeStruct((2 * pairs, 1, length), F32),
        ],
        cost_estimate=pl.CostEstimate(
            flops=2 * length * length * width * 2,
            bytes_accessed=8 * length * width,
            transcendentals=length * length * pairs,
        ),
        name="attention",
    )(queries, keys, values)


def attention_back_kernel(
    q_ref, k_ref, v_ref, g_ref, lse_ref, dq_ref, dk_ref, dv_ref, dk_sum, dv_sum, *, block
):
    parity = pl.program_id(1)
    length = q_ref.shape[0]
    mask = head_mask(parity, 1.0)
    scale_mask = head_mask(parity, HEAD**-0.5)
    queries = q_ref[...] * scale_mask
    grads = g_ref[...] * mask
    keys_scaled = k_ref[...] * scale_mask
    row = lax.broadcasted_iota(jnp.int32, (block, block), 0)
    column = lax.broadcasted_iota(jnp.int32, (block, block), 1)
    dk_sum[...] = jnp.zeros_like(dk_sum)
    dv_sum[...] = jnp.zeros_like(dv_sum)
    dq_parts = []
    for index in range(length // block):
        first, finish = index * block, (index + 1) * block
        scores = contract(k_ref[:finish, :], queries[first:finish], 1, 1)
        diagonal = jnp.where(row <= column, scores[first:], -1e30)
        if index:
            scores = jnp.concatenate([scores[:first], diagonal], axis=0)
        else:
            scores = diagonal
        probs = jnp.exp(scores - lse_ref[0, :, first:finish])
        dv_sum[:finish, :] += contract(probs.astype(BF16), grads[first:finish], 1, 0)
        grad_probs = contract(v_ref[:finish, :], grads[first:finish], 1, 1)
        delta = jnp.sum(probs * grad_probs, axis=0, keepdims=True)
        grad_scores = (probs * (grad_probs - delta)).astype(BF16)
        dk_sum[:finish, :] += contract(grad_scores, queries[first:finish], 1, 0)
        dq_parts.append(contract(grad_scores, keys_scaled[:finish], 0, 0).astype(BF16))
    dq = jnp.concatenate(dq_parts, axis=0)
    dk = dk_sum[...].astype(BF16)
    dv = dv_sum[...].astype(BF16)

    @pl.when(parity == 0)
    def _():
        dq_ref[...] = dq
        dk_ref[...] = dk
        dv_ref[...] = dv

    @pl.when(parity == 1)
    def _():
        dq_ref[...] = dq_ref[...] + dq
        dk_ref[...] = dk_ref[...] + dk
        dv_ref[...] = dv_ref[...] + dv


def attention_back(queries, keys, values, grads, lse, start, pairs):
    length = queries.shape[0]
    block = min(256, length)
    spec = pl.BlockSpec((length, LANES), lambda pair, parity: (0, start + pair))
    out_spec = pl.BlockSpec((length, LANES), lambda pair, parity: (0, pair))
    out = jax.ShapeDtypeStruct((length, pairs * LANES), BF16)
    return pl.pallas_call(
        functools.partial(attention_back_kernel, block=block),
        grid=(pairs, 2),
        in_specs=[
            spec,
            spec,
            spec,
            spec,
            pl.BlockSpec(
                (1, 1, length), lambda pair, parity: ((start + pair) * 2 + parity, 0, 0)
            ),
        ],
        out_specs=[out_spec] * 3,
        out_shape=[out] * 3,
        scratch_shapes=[pltpu.VMEM((length, LANES), F32)] * 2,
        cost_estimate=pl.CostEstimate(
            flops=5 * length * length * pairs * LANES * 2,
            bytes_accessed=14 * length * pairs * LANES,
            transcendentals=length * length * pairs,
        ),
        name="attention_back",
    )(queries, keys, values, grads, lse)


ERF = (0.254829592, -0.284496736, 1.421413741, -1.453152027, 1.061405429)


def gelu_parts(value):
    size = jnp.abs(value)
    t = 1.0 / (1.0 + (0.3275911 * 0.5**0.5) * size)
    poly = ERF[4]
    for term in (ERF[3], ERF[2], ERF[1], ERF[0]):
        poly = poly * t + term
    density = jnp.exp(-0.5 * value * value)
    half = 0.5 * poly * t * density
    cdf = jnp.where(value >= 0, 1.0 - half, half)
    return cdf, density


def expert_kernel(
    x_ref, c_ref, cen_ref, up_ref, down_ref,
    y_ref, gs_ref, dy_ref, h_ref, dp_ref,
    y_sum, dx_sum, gate_ref,
):
    step = pl.program_id(0)

    @pl.when(step == 0)
    def _():
        logit = jnp.sum(x_ref[...].astype(F32) * cen_ref[...], axis=1, keepdims=True)
        gate = jax.nn.sigmoid(logit)
        gate_ref[...] = jnp.broadcast_to(gate, gate_ref.shape)
        dy_ref[...] = (c_ref[...].astype(F32) * gate).astype(BF16)
        y_sum[...] = jnp.zeros_like(y_sum)
        dx_sum[...] = jnp.zeros_like(dx_sum)

    pre = contract(x_ref[...], up_ref[0], 1, 0)
    cdf, density = gelu_parts(pre)
    hidden = (pre * cdf).astype(BF16)
    slope = cdf + pre * density * 0.3989422804014327
    h_ref[...] = hidden
    y_sum[...] += contract(hidden, down_ref[0], 1, 0)
    grad_hidden = contract(dy_ref[...], down_ref[0], 1, 1)
    grad_pre = (grad_hidden * slope).astype(BF16)
    dp_ref[...] = grad_pre
    dx_sum[...] += contract(grad_pre, up_ref[0], 1, 1)

    @pl.when(step == pl.num_programs(0) - 1)
    def _():
        produced = y_sum[...].astype(BF16)
        y_ref[...] = produced
        gate = gate_ref[:, 0:1]
        dot = jnp.sum(c_ref[...].astype(F32) * produced.astype(F32), axis=1, keepdims=True)
        grad_logit = dot * gate * (1.0 - gate)
        back = dx_sum[...].astype(BF16).astype(F32) + grad_logit * cen_ref[...]
        gs_ref[...] = back.astype(BF16)


def expert(rows, cots, centroid, up, down):
    count, width = rows.shape
    hidden = up.shape[2]
    tile = min(512, hidden)
    whole = pl.BlockSpec((count, width), lambda f: (0, 0))
    wide = jax.ShapeDtypeStruct((count, width), BF16)
    deep = jax.ShapeDtypeStruct((count, hidden), BF16)
    return pl.pallas_call(
        expert_kernel,
        grid=(hidden // tile,),
        in_specs=[
            whole,
            whole,
            pl.BlockSpec((1, width), lambda f: (0, 0)),
            pl.BlockSpec((1, width, tile), lambda f: (0, 0, f)),
            pl.BlockSpec((1, tile, width), lambda f: (0, f, 0)),
        ],
        out_specs=[whole, whole, whole]
        + [pl.BlockSpec((count, tile), lambda f: (0, f))] * 2,
        out_shape=[wide, wide, wide, deep, deep],
        scratch_shapes=[
            pltpu.VMEM((count, width), F32),
            pltpu.VMEM((count, width), F32),
            pltpu.VMEM((count, LANES), F32),
        ],
        cost_estimate=pl.CostEstimate(
            flops=8 * count * width * hidden,
            bytes_accessed=4 * width * hidden + 4 * count * hidden,
            transcendentals=2 * count * hidden,
        ),
        name="expert",
    )(rows, cots, centroid, up, down)


def expert_weights_kernel(x_ref, dy_ref, h_ref, dp_ref, up_ref, down_ref, xt_ref):
    @pl.when(pl.program_id(0) == 0)
    def _():
        xt_ref[...] = jnp.transpose(x_ref[...])

    up_ref[0] = contract(xt_ref[...], dp_ref[...], 1, 0).astype(BF16)
    down_ref[0] = contract(h_ref[...], dy_ref[...], 0, 0).astype(BF16)


def expert_weights(rows, grads, hidden_rows, grad_pre, parts):
    count, width = rows.shape
    hidden = hidden_rows.shape[1]
    share = hidden // parts
    tile = min(384, share)
    each = share // tile
    whole = pl.BlockSpec((count, width), lambda f: (0, 0))
    deep = pl.BlockSpec((count, tile), lambda f: (0, f))
    return pl.pallas_call(
        expert_weights_kernel,
        grid=(hidden // tile,),
        in_specs=[whole, whole, deep, deep],
        out_specs=[
            pl.BlockSpec((1, width, tile), lambda f: (f // each, 0, f % each)),
            pl.BlockSpec((1, tile, width), lambda f: (f // each, f % each, 0)),
        ],
        out_shape=[
            jax.ShapeDtypeStruct((parts, width, share), BF16),
            jax.ShapeDtypeStruct((parts, share, width), BF16),
        ],
        scratch_shapes=[pltpu.VMEM((width, count), BF16)],
        cost_estimate=pl.CostEstimate(
            flops=4 * count * width * hidden,
            bytes_accessed=4 * width * hidden + 4 * count * hidden,
            transcendentals=0,
        ),
        name="expert_weights",
    )(rows, grads, hidden_rows, grad_pre)


def swap(value, axis, bit):
    size = lax.axis_size(axis)
    return lax.ppermute(value, axis, [(i, i ^ bit) for i in range(size)])


def stages():
    found = []
    for axis in ("dp", "expert"):
        bit = 1
        while bit < lax.axis_size(axis):
            found.append((axis, bit))
            bit *= 2
    return found


def bit_of(axis, bit):
    return (lax.axis_index(axis) // bit) % 2


def add_low(left, right):
    return (left.astype(F32) + right.astype(F32)).astype(BF16)


def sum_everywhere(rows):
    for axis, bit in stages():
        half = rows.shape[0] // 2
        mine = bit_of(axis, bit)
        send = lax.dynamic_slice_in_dim(rows, (1 - mine) * half, half, 0)
        keep = lax.dynamic_slice_in_dim(rows, mine * half, half, 0)
        rows = add_low(keep, swap(send, axis, bit))
    for axis, bit in stages()[::-1]:
        mine = bit_of(axis, bit)
        other = swap(rows, axis, bit)
        half = rows.shape[0]
        full = jnp.zeros((2 * half, rows.shape[1]), rows.dtype)
        full = lax.dynamic_update_slice_in_dim(full, rows, mine * half, 0)
        rows = lax.dynamic_update_slice_in_dim(full, other, (1 - mine) * half, 0)
    return rows


def sum_small(value):
    for axis, bit in stages():
        value = value + swap(value, axis, bit)
    return value


def scatter_parts(parts):
    count = parts.shape[0]
    mine = lax.axis_index("dp") % 2
    pairs = parts.reshape((count // 2, 2) + parts.shape[1:])
    send = lax.dynamic_index_in_dim(pairs, 1 - mine, 1, keepdims=False)
    keep = lax.dynamic_index_in_dim(pairs, mine, 1, keepdims=False)
    got = swap(send, "dp", 1)
    total = keep.astype(F32) + got.astype(F32)
    bit = count // 2
    while bit > 1:
        total = total.astype(BF16)
        half = total.shape[0] // 2
        mine = bit_of("dp", bit)
        send = lax.dynamic_slice_in_dim(total, (1 - mine) * half, half, 0)
        keep = lax.dynamic_slice_in_dim(total, mine * half, half, 0)
        got = swap(send, "dp", bit)
        total = keep.astype(F32) + got.astype(F32)
        bit //= 2
    return total


def exchange(rows):
    return lax.all_to_all(rows, "expert", split_axis=0, concat_axis=0, tiled=True)


def local(
    tokens,
    routing,
    query_weight,
    key_weight,
    value_weight,
    output_weight,
    first_gain,
    first_bias,
    second_gain,
    second_bias,
    centroids,
    expert_up,
    expert_down,
    cotangent,
):
    length, width = tokens.shape
    experts = centroids.shape[0]
    capacity = length // experts
    peers = lax.axis_size("expert")
    parts = lax.axis_size("dp")
    slots = experts * capacity

    chosen = routing[:, 0]
    one_hot = (chosen[:, None] == jnp.arange(experts, dtype=jnp.int32)[None, :]).astype(BF16)
    earlier = (
        jnp.arange(length, dtype=jnp.int32)[:, None] > jnp.arange(length, dtype=jnp.int32)[None, :]
    ).astype(BF16)
    before = jnp.dot(earlier, one_hot, preferred_element_type=F32)
    position = jnp.sum(before * one_hot.astype(F32), axis=1).astype(jnp.int32)
    slot = jnp.where(position < capacity, chosen * capacity + position, -1)
    place = (jnp.arange(slots, dtype=jnp.int32)[:, None] == slot[None, :]).astype(BF16)

    def dispatch(rows):
        sent = jnp.dot(place, rows, preferred_element_type=F32).astype(BF16)
        return exchange(sent.reshape(peers, slots // peers, width)).reshape(slots, width)

    def combine(rows):
        return contract(place, rows, 0, 0)

    cots = dispatch(cotangent)

    inputs = tokens.astype(F32)
    normed, first_hat, first_scale = normalize(inputs, first_gain, first_bias)
    normed = normed.astype(BF16)
    queries, keys, values = (
        jnp.dot(normed, weight, preferred_element_type=F32).astype(BF16)
        for weight in (query_weight, key_weight, value_weight)
    )
    mixed, lse = attention(queries, keys, values)
    resid = inputs + jnp.dot(mixed, output_weight, preferred_element_type=F32)
    second, second_hat, second_scale = normalize(resid, second_gain, second_bias)

    rows = dispatch(second.astype(BF16))
    own = centroids[lax.axis_index("expert")][None, :]
    produced, returned, grad_rows, hidden, grad_pre = expert(
        rows, cots, own, expert_up, expert_down
    )
    grad_second = combine(exchange(returned.reshape(peers, -1, width)).reshape(slots, width))
    produced = exchange(produced.reshape(peers, -1, width)).reshape(slots, width)
    up_parts, down_parts = expert_weights(rows, grad_rows, hidden, grad_pre, parts)
    grad_up = scatter_parts(up_parts)
    grad_down = scatter_parts(down_parts)

    grad_out = cotangent.astype(F32)
    grad_second_gain = jnp.sum(grad_second * second_hat, axis=0)
    grad_second_bias = jnp.sum(grad_second, axis=0)
    grad_resid = grad_out + normalize_back(grad_second, second_hat, second_scale, second_gain)
    grad_branch = grad_resid.astype(BF16)
    grad_output = sum_everywhere(contract(mixed, grad_branch, 0, 0).astype(BF16)).astype(F32)
    grad_mixed = contract(grad_branch, output_weight, 1, 1).astype(BF16)

    grad_queries, grad_keys, grad_values = attention_back(
        queries, keys, values, grad_mixed, lse, 0, width // LANES
    )
    weight_grads = sum_everywhere(
        jnp.concatenate(
            [
                contract(normed, grad, 0, 0).astype(BF16)
                for grad in (grad_queries, grad_keys, grad_values)
            ],
            axis=0,
        )
    ).astype(F32)
    grad_normed = (
        contract(grad_queries, query_weight, 1, 1)
        + contract(grad_keys, key_weight, 1, 1)
        + contract(grad_values, value_weight, 1, 1)
    )
    grad_first_gain = jnp.sum(grad_normed * first_hat, axis=0)
    grad_first_bias = jnp.sum(grad_normed, axis=0)
    grad_tokens = grad_resid + normalize_back(grad_normed, first_hat, first_scale, first_gain)
    small = sum_small(
        jnp.stack([grad_first_gain, grad_first_bias, grad_second_gain, grad_second_bias])
    )

    one_hot = one_hot.astype(F32)
    logits = jnp.dot(second, centroids.T, precision=lax.Precision.HIGHEST)
    gating = jax.nn.sigmoid(jnp.sum(logits * one_hot, axis=1, keepdims=True))
    layer_out = (resid + gating * combine(produced)).astype(BF16)
    return (
        layer_out,
        grad_tokens,
        weight_grads[:width],
        weight_grads[width : 2 * width],
        weight_grads[2 * width :],
        grad_output,
        small[0],
        small[1],
        small[2],
        small[3],
        grad_up,
        grad_down,
    )


def solution(mesh):
    rows = P(("dp", "expert"), None)
    return jax.shard_map(
        local,
        mesh=mesh,
        in_specs=(rows, rows)
        + (P(),) * 9
        + (P("expert", None, None), P("expert", None, None), rows),
        out_specs=(rows, rows) + (P(),) * 8 + (P("expert", None, "dp"), P("expert", "dp", None)),
        check_vma=False,
    )
```

```python
import functools
import math

import jax
import jax.numpy as jnp
from jax import lax
from jax.experimental import pallas as pl
from jax.experimental.pallas import tpu as pltpu
from jax.sharding import PartitionSpec as P

HEADS = 12
HEAD = 64
LANES = 128
EPS = 1e-05
F32 = jnp.float32
BF16 = jnp.bfloat16
ROWS = 256

LIGHT = pl.CostEstimate(flops=1000000, bytes_accessed=100000, transcendentals=0)


def contract(left, right, left_dim, right_dim):
    return lax.dot_general(
        left, right, (((left_dim,), (right_dim,)), ((), ())), preferred_element_type=F32
    )


def normalize(values, gain, bias):
    centered = values - jnp.mean(values, axis=-1, keepdims=True)
    variance = jnp.mean(centered * centered, axis=-1, keepdims=True)
    scale = lax.rsqrt(variance + EPS)
    xhat = centered * scale
    return xhat * gain + bias, xhat, scale


def normalize_back(grad, xhat, scale, gain):
    scaled = grad * gain
    first = jnp.mean(scaled, axis=-1, keepdims=True)
    cross = jnp.mean(scaled * xhat, axis=-1, keepdims=True)
    return scale * (scaled - first - xhat * cross)


def head_mask(parity, value):
    lane = lax.broadcasted_iota(jnp.int32, (1, LANES), 1)
    return jnp.where(lane // HEAD == parity, value, 0.0).astype(BF16)


def causal_bias(bias_ref, keys_dim):
    @pl.when((pl.program_id(0) == 0) & (pl.program_id(1) == 0))
    def _():
        key = lax.broadcasted_iota(jnp.int32, bias_ref.shape, keys_dim)
        query = lax.broadcasted_iota(jnp.int32, bias_ref.shape, 1 - keys_dim)
        bias_ref[...] = jnp.where(key <= query, 0.0, -1e30)


def attention_kernel(q_ref, k_ref, v_ref, o_ref, lse_ref, bias_ref, *, block):
    causal_bias(bias_ref, 1)
    parity = pl.program_id(1)
    length = q_ref.shape[0]
    queries = q_ref[...] * head_mask(parity, HEAD**-0.5)
    values = v_ref[...] * head_mask(parity, 1.0)
    outs = []
    for index in range(length // block):
        first, finish = index * block, (index + 1) * block
        scores = contract(queries[first:finish], k_ref[:finish, :], 1, 1)
        diagonal = scores[:, first:] + bias_ref[...]
        if index:
            scores = jnp.concatenate([scores[:, :first], diagonal], axis=1)
        else:
            scores = diagonal
        top = jnp.max(scores, axis=1, keepdims=True)
        shifted = jnp.exp(scores - top)
        total = jnp.sum(shifted, axis=1, keepdims=True)
        probs = (shifted * (1.0 / total)).astype(BF16)
        outs.append(contract(probs, values[:finish], 1, 0).astype(BF16))
        lse = jnp.broadcast_to(top + jnp.log(total), (block, LANES))
        lse_ref[0, :, first:finish] = jnp.transpose(lse)[0:1, :]
    mixed = jnp.concatenate(outs, axis=0)

    @pl.when(parity == 0)
    def _():
        o_ref[...] = mixed

    @pl.when(parity == 1)
    def _():
        o_ref[...] = o_ref[...] + mixed


def attention(queries, keys, values):
    length, width = queries.shape
    pairs = width // LANES
    block = min(256, length)
    spec = pl.BlockSpec((length, LANES), lambda pair, parity: (0, pair))
    return pl.pallas_call(
        functools.partial(attention_kernel, block=block),
        grid=(pairs, 2),
        in_specs=[spec, spec, spec],
        out_specs=[
            spec,
            pl.BlockSpec((1, 1, length), lambda pair, parity: (pair * 2 + parity, 0, 0)),
        ],
        out_shape=[
            jax.ShapeDtypeStruct((length, width), BF16),
            jax.ShapeDtypeStruct((2 * pairs, 1, length), F32),
        ],
        scratch_shapes=[pltpu.VMEM((block, block), F32)],
        cost_estimate=LIGHT,
        name="attention",
    )(queries, keys, values)


def attention_back_kernel(
    q_ref, k_ref, v_ref, g_ref, lse_ref, grads_ref, dk_sum, dv_sum, bias_ref, *, block
):
    causal_bias(bias_ref, 0)
    parity = pl.program_id(1)
    length = q_ref.shape[0]
    scale_mask = head_mask(parity, HEAD**-0.5)
    queries = q_ref[...] * scale_mask
    grads = g_ref[...] * head_mask(parity, 1.0)
    keys_scaled = k_ref[...] * scale_mask
    dk_sum[...] = jnp.zeros_like(dk_sum)
    dv_sum[...] = jnp.zeros_like(dv_sum)
    dq_parts = []
    for index in range(length // block):
        first, finish = index * block, (index + 1) * block
        scores = contract(k_ref[:finish, :], queries[first:finish], 1, 1)
        diagonal = scores[first:] + bias_ref[...]
        if index:
            scores = jnp.concatenate([scores[:first], diagonal], axis=0)
        else:
            scores = diagonal
        probs = jnp.exp(scores - lse_ref[0, :, first:finish])
        dv_sum[:finish, :] += contract(probs.astype(BF16), grads[first:finish], 1, 0)
        grad_probs = contract(v_ref[:finish, :], grads[first:finish], 1, 1)
        delta = jnp.sum(probs * grad_probs, axis=0, keepdims=True)
        grad_scores = (probs * (grad_probs - delta)).astype(BF16)
        dk_sum[:finish, :] += contract(grad_scores, queries[first:finish], 1, 0)
        dq_parts.append(contract(grad_scores, keys_scaled[:finish], 0, 0).astype(BF16))
    parts = (
        jnp.concatenate(dq_parts, axis=0),
        dk_sum[...].astype(BF16),
        dv_sum[...].astype(BF16),
    )

    @pl.when(parity == 0)
    def _():
        for index, part in enumerate(parts):
            grads_ref[index] = part

    @pl.when(parity == 1)
    def _():
        for index, part in enumerate(parts):
            grads_ref[index] = grads_ref[index] + part


def attention_back(queries, keys, values, grads, lse, start, pairs):
    length = queries.shape[0]
    block = min(256, length)
    spec = pl.BlockSpec((length, LANES), lambda pair, parity: (0, start + pair))
    return pl.pallas_call(
        functools.partial(attention_back_kernel, block=block),
        grid=(pairs, 2),
        in_specs=[
            spec,
            spec,
            spec,
            spec,
            pl.BlockSpec(
                (1, 1, length), lambda pair, parity: ((start + pair) * 2 + parity, 0, 0)
            ),
        ],
        out_specs=pl.BlockSpec((3, length, LANES), lambda pair, parity: (0, 0, pair)),
        out_shape=jax.ShapeDtypeStruct((3, length, pairs * LANES), BF16),
        scratch_shapes=[pltpu.VMEM((length, LANES), F32)] * 2 + [pltpu.VMEM((block, block), F32)],
        cost_estimate=LIGHT,
        name="attention_back",
    )(queries, keys, values, grads, lse)


def gelu_parts(value):
    cdf = 0.5 + 0.5 * lax.erf(value * 0.5**0.5)
    density = jnp.exp2(value * value * (-0.5 / math.log(2.0)))
    return cdf, value * (density * (1.0 / math.sqrt(2.0 * math.pi)))


def expert_kernel(
    x_ref, c_ref, cen_ref, up_ref, down_ref,
    y_ref, gs_ref, dy_ref, h_ref, dp_ref,
    y_sum, dx_sum, gate_ref,
):
    step = pl.program_id(0)

    @pl.when(step == 0)
    def _():
        logit = jnp.sum(x_ref[...].astype(F32) * cen_ref[...], axis=1, keepdims=True)
        gate = jax.nn.sigmoid(logit)
        gate_ref[...] = jnp.broadcast_to(gate, gate_ref.shape)
        dy_ref[...] = (c_ref[...].astype(F32) * gate).astype(BF16)
        y_sum[...] = jnp.zeros_like(y_sum)
        dx_sum[...] = jnp.zeros_like(dx_sum)

    pre = contract(x_ref[...], up_ref[0], 1, 0)
    cdf, weighted = gelu_parts(pre)
    hidden = (pre * cdf).astype(BF16)
    slope = cdf + weighted
    h_ref[...] = hidden
    y_sum[...] += contract(hidden, down_ref[0], 1, 0)
    grad_hidden = contract(dy_ref[...], down_ref[0], 1, 1)
    grad_pre = (grad_hidden * slope).astype(BF16)
    dp_ref[...] = grad_pre
    dx_sum[...] += contract(grad_pre, up_ref[0], 1, 1)

    @pl.when(step == pl.num_programs(0) - 1)
    def _():
        produced = y_sum[...].astype(BF16)
        y_ref[...] = produced
        gate = gate_ref[:, 0:1]
        dot = jnp.sum(c_ref[...].astype(F32) * produced.astype(F32), axis=1, keepdims=True)
        grad_logit = dot * gate * (1.0 - gate)
        back = dx_sum[...].astype(BF16).astype(F32) + grad_logit * cen_ref[...]
        gs_ref[...] = back.astype(BF16)


def expert(rows, cots, centroid, up, down):
    count, width = rows.shape
    hidden = up.shape[2]
    tile = min(512, hidden)
    whole = pl.BlockSpec((count, width), lambda f: (0, 0))
    wide = jax.ShapeDtypeStruct((count, width), BF16)
    deep = jax.ShapeDtypeStruct((count, hidden), BF16)
    return pl.pallas_call(
        expert_kernel,
        grid=(hidden // tile,),
        in_specs=[
            whole,
            whole,
            pl.BlockSpec((1, width), lambda f: (0, 0)),
            pl.BlockSpec((1, width, tile), lambda f: (0, 0, f)),
            pl.BlockSpec((1, tile, width), lambda f: (0, f, 0)),
        ],
        out_specs=[whole, whole, whole]
        + [pl.BlockSpec((count, tile), lambda f: (0, f))] * 2,
        out_shape=[wide, wide, wide, deep, deep],
        scratch_shapes=[
            pltpu.VMEM((count, width), F32),
            pltpu.VMEM((count, width), F32),
            pltpu.VMEM((count, LANES), F32),
        ],
        cost_estimate=LIGHT,
        name="expert",
    )(rows, cots, centroid, up, down)


def expert_weights_kernel(
    core_ref, x_ref, dy_ref, h_ref, dp_ref,
    up_send_ref, down_send_ref, up_keep_ref, down_keep_ref, xt_ref,
):
    @pl.when(pl.program_id(0) == 0)
    def _():
        xt_ref[...] = jnp.transpose(x_ref[...])

    up = contract(xt_ref[...], dp_ref[...], 1, 0).astype(BF16)
    down = contract(h_ref[...], dy_ref[...], 0, 0).astype(BF16)
    sending = pl.program_id(0) < pl.num_programs(0) // 2

    @pl.when(sending)
    def _():
        up_send_ref[0] = up
        down_send_ref[0] = down

    @pl.when(jnp.logical_not(sending))
    def _():
        up_keep_ref[0] = up
        down_keep_ref[0] = down


def expert_weights(rows, grads, hidden_rows, grad_pre, parts, core):
    count, width = rows.shape
    hidden = hidden_rows.shape[1]
    share = hidden // parts
    tile = min(384, share)
    each = share // tile
    half = hidden // tile // 2

    def column(f, core):
        step = f % half
        other = jnp.where(f < half, 1 - core[0], core[0])
        return ((step // each) * 2 + other) * each + step % each

    def send(f):
        return jnp.minimum(f, half - 1)

    def keep(f):
        return jnp.maximum(f - half, 0)

    whole = pl.BlockSpec((count, width), lambda f, core: (0, 0))
    deep = pl.BlockSpec((count, tile), lambda f, core: (0, column(f, core)))
    up = [
        pl.BlockSpec((1, width, tile), lambda f, core, at=at: (at(f) // each, 0, at(f) % each))
        for at in (send, keep)
    ]
    down = [
        pl.BlockSpec((1, tile, width), lambda f, core, at=at: (at(f) // each, at(f) % each, 0))
        for at in (send, keep)
    ]
    up_shape = jax.ShapeDtypeStruct((parts // 2, width, share), BF16)
    down_shape = jax.ShapeDtypeStruct((parts // 2, share, width), BF16)
    return pl.pallas_call(
        expert_weights_kernel,
        grid_spec=pltpu.PrefetchScalarGridSpec(
            num_scalar_prefetch=1,
            grid=(2 * half,),
            in_specs=[whole, whole, deep, deep],
            out_specs=[up[0], down[0], up[1], down[1]],
            scratch_shapes=[pltpu.VMEM((width, count), BF16)],
        ),
        out_shape=[up_shape, down_shape, up_shape, down_shape],
        cost_estimate=LIGHT,
        name="expert_weights",
    )(core, rows, grads, hidden_rows, grad_pre)


def one_hot(condition):
    return jnp.where(condition, 1.0, 0.0).astype(BF16)


def block_rows(step, count, length, dim):
    return step * count + lax.broadcasted_iota(jnp.int32, (count, length), dim)


def const(*shape):
    return pl.BlockSpec(shape, lambda *step: (0,) * len(shape))


def route_kernel(routing_ref, cot_ref, send_ref, slot_ref, wide_ref, *, experts, capacity):
    length = routing_ref.shape[1]
    step = pl.program_id(0)

    @pl.when(step == 0)
    def _():
        chosen = routing_ref[...]
        named = lax.broadcasted_iota(jnp.int32, (experts, length), 0) == chosen
        named = jnp.where(named, 1.0, 0.0)
        lane = lax.broadcasted_iota(jnp.int32, (experts, length), 1)
        count = named
        shift = 1
        while shift < length:
            count = count + jnp.where(lane >= shift, pltpu.roll(count, shift, 1), 0.0)
            shift *= 2
        position = jnp.sum(named * (count - named), axis=0, keepdims=True)
        slot = chosen.astype(F32) * capacity + position
        slot = jnp.where(position < capacity, slot, -1.0)
        slot_ref[...] = slot.astype(jnp.int32)
        wide_ref[...] = jnp.transpose(jnp.broadcast_to(slot, (LANES, length))).astype(jnp.int32)

    place = one_hot(block_rows(step, send_ref.shape[0], length, 0) == slot_ref[...])
    send_ref[...] = contract(place, cot_ref[...], 1, 0).astype(BF16)


def route(routing, cotangent, experts, capacity):
    length, width = cotangent.shape
    slots = experts * capacity
    return pl.pallas_call(
        functools.partial(route_kernel, experts=experts, capacity=capacity),
        grid=(slots // ROWS,),
        in_specs=[const(1, length), const(length, width)],
        out_specs=[
            pl.BlockSpec((ROWS, width), lambda i: (i, 0)),
            const(1, length),
            const(length, LANES),
        ],
        out_shape=[
            jax.ShapeDtypeStruct((slots, width), BF16),
            jax.ShapeDtypeStruct((1, length), jnp.int32),
            jax.ShapeDtypeStruct((length, LANES), jnp.int32),
        ],
        cost_estimate=LIGHT,
        name="route",
    )(routing, cotangent)


def project_kernel(
    tokens_ref, gain_ref, bias_ref, wq_ref, wk_ref, wv_ref, turned_ref, q_ref, k_ref, v_ref
):
    normed, _, _ = normalize(tokens_ref[...].astype(F32), gain_ref[...], bias_ref[...])
    normed = normed.astype(BF16)
    turned_ref[...] = jnp.transpose(normed)
    for weight, out in ((wq_ref, q_ref), (wk_ref, k_ref), (wv_ref, v_ref)):
        out[...] = contract(normed, weight[...], 1, 0).astype(BF16)


def project(tokens, gain, bias, weights):
    length, width = tokens.shape
    rows = pl.BlockSpec((ROWS, width), lambda i: (i, 0))
    out = jax.ShapeDtypeStruct((length, width), BF16)
    return pl.pallas_call(
        project_kernel,
        grid=(length // ROWS,),
        in_specs=[rows, const(1, width), const(1, width)] + [const(width, width)] * 3,
        out_specs=[pl.BlockSpec((width, ROWS), lambda i: (0, i))] + [rows] * 3,
        out_shape=[jax.ShapeDtypeStruct((width, length), BF16)] + [out] * 3,
        cost_estimate=LIGHT,
        name="project",
    )(tokens, gain, bias, *weights)


def branch_kernel(
    mixed_ref, tokens_ref, weight_ref, gain_ref, bias_ref, cen_ref, chosen_ref, slot_ref,
    resid_ref, gate_ref, turned_ref, send_ref, low_ref, *, blocks,
):
    step = pl.program_id(0)

    @pl.when(step < blocks)
    def _():
        mixed = mixed_ref[...]
        turned_ref[...] = jnp.transpose(mixed)
        resid = tokens_ref[...].astype(F32) + contract(mixed, weight_ref[...], 1, 0)
        second, _, _ = normalize(resid, gain_ref[...], bias_ref[...])
        resid_ref[...] = resid
        low_ref[pl.ds(pl.multiple_of(step * ROWS, ROWS), ROWS), :] = second.astype(BF16)
        centroid = jnp.zeros_like(second)
        for index in range(cen_ref.shape[0]):
            centroid = jnp.where(chosen_ref[...] == index, cen_ref[index : index + 1, :], centroid)
        gate_ref[...] = jax.nn.sigmoid(jnp.sum(second * centroid, axis=1, keepdims=True))

    @pl.when(step >= blocks)
    def _():
        place = one_hot(block_rows(step - blocks, ROWS, slot_ref.shape[1], 0) == slot_ref[...])
        send_ref[...] = contract(place, low_ref[...], 1, 0).astype(BF16)


def branch(mixed, tokens, weight, gain, bias, centroids, routing, slot, slots):
    length, width = mixed.shape
    blocks = length // ROWS

    def at(i):
        return jnp.minimum(i, blocks - 1)

    rows = pl.BlockSpec((ROWS, width), lambda i: (at(i), 0))
    thin = pl.BlockSpec((ROWS, 1), lambda i: (at(i), 0))
    return pl.pallas_call(
        functools.partial(branch_kernel, blocks=blocks),
        grid=(blocks + slots // ROWS,),
        in_specs=[
            rows,
            rows,
            const(width, width),
            const(1, width),
            const(1, width),
            const(*centroids.shape),
            thin,
            const(1, length),
        ],
        out_specs=[
            rows,
            thin,
            pl.BlockSpec((width, ROWS), lambda i: (0, at(i))),
            pl.BlockSpec((ROWS, width), lambda i: (jnp.maximum(i - blocks, 0), 0)),
        ],
        out_shape=[
            jax.ShapeDtypeStruct((length, width), F32),
            jax.ShapeDtypeStruct((length, 1), F32),
            jax.ShapeDtypeStruct((width, length), BF16),
            jax.ShapeDtypeStruct((slots, width), BF16),
        ],
        scratch_shapes=[pltpu.VMEM((length, width), BF16)],
        cost_estimate=LIGHT,
        name="branch",
    )(mixed, tokens, weight, gain, bias, centroids, routing, slot)


def gathered(wide_ref, rows_ref):
    slots = rows_ref.shape[0]
    count = wide_ref.shape[0]
    wide = jnp.concatenate([wide_ref[...]] * (slots // LANES), axis=1)
    place = one_hot(lax.broadcasted_iota(jnp.int32, (count, slots), 1) == wide)
    return contract(place, rows_ref[...], 1, 0)


def second_back_kernel(
    wide_ref, back_ref, resid_ref, cot_ref, gain_ref, weight_ref,
    grad_ref, low_ref, mixed_ref, sums_ref,
):
    grad = gathered(wide_ref, back_ref)
    _, xhat, scale = normalize(resid_ref[...], gain_ref[...], gain_ref[...])
    sums = jnp.concatenate(
        [jnp.sum(grad * xhat, axis=0, keepdims=True), jnp.sum(grad, axis=0, keepdims=True)], axis=0
    )

    @pl.when(pl.program_id(0) == 0)
    def _():
        sums_ref[...] = sums

    @pl.when(pl.program_id(0) > 0)
    def _():
        sums_ref[...] = sums_ref[...] + sums

    grad = cot_ref[...].astype(F32) + normalize_back(grad, xhat, scale, gain_ref[...])
    grad_ref[...] = grad
    low = grad.astype(BF16)
    low_ref[...] = low
    mixed_ref[...] = contract(low, weight_ref[...], 1, 1).astype(BF16)


def second_back(wide, back, resid, cotangent, gain, weight):
    length, width = resid.shape
    rows = pl.BlockSpec((ROWS, width), lambda i: (i, 0))
    low = jax.ShapeDtypeStruct((length, width), BF16)
    return pl.pallas_call(
        second_back_kernel,
        grid=(length // ROWS,),
        in_specs=[
            pl.BlockSpec((ROWS, LANES), lambda i: (i, 0)),
            const(*back.shape),
            rows,
            rows,
            const(1, width),
            const(width, width),
        ],
        out_specs=[rows, rows, rows, const(2, width)],
        out_shape=[
            jax.ShapeDtypeStruct((length, width), F32),
            low,
            low,
            jax.ShapeDtypeStruct((2, width), F32),
        ],
        cost_estimate=LIGHT,
        name="second_back",
    )(wide, back, resid, cotangent, gain, weight)


def first_back_kernel(
    left_ref, right_ref, tokens_ref, resid_ref, gain_ref, wq_ref, wk_ref, wv_ref,
    grad_ref, sums_ref,
):
    side = left_ref.shape[2]
    grad = 0.0
    for index, weight in enumerate((wq_ref, wk_ref, wv_ref)):
        grad = grad + contract(left_ref[index], weight[:, :side], 1, 1)
        grad = grad + contract(right_ref[index], weight[:, side:], 1, 1)
    gain = gain_ref[...]
    _, xhat, scale = normalize(tokens_ref[...].astype(F32), gain, gain)
    sums = jnp.concatenate(
        [jnp.sum(grad * xhat, axis=0, keepdims=True), jnp.sum(grad, axis=0, keepdims=True)], axis=0
    )

    @pl.when(pl.program_id(0) == 0)
    def _():
        sums_ref[...] = sums

    @pl.when(pl.program_id(0) > 0)
    def _():
        sums_ref[...] = sums_ref[...] + sums

    grad_ref[...] = resid_ref[...] + normalize_back(grad, xhat, scale, gain)


def first_back(left, right, tokens, resid, gain, weights):
    length, width = tokens.shape
    rows = pl.BlockSpec((ROWS, width), lambda i: (i, 0))
    return pl.pallas_call(
        first_back_kernel,
        grid=(length // ROWS,),
        in_specs=[
            pl.BlockSpec((3, ROWS, part.shape[2]), lambda i: (0, i, 0)) for part in (left, right)
        ]
        + [rows, rows, const(1, width)]
        + [const(width, width)] * 3,
        out_specs=[rows, const(2, width)],
        out_shape=[
            jax.ShapeDtypeStruct((length, width), F32),
            jax.ShapeDtypeStruct((2, width), F32),
        ],
        cost_estimate=LIGHT,
        name="first_back",
    )(left, right, tokens, resid, gain, *weights)


def layer_out_kernel(wide_ref, rows_ref, resid_ref, gate_ref, out_ref):
    out_ref[...] = (resid_ref[...] + gate_ref[...] * gathered(wide_ref, rows_ref)).astype(BF16)


def layer_output(wide, produced, resid, gate):
    length, width = resid.shape
    rows = pl.BlockSpec((ROWS, width), lambda i: (i, 0))
    return pl.pallas_call(
        layer_out_kernel,
        grid=(length // ROWS,),
        in_specs=[
            pl.BlockSpec((ROWS, LANES), lambda i: (i, 0)),
            const(*produced.shape),
            rows,
            pl.BlockSpec((ROWS, 1), lambda i: (i, 0)),
        ],
        out_specs=rows,
        out_shape=jax.ShapeDtypeStruct((length, width), BF16),
        cost_estimate=LIGHT,
        name="layer_output",
    )(wide, produced, resid, gate)


def weight_grads_kernel(core_ref, *refs, sources):
    lefts, rights, send_ref, keep_ref = refs[:-2:2], refs[1:-2:2], refs[-2], refs[-1]
    matrix = pl.program_id(0)
    rows = send_ref.shape[1]
    first = 0
    for left, right, count in zip(lefts, rights, sources):
        @pl.when((matrix >= first) & (matrix < first + count))
        def _(left=left, right=right):
            grad = right[0] if len(right.shape) == 3 else right[...]
            for half, out in ((1 - core_ref[0], send_ref), (core_ref[0], keep_ref)):
                turned = left[pl.ds(pl.multiple_of(half * rows, rows), rows), :]
                out[0] = contract(turned, grad, 1, 0).astype(BF16)

        first += count


def weight_grads(core, side, *sources):
    width, length = sources[0][0].shape
    counts, specs, args = [], [], []
    for turned, grads in sources:
        counts.append(3 if grads.ndim == 3 else grads.shape[1] // side)
    total = sum(counts)
    first = 0
    for (turned, grads), count in zip(sources, counts):
        def which(step, first=first, count=count):
            return jnp.clip(step - first, 0, count - 1)

        specs.append(pl.BlockSpec((width, length), lambda i, core: (0, 0)))
        if grads.ndim == 3:
            specs.append(
                pl.BlockSpec((1, length, side), lambda i, core, which=which: (which(i), 0, 0))
            )
        else:
            specs.append(pl.BlockSpec((length, side), lambda i, core, which=which: (0, which(i))))
        args += [turned, grads]
        first += count
    shape = jax.ShapeDtypeStruct((total, width // 2, side), BF16)
    send, keep = pl.pallas_call(
        functools.partial(weight_grads_kernel, sources=tuple(counts)),
        grid_spec=pltpu.PrefetchScalarGridSpec(
            num_scalar_prefetch=1,
            grid=(total,),
            in_specs=specs,
            out_specs=[pl.BlockSpec((1, width // 2, side), lambda i, core: (i, 0, 0))] * 2,
        ),
        out_shape=[shape, shape],
        cost_estimate=LIGHT,
        name="weight_grads",
    )(core, *args)
    return send.reshape(-1, side), keep.reshape(-1, side)


def assemble_kernel(core_ref, early_mine, early_other, late_mine, late_other, *outs):
    mine = pl.program_id(0) == core_ref[0]
    side = early_mine.shape[2]

    def write(early, late):
        outs[0][:, :side] = early[0].astype(F32)
        outs[0][:, side:] = early[1].astype(F32)
        for index in range(3):
            outs[1 + index][:, :side] = early[2 + index].astype(F32)
            outs[1 + index][:, side:] = late[index].astype(F32)

    @pl.when(mine)
    def _():
        write(early_mine, late_mine)

    @pl.when(jnp.logical_not(mine))
    def _():
        write(early_other, late_other)


def assemble(core, early_mine, early_other, late_mine, late_other, width):
    side = early_mine.shape[1]
    args = [
        part.reshape(-1, width // 2, side)
        for part in (early_mine, early_other, late_mine, late_other)
    ]
    out = jax.ShapeDtypeStruct((width, width), F32)
    return pl.pallas_call(
        assemble_kernel,
        grid_spec=pltpu.PrefetchScalarGridSpec(
            num_scalar_prefetch=1,
            grid=(2,),
            in_specs=[const(*part.shape) for part in args],
            out_specs=[pl.BlockSpec((width // 2, width), lambda i, core: (i, 0))] * 4,
        ),
        out_shape=[out] * 4,
        cost_estimate=LIGHT,
        name="assemble",
    )(core, *args)


def swap(value, axis, bit):
    size = lax.axis_size(axis)
    return lax.ppermute(value, axis, [(i, i ^ bit) for i in range(size)])


def stages(axis, low, high):
    found = []
    bit = low
    while bit < min(high, lax.axis_size(axis)):
        found.append((axis, bit))
        bit *= 2
    return found


def bit_of(axis, bit):
    return (lax.axis_index(axis) // bit) % 2


def add_low(left, right):
    return (left.astype(F32) + right.astype(F32)).astype(BF16)


def add(left, right):
    return left + right


def halves(rows, stage):
    axis, bit = stage
    half = rows.shape[0] // 2
    mine = bit_of(axis, bit)
    return (
        lax.dynamic_slice_in_dim(rows, (1 - mine) * half, half, 0),
        lax.dynamic_slice_in_dim(rows, mine * half, half, 0),
    )


def joined(rows, other, stage):
    first = bit_of(*stage) == 0
    return jnp.concatenate([jnp.where(first, rows, other), jnp.where(first, other, rows)], axis=0)


def add_split_kernel(mine_ref, left_ref, right_ref, send_ref, keep_ref):
    value = add_low(left_ref[...], right_ref[...])

    @pl.when(pl.program_id(0) == 0)
    def _():
        send_ref[...] = value

    @pl.when(pl.program_id(0) == 1)
    def _():
        keep_ref[...] = value


def add_split(left, right, stage):
    half, width = left.shape[0] // 2, left.shape[1]
    if half % 8:
        return halves(add_low(left, right), stage)
    mine = bit_of(*stage).astype(jnp.int32)[None]
    block = pl.BlockSpec((half, width), lambda i, mine: (jnp.where(i == 0, 1 - mine[0], mine[0]), 0))
    out = pl.BlockSpec((half, width), lambda i, mine: (0, 0))
    shape = jax.ShapeDtypeStruct((half, width), BF16)
    return pl.pallas_call(
        add_split_kernel,
        grid_spec=pltpu.PrefetchScalarGridSpec(
            num_scalar_prefetch=1,
            grid=(2,),
            in_specs=[block, block],
            out_specs=[out, out],
        ),
        out_shape=[shape, shape],
        cost_estimate=LIGHT,
        name="add_split",
    )(mine, left, right)


def halves_sum(left, right, stage):
    width = left.shape[2]
    parts = add_split(left.reshape(-1, width), right.reshape(-1, width), stage)
    return [part.reshape(-1, *left.shape[1:]) for part in parts]


class Sum:
    def __init__(self, keep, send, stages, plus=add_low, split=True):
        self.keep, self.send, self.plus = keep, send, plus
        if split:
            self.steps = [("whole", stages[0])]
            self.steps += [("halve", stage) for stage in stages[1:-1]]
            self.steps += [("whole", stages[-1])]
            self.steps += [("join", stage) for stage in stages[-2:0:-1]]
        else:
            self.steps = [("whole", stage) for stage in stages]

    def start(self):
        return swap(self.send, *self.steps[0][1])

    def finish(self, got):
        kind, stage = self.steps.pop(0)
        if self.steps and self.steps[0][0] == "halve":
            self.send, self.keep = add_split(self.keep, got, self.steps[0][1])
        else:
            join = functools.partial(joined, stage=stage)
            self.keep = self.send = (join if kind == "join" else self.plus)(self.keep, got)


def advance(sums, *others):
    sums = [each for each in sums if each.steps]
    tied = tie((*(each.start() for each in sums), *others))
    for each, got in zip(sums, tied):
        each.finish(got)
    rest = tied[len(sums) :]
    return rest[0] if len(rest) == 1 else rest


def chip_stages(total):
    return [("dp", 2 << index) for index in range((total.shape[0]).bit_length() - 1)][::-1]


tie = lax.optimization_barrier


def exchange(rows):
    return lax.all_to_all(rows, "expert", split_axis=0, concat_axis=0, tiled=True)


def local(
    tokens,
    routing,
    query_weight,
    key_weight,
    value_weight,
    output_weight,
    first_gain,
    first_bias,
    second_gain,
    second_bias,
    centroids,
    expert_up,
    expert_down,
    cotangent,
):
    length, width = tokens.shape
    experts = centroids.shape[0]
    capacity = length // experts
    peers = lax.axis_size("expert")
    parts = lax.axis_size("dp")
    slots = experts * capacity
    core = (lax.axis_index("dp") % 2).astype(jnp.int32)[None]
    vectors = tie(jnp.stack([first_gain, first_bias, second_gain, second_bias]))
    first_gain, first_bias, second_gain, second_bias = (vectors[i : i + 1] for i in range(4))
    weights = (query_weight, key_weight, value_weight)

    cots, slot, wide = route(routing.reshape(1, length), cotangent, experts, capacity)
    cots, tokens = tie((cots, tokens))
    cots = exchange(cots.reshape(peers, -1, width)).reshape(slots, width)

    normed_turned, queries, keys, values = project(tokens, first_gain, first_bias, weights)
    mixed, lse = attention(queries, keys, values)
    mixed, cots = tie((mixed, cots))
    resid, gate, mixed_turned, rows = branch(
        mixed, tokens, output_weight, second_gain, second_bias, centroids, routing, slot, slots
    )

    rows = exchange(rows.reshape(peers, -1, width)).reshape(slots, width)
    own = centroids[lax.axis_index("expert")][None, :]
    produced, returned, grad_rows, hidden, grad_pre = expert(
        rows, cots, own, expert_up, expert_down
    )
    returned = exchange(returned.reshape(peers, -1, width))
    up_send, down_send, up_keep, down_keep = expert_weights(
        rows, grad_rows, hidden, grad_pre, parts, core
    )
    chips = chip_stages(up_send)
    up_send, up_keep = halves_sum(up_keep, swap(up_send, "dp", 1), chips[0])
    down_send, down_keep = halves_sum(down_keep, swap(down_send, "dp", 1), chips[0])
    returned, produced, up_send, up_keep, down_send, down_keep = tie(
        (returned, produced, up_send, up_keep, down_send, down_keep)
    )
    returned = returned.reshape(slots, width)
    up_got = swap(up_send, *chips[0])
    down_got = swap(down_send, *chips[0])
    produced = exchange(produced.reshape(peers, -1, width))

    grad_resid, grad_branch, grad_mixed, second_sums = second_back(
        wide, returned, resid, cotangent, second_gain, output_weight
    )

    pairs = width // LANES
    split = pairs // 2
    side = split * LANES
    cross = stages("expert", 1, 1 << 20)
    apart = stages("dp", 2, 1 << 20)
    left = attention_back(queries, keys, values, grad_mixed, lse, 0, split)
    left, up_got = tie((left, up_got))
    send, keep = weight_grads(core, side, (mixed_turned, grad_branch), (normed_turned, left))
    early = Sum(keep, send, [("dp", 1)] + cross + apart)
    advance([early])
    early.send, lse = tie((early.send, lse))
    right = attention_back(queries, keys, values, grad_mixed, lse, split, pairs - split)
    right, produced = advance([early], right, produced)
    produced = produced.reshape(slots, width)
    send, keep = weight_grads(core, side, (normed_turned, right))
    send, keep = tie((send, keep))
    grad_tokens, first_sums = first_back(left, right, tokens, grad_resid, first_gain, weights)
    late = Sum(keep, send, [("dp", 1)] + apart + cross)
    grad_tokens, first_sums, down_got = advance([early, late], grad_tokens, first_sums, down_got)
    grad_up = up_keep.astype(F32) + up_got.astype(F32)
    grad_down = down_keep.astype(F32) + down_got.astype(F32)
    for stage in chips[1:]:
        grad_up, grad_down = (
            keep.astype(F32) + swap(send, *stage).astype(F32)
            for send, keep in (halves(value.astype(BF16), stage) for value in (grad_up, grad_down))
        )
    grad_up, grad_down = (value.reshape(value.shape[1:])[None] for value in (grad_up, grad_down))
    small = jnp.concatenate([first_sums, second_sums], axis=0)
    small = Sum(small, small, stages("dp", 1, 1 << 20) + cross, plus=add, split=False)
    layer_out = layer_output(wide, produced, resid, gate)
    layer_out = advance([early, late, small], layer_out)
    while early.steps or late.steps or small.steps:
        advance([early, late, small])
    early, late, small = early.keep, late.keep, small.keep
    grad_output, grad_query, grad_key, grad_value = assemble(
        core, early, swap(early, "dp", 1), late, swap(late, "dp", 1), width
    )
    return (
        layer_out,
        grad_tokens,
        grad_query,
        grad_key,
        grad_value,
        grad_output,
        small[0],
        small[1],
        small[2],
        small[3],
        grad_up,
        grad_down,
    )


def solution(mesh):
    rows = P(("dp", "expert"), None)
    return jax.shard_map(
        local,
        mesh=mesh,
        in_specs=(rows, rows)
        + (P(),) * 9
        + (P("expert", None, None), P("expert", None, None), rows),
        out_specs=(rows, rows) + (P(),) * 8 + (P("expert", None, "dp"), P("expert", "dp", None)),
        check_vma=False,
    )
```

```python
import functools
import math

import jax
import jax.numpy as jnp
from jax import lax
from jax.experimental import pallas as pl
from jax.experimental.pallas import tpu as pltpu
from jax.sharding import PartitionSpec as P

HEADS = 12
HEAD = 64
LANES = 128
EPS = 1e-05
F32 = jnp.float32
BF16 = jnp.bfloat16
ROWS = 256

LIGHT = pl.CostEstimate(flops=1000000, bytes_accessed=100000, transcendentals=0)


def contract(left, right, left_dim, right_dim):
    return lax.dot_general(
        left, right, (((left_dim,), (right_dim,)), ((), ())), preferred_element_type=F32
    )


def normalize(values, gain, bias):
    centered = values - jnp.mean(values, axis=-1, keepdims=True)
    variance = jnp.mean(centered * centered, axis=-1, keepdims=True)
    scale = lax.rsqrt(variance + EPS)
    xhat = centered * scale
    return xhat * gain + bias, xhat, scale


def normalize_back(grad, xhat, scale, gain):
    scaled = grad * gain
    first = jnp.mean(scaled, axis=-1, keepdims=True)
    cross = jnp.mean(scaled * xhat, axis=-1, keepdims=True)
    return scale * (scaled - first - xhat * cross)


def head_mask(parity, value):
    lane = lax.broadcasted_iota(jnp.int32, (1, LANES), 1)
    return jnp.where(lane // HEAD == parity, value, 0.0).astype(BF16)


def causal_bias(bias_ref, keys_dim):
    @pl.when((pl.program_id(0) == 0) & (pl.program_id(1) == 0))
    def _():
        key = lax.broadcasted_iota(jnp.int32, bias_ref.shape, keys_dim)
        query = lax.broadcasted_iota(jnp.int32, bias_ref.shape, 1 - keys_dim)
        bias_ref[...] = jnp.where(key <= query, 0.0, -1e30)


def attention_kernel(q_ref, k_ref, v_ref, o_ref, *refs, block):
    *probs_refs, bias_ref = refs
    causal_bias(bias_ref, 0)
    parity = pl.program_id(1)
    queries = q_ref[...] * head_mask(parity, HEAD**-0.5)
    values = v_ref[...] * head_mask(parity, 1.0)
    outs = []
    for index, probs_ref in enumerate(probs_refs):
        first, finish = index * block, (index + 1) * block
        scores = contract(k_ref[:finish, :], queries[first:finish], 1, 1)
        diagonal = scores[first:] + bias_ref[...]
        if index:
            scores = jnp.concatenate([scores[:first], diagonal], axis=0)
        else:
            scores = diagonal
        shifted = jnp.exp(scores - jnp.max(scores, axis=0, keepdims=True))
        total = jnp.sum(shifted, axis=0, keepdims=True)
        probs = (shifted * (1.0 / total)).astype(BF16)
        probs_ref[0] = probs
        outs.append(contract(probs, values[:finish], 0, 0).astype(BF16))
    mixed = jnp.concatenate(outs, axis=0)

    @pl.when(parity == 0)
    def _():
        o_ref[...] = mixed

    @pl.when(parity == 1)
    def _():
        o_ref[...] = o_ref[...] + mixed


def attention(queries, keys, values):
    length, width = queries.shape
    pairs = width // LANES
    block = min(256, length)
    finishes = range(block, length + 1, block)
    spec = pl.BlockSpec((length, LANES), lambda pair, parity: (0, pair))
    mixed, *probs = pl.pallas_call(
        functools.partial(attention_kernel, block=block),
        grid=(pairs, 2),
        in_specs=[spec, spec, spec],
        out_specs=[spec]
        + [
            pl.BlockSpec((1, finish, block), lambda pair, parity: (pair * 2 + parity, 0, 0))
            for finish in finishes
        ],
        out_shape=[jax.ShapeDtypeStruct((length, width), BF16)]
        + [jax.ShapeDtypeStruct((2 * pairs, finish, block), BF16) for finish in finishes],
        scratch_shapes=[pltpu.VMEM((block, block), F32)],
        cost_estimate=LIGHT,
        name="attention",
    )(queries, keys, values)
    return mixed, probs


def attention_back_kernel(
    core_ref, q_ref, k_ref, v_ref, g_ref, o_ref, turned_ref, *refs, block, blocks
):
    probs_refs = refs[:blocks]
    grads_ref, send_ref, keep_ref, dk_sum, dv_sum = refs[-5:]
    parity = pl.program_id(1)
    scale_mask = head_mask(parity, HEAD**-0.5)
    queries = q_ref[...] * scale_mask
    grads = g_ref[...] * head_mask(parity, 1.0)
    keys_scaled = k_ref[...] * scale_mask
    dk_sum[...] = jnp.zeros_like(dk_sum)
    dv_sum[...] = jnp.zeros_like(dv_sum)
    dq_parts = []
    for index, probs_ref in enumerate(probs_refs):
        first, finish = index * block, (index + 1) * block
        probs = probs_ref[0]
        some = grads[first:finish]
        dv_sum[:finish, :] += contract(probs, some, 1, 0)
        grad_probs = contract(v_ref[:finish, :], some, 1, 1)
        shares = some.astype(F32) * o_ref[first:finish, :].astype(F32)
        delta = jnp.sum(jnp.transpose(shares), axis=0, keepdims=True)
        grad_scores = (probs.astype(F32) * (grad_probs - delta)).astype(BF16)
        dk_sum[:finish, :] += contract(grad_scores, queries[first:finish], 1, 0)
        dq_parts.append(contract(grad_scores, keys_scaled[:finish], 0, 0).astype(BF16))
    parts = (
        jnp.concatenate(dq_parts, axis=0),
        dk_sum[...].astype(BF16),
        dv_sum[...].astype(BF16),
    )

    @pl.when(parity == 0)
    def _():
        for index, part in enumerate(parts):
            grads_ref[index] = part

    @pl.when(parity == 1)
    def _():
        whole = [grads_ref[index] + part for index, part in enumerate(parts)]
        for index, part in enumerate(whole):
            grads_ref[index] = part
        weight_parts(core_ref, turned_ref[...], jnp.concatenate(whole, axis=1), send_ref, keep_ref)


def weight_parts(core_ref, turned, grads, send_ref, keep_ref):
    product = contract(turned, grads, 1, 0).astype(BF16)
    rows = send_ref.shape[1]

    def write(upper, lower):
        for index in range(grads.shape[1] // LANES):
            columns = slice(index * LANES, (index + 1) * LANES)
            upper[index] = product[:rows, columns]
            lower[index] = product[rows:, columns]

    @pl.when(core_ref[0] == 0)
    def _():
        write(keep_ref, send_ref)

    @pl.when(core_ref[0] != 0)
    def _():
        write(send_ref, keep_ref)


SCALAR = pl.BlockSpec(memory_space=pltpu.SMEM)


def attention_back(core, queries, keys, values, grads, mixed, turned, probs, start, pairs, units):
    length, width = queries.shape
    block = probs[0].shape[2]
    spec = pl.BlockSpec((length, LANES), lambda pair, parity: (0, start + pair))
    whole = pl.BlockSpec((width, length), lambda pair, parity: (0, 0))
    ahead = 0 if units is None else units[0].shape[0] // 3 - pairs
    shape = jax.ShapeDtypeStruct((3 * (ahead + pairs), width // 2, LANES), BF16)
    unit = pl.BlockSpec((3, width // 2, LANES), lambda pair, parity: (ahead + pair, 0, 0))
    args = [core, queries, keys, values, grads, mixed, turned, *probs]
    alias = {}
    if units is not None:
        alias = {len(args): 1, len(args) + 1: 2}
        args += units
    return pl.pallas_call(
        functools.partial(attention_back_kernel, block=block, blocks=len(probs)),
        grid=(pairs, 2),
        in_specs=[SCALAR, spec, spec, spec, spec, spec, whole]
        + [
            pl.BlockSpec(
                (1, *part.shape[1:]), lambda pair, parity: ((start + pair) * 2 + parity, 0, 0)
            )
            for part in probs
        ]
        + [pl.BlockSpec(memory_space=pl.ANY)] * len(alias),
        out_specs=[pl.BlockSpec((3, length, LANES), lambda pair, parity: (0, 0, pair)), unit, unit],
        out_shape=[jax.ShapeDtypeStruct((3, length, pairs * LANES), BF16), shape, shape],
        input_output_aliases=alias,
        scratch_shapes=[pltpu.VMEM((length, LANES), F32)] * 2,
        cost_estimate=LIGHT,
        name="attention_back",
    )(*args)


def gelu_parts(value):
    cdf = 0.5 + 0.5 * lax.erf(value * 0.5**0.5)
    density = jnp.exp2(value * value * (-0.5 / math.log(2.0)))
    return cdf, value * (density * (1.0 / math.sqrt(2.0 * math.pi)))


def expert_kernel(
    x_ref, c_ref, cen_ref, up_ref, down_ref,
    y_ref, gs_ref, dy_ref, h_ref, dp_ref,
    y_sum, dx_sum, gate_ref,
):
    step = pl.program_id(0)

    @pl.when(step == 0)
    def _():
        logit = jnp.sum(x_ref[...].astype(F32) * cen_ref[...], axis=1, keepdims=True)
        gate = jax.nn.sigmoid(logit)
        gate_ref[...] = jnp.broadcast_to(gate, gate_ref.shape)
        dy_ref[...] = (c_ref[...].astype(F32) * gate).astype(BF16)
        y_sum[...] = jnp.zeros_like(y_sum)
        dx_sum[...] = jnp.zeros_like(dx_sum)

    pre = contract(x_ref[...], up_ref[0], 1, 0)
    cdf, weighted = gelu_parts(pre)
    hidden = (pre * cdf).astype(BF16)
    slope = cdf + weighted
    h_ref[...] = hidden
    y_sum[...] += contract(hidden, down_ref[0], 1, 0)
    grad_hidden = contract(dy_ref[...], down_ref[0], 1, 1)
    grad_pre = (grad_hidden * slope).astype(BF16)
    dp_ref[...] = grad_pre
    dx_sum[...] += contract(grad_pre, up_ref[0], 1, 1)

    @pl.when(step == pl.num_programs(0) - 1)
    def _():
        produced = y_sum[...].astype(BF16)
        y_ref[...] = produced
        gate = gate_ref[:, 0:1]
        dot = jnp.sum(c_ref[...].astype(F32) * produced.astype(F32), axis=1, keepdims=True)
        grad_logit = dot * gate * (1.0 - gate)
        back = dx_sum[...].astype(BF16).astype(F32) + grad_logit * cen_ref[...]
        gs_ref[...] = back.astype(BF16)


def expert(rows, cots, centroid, up, down):
    count, width = rows.shape
    hidden = up.shape[2]
    tile = min(512, hidden)
    whole = pl.BlockSpec((count, width), lambda f: (0, 0))
    wide = jax.ShapeDtypeStruct((count, width), BF16)
    deep = jax.ShapeDtypeStruct((count, hidden), BF16)
    return pl.pallas_call(
        expert_kernel,
        grid=(hidden // tile,),
        in_specs=[
            whole,
            whole,
            pl.BlockSpec((1, width), lambda f: (0, 0)),
            pl.BlockSpec((1, width, tile), lambda f: (0, 0, f)),
            pl.BlockSpec((1, tile, width), lambda f: (0, f, 0)),
        ],
        out_specs=[whole, whole, whole]
        + [pl.BlockSpec((count, tile), lambda f: (0, f))] * 2,
        out_shape=[wide, wide, wide, deep, deep],
        scratch_shapes=[
            pltpu.VMEM((count, width), F32),
            pltpu.VMEM((count, width), F32),
            pltpu.VMEM((count, LANES), F32),
        ],
        cost_estimate=LIGHT,
        name="expert",
    )(rows, cots, centroid, up, down)


def expert_weights_kernel(
    core_ref, x_ref, dy_ref, h_ref, dp_ref,
    up_send_ref, down_send_ref, up_keep_ref, down_keep_ref, xt_ref,
):
    @pl.when(pl.program_id(0) == 0)
    def _():
        xt_ref[...] = jnp.transpose(x_ref[...])

    up = contract(xt_ref[...], dp_ref[...], 1, 0).astype(BF16)
    down = contract(h_ref[...], dy_ref[...], 0, 0).astype(BF16)
    sending = pl.program_id(0) < pl.num_programs(0) // 2

    @pl.when(sending)
    def _():
        up_send_ref[0] = up
        down_send_ref[0] = down

    @pl.when(jnp.logical_not(sending))
    def _():
        up_keep_ref[0] = up
        down_keep_ref[0] = down


def expert_weights(rows, grads, hidden_rows, grad_pre, parts, core):
    count, width = rows.shape
    hidden = hidden_rows.shape[1]
    share = hidden // parts
    tile = min(384, share)
    each = share // tile
    half = hidden // tile // 2

    def column(f, core):
        step = f % half
        other = jnp.where(f < half, 1 - core[0], core[0])
        return ((step // each) * 2 + other) * each + step % each

    def send(f):
        return jnp.minimum(f, half - 1)

    def keep(f):
        return jnp.maximum(f - half, 0)

    whole = pl.BlockSpec((count, width), lambda f, core: (0, 0))
    deep = pl.BlockSpec((count, tile), lambda f, core: (0, column(f, core)))
    up = [
        pl.BlockSpec((1, width, tile), lambda f, core, at=at: (at(f) // each, 0, at(f) % each))
        for at in (send, keep)
    ]
    down = [
        pl.BlockSpec((1, tile, width), lambda f, core, at=at: (at(f) // each, at(f) % each, 0))
        for at in (send, keep)
    ]
    up_shape = jax.ShapeDtypeStruct((parts // 2, width, share), BF16)
    down_shape = jax.ShapeDtypeStruct((parts // 2, share, width), BF16)
    return pl.pallas_call(
        expert_weights_kernel,
        grid_spec=pltpu.PrefetchScalarGridSpec(
            num_scalar_prefetch=1,
            grid=(2 * half,),
            in_specs=[whole, whole, deep, deep],
            out_specs=[up[0], down[0], up[1], down[1]],
            scratch_shapes=[pltpu.VMEM((width, count), BF16)],
        ),
        out_shape=[up_shape, down_shape, up_shape, down_shape],
        cost_estimate=LIGHT,
        name="expert_weights",
    )(core, rows, grads, hidden_rows, grad_pre)


def one_hot(condition):
    return jnp.where(condition, 1.0, 0.0).astype(BF16)


def block_rows(step, count, length, dim):
    return step * count + lax.broadcasted_iota(jnp.int32, (count, length), dim)


def const(*shape):
    return pl.BlockSpec(shape, lambda *step: (0,) * len(shape))


def route_kernel(routing_ref, cot_ref, send_ref, slot_ref, wide_ref, *, experts, capacity):
    length = routing_ref.shape[1]
    step = pl.program_id(0)

    @pl.when(step == 0)
    def _():
        chosen = routing_ref[...]
        named = lax.broadcasted_iota(jnp.int32, (experts, length), 0) == chosen
        named = jnp.where(named, 1.0, 0.0)
        lane = lax.broadcasted_iota(jnp.int32, (experts, length), 1)
        count = named
        shift = 1
        while shift < length:
            count = count + jnp.where(lane >= shift, pltpu.roll(count, shift, 1), 0.0)
            shift *= 2
        position = jnp.sum(named * (count - named), axis=0, keepdims=True)
        slot = chosen.astype(F32) * capacity + position
        slot = jnp.where(position < capacity, slot, -1.0)
        slot_ref[...] = slot.astype(jnp.int32)
        wide_ref[...] = jnp.transpose(jnp.broadcast_to(slot, (LANES, length))).astype(jnp.int32)

    place = one_hot(block_rows(step, send_ref.shape[0], length, 0) == slot_ref[...])
    send_ref[...] = contract(place, cot_ref[...], 1, 0).astype(BF16)


def route(routing, cotangent, experts, capacity):
    length, width = cotangent.shape
    slots = experts * capacity
    return pl.pallas_call(
        functools.partial(route_kernel, experts=experts, capacity=capacity),
        grid=(slots // ROWS,),
        in_specs=[const(1, length), const(length, width)],
        out_specs=[
            pl.BlockSpec((ROWS, width), lambda i: (i, 0)),
            const(1, length),
            const(length, LANES),
        ],
        out_shape=[
            jax.ShapeDtypeStruct((slots, width), BF16),
            jax.ShapeDtypeStruct((1, length), jnp.int32),
            jax.ShapeDtypeStruct((length, LANES), jnp.int32),
        ],
        cost_estimate=LIGHT,
        name="route",
    )(routing, cotangent)


def project_kernel(
    tokens_ref, gain_ref, bias_ref, wq_ref, wk_ref, wv_ref, turned_ref, q_ref, k_ref, v_ref
):
    normed, _, _ = normalize(tokens_ref[...].astype(F32), gain_ref[...], bias_ref[...])
    normed = normed.astype(BF16)
    turned_ref[...] = jnp.transpose(normed)
    for weight, out in ((wq_ref, q_ref), (wk_ref, k_ref), (wv_ref, v_ref)):
        out[...] = contract(normed, weight[...], 1, 0).astype(BF16)


def project(tokens, gain, bias, weights):
    length, width = tokens.shape
    rows = pl.BlockSpec((ROWS, width), lambda i: (i, 0))
    out = jax.ShapeDtypeStruct((length, width), BF16)
    return pl.pallas_call(
        project_kernel,
        grid=(length // ROWS,),
        in_specs=[rows, const(1, width), const(1, width)] + [const(width, width)] * 3,
        out_specs=[pl.BlockSpec((width, ROWS), lambda i: (0, i))] + [rows] * 3,
        out_shape=[jax.ShapeDtypeStruct((width, length), BF16)] + [out] * 3,
        cost_estimate=LIGHT,
        name="project",
    )(tokens, gain, bias, *weights)


def branch_kernel(
    mixed_ref, tokens_ref, weight_ref, gain_ref, bias_ref, cen_ref, chosen_ref, slot_ref,
    resid_ref, gate_ref, turned_ref, send_ref, low_ref, *, blocks,
):
    step = pl.program_id(0)

    @pl.when(step < blocks)
    def _():
        mixed = mixed_ref[...]
        turned_ref[...] = jnp.transpose(mixed)
        resid = tokens_ref[...].astype(F32) + contract(mixed, weight_ref[...], 1, 0)
        second, _, _ = normalize(resid, gain_ref[...], bias_ref[...])
        resid_ref[...] = resid
        low_ref[pl.ds(pl.multiple_of(step * ROWS, ROWS), ROWS), :] = second.astype(BF16)
        centroid = jnp.zeros_like(second)
        for index in range(cen_ref.shape[0]):
            centroid = jnp.where(chosen_ref[...] == index, cen_ref[index : index + 1, :], centroid)
        gate_ref[...] = jax.nn.sigmoid(jnp.sum(second * centroid, axis=1, keepdims=True))

    @pl.when(step >= blocks)
    def _():
        place = one_hot(block_rows(step - blocks, ROWS, slot_ref.shape[1], 0) == slot_ref[...])
        send_ref[...] = contract(place, low_ref[...], 1, 0).astype(BF16)


def branch(mixed, tokens, weight, gain, bias, centroids, routing, slot, slots):
    length, width = mixed.shape
    blocks = length // ROWS

    def at(i):
        return jnp.minimum(i, blocks - 1)

    rows = pl.BlockSpec((ROWS, width), lambda i: (at(i), 0))
    thin = pl.BlockSpec((ROWS, 1), lambda i: (at(i), 0))
    return pl.pallas_call(
        functools.partial(branch_kernel, blocks=blocks),
        grid=(blocks + slots // ROWS,),
        in_specs=[
            rows,
            rows,
            const(width, width),
            const(1, width),
            const(1, width),
            const(*centroids.shape),
            thin,
            const(1, length),
        ],
        out_specs=[
            rows,
            thin,
            pl.BlockSpec((width, ROWS), lambda i: (0, at(i))),
            pl.BlockSpec((ROWS, width), lambda i: (jnp.maximum(i - blocks, 0), 0)),
        ],
        out_shape=[
            jax.ShapeDtypeStruct((length, width), F32),
            jax.ShapeDtypeStruct((length, 1), F32),
            jax.ShapeDtypeStruct((width, length), BF16),
            jax.ShapeDtypeStruct((slots, width), BF16),
        ],
        scratch_shapes=[pltpu.VMEM((length, width), BF16)],
        cost_estimate=LIGHT,
        name="branch",
    )(mixed, tokens, weight, gain, bias, centroids, routing, slot)


def gathered(wide_ref, rows_ref):
    slots = rows_ref.shape[0]
    count = wide_ref.shape[0]
    wide = jnp.concatenate([wide_ref[...]] * (slots // LANES), axis=1)
    place = one_hot(lax.broadcasted_iota(jnp.int32, (count, slots), 1) == wide)
    return contract(place, rows_ref[...], 1, 0)


def second_back_kernel(
    core_ref, wide_ref, back_ref, resid_ref, cot_ref, gain_ref, weight_ref, turned_ref,
    grad_ref, mixed_ref, sums_ref, send_ref, keep_ref, total_ref,
):
    grad = gathered(wide_ref, back_ref)
    _, xhat, scale = normalize(resid_ref[...], gain_ref[...], gain_ref[...])
    sums = jnp.concatenate(
        [jnp.sum(grad * xhat, axis=0, keepdims=True), jnp.sum(grad, axis=0, keepdims=True)], axis=0
    )

    @pl.when(pl.program_id(0) == 0)
    def _():
        sums_ref[...] = sums

    @pl.when(pl.program_id(0) > 0)
    def _():
        sums_ref[...] = sums_ref[...] + sums

    grad = cot_ref[...].astype(F32) + normalize_back(grad, xhat, scale, gain_ref[...])
    grad_ref[...] = grad
    low = grad.astype(BF16)
    mixed_ref[...] = contract(low, weight_ref[...], 1, 1).astype(BF16)
    product = contract(turned_ref[...], low, 1, 0)

    @pl.when(pl.program_id(0) == 0)
    def _():
        total_ref[...] = product

    @pl.when(pl.program_id(0) > 0)
    def _():
        total_ref[...] += product

    @pl.when(pl.program_id(0) == pl.num_programs(0) - 1)
    def _():
        rows = send_ref.shape[1]
        for index in range(send_ref.shape[0]):
            columns = slice(index * LANES, (index + 1) * LANES)
            for half, out in ((1 - core_ref[0], send_ref), (core_ref[0], keep_ref)):
                at = pl.ds(pl.multiple_of(half * rows, rows), rows)
                out[index] = total_ref[at, columns].astype(BF16)


def second_back(core, wide, back, resid, cotangent, gain, weight, turned, units):
    length, width = resid.shape
    rows = pl.BlockSpec((ROWS, width), lambda i: (i, 0))
    own = const(width // LANES, width // 2, LANES)
    shape = jax.ShapeDtypeStruct((units, width // 2, LANES), BF16)
    return pl.pallas_call(
        second_back_kernel,
        grid=(length // ROWS,),
        in_specs=[
            SCALAR,
            pl.BlockSpec((ROWS, LANES), lambda i: (i, 0)),
            const(*back.shape),
            rows,
            rows,
            const(1, width),
            const(width, width),
            pl.BlockSpec((width, ROWS), lambda i: (0, i)),
        ],
        out_specs=[rows, rows, const(2, width), own, own],
        out_shape=[
            jax.ShapeDtypeStruct((length, width), F32),
            jax.ShapeDtypeStruct((length, width), BF16),
            jax.ShapeDtypeStruct((2, width), F32),
            shape,
            shape,
        ],
        scratch_shapes=[pltpu.VMEM((width, width), F32)],
        cost_estimate=LIGHT,
        name="second_back",
    )(core, wide, back, resid, cotangent, gain, weight, turned)


def first_back_kernel(
    left_ref, right_ref, tokens_ref, resid_ref, gain_ref, wq_ref, wk_ref, wv_ref,
    grad_ref, sums_ref,
):
    side = left_ref.shape[2]
    grad = 0.0
    for index, weight in enumerate((wq_ref, wk_ref, wv_ref)):
        grad = grad + contract(left_ref[index], weight[:, :side], 1, 1)
        grad = grad + contract(right_ref[index], weight[:, side:], 1, 1)
    gain = gain_ref[...]
    _, xhat, scale = normalize(tokens_ref[...].astype(F32), gain, gain)
    sums = jnp.concatenate(
        [jnp.sum(grad * xhat, axis=0, keepdims=True), jnp.sum(grad, axis=0, keepdims=True)], axis=0
    )

    @pl.when(pl.program_id(0) == 0)
    def _():
        sums_ref[...] = sums

    @pl.when(pl.program_id(0) > 0)
    def _():
        sums_ref[...] = sums_ref[...] + sums

    grad_ref[...] = resid_ref[...] + normalize_back(grad, xhat, scale, gain)


def first_back(left, right, tokens, resid, gain, weights):
    length, width = tokens.shape
    rows = pl.BlockSpec((ROWS, width), lambda i: (i, 0))
    return pl.pallas_call(
        first_back_kernel,
        grid=(length // ROWS,),
        in_specs=[
            pl.BlockSpec((3, ROWS, part.shape[2]), lambda i: (0, i, 0)) for part in (left, right)
        ]
        + [rows, rows, const(1, width)]
        + [const(width, width)] * 3,
        out_specs=[rows, const(2, width)],
        out_shape=[
            jax.ShapeDtypeStruct((length, width), F32),
            jax.ShapeDtypeStruct((2, width), F32),
        ],
        cost_estimate=LIGHT,
        name="first_back",
    )(left, right, tokens, resid, gain, *weights)


def layer_out_kernel(wide_ref, rows_ref, resid_ref, gate_ref, out_ref):
    out_ref[...] = (resid_ref[...] + gate_ref[...] * gathered(wide_ref, rows_ref)).astype(BF16)


def layer_output(wide, produced, resid, gate):
    length, width = resid.shape
    rows = pl.BlockSpec((ROWS, width), lambda i: (i, 0))
    return pl.pallas_call(
        layer_out_kernel,
        grid=(length // ROWS,),
        in_specs=[
            pl.BlockSpec((ROWS, LANES), lambda i: (i, 0)),
            const(*produced.shape),
            rows,
            pl.BlockSpec((ROWS, 1), lambda i: (i, 0)),
        ],
        out_specs=rows,
        out_shape=jax.ShapeDtypeStruct((length, width), BF16),
        cost_estimate=LIGHT,
        name="layer_output",
    )(wide, produced, resid, gate)


def assemble_kernel(core_ref, early_mine, early_other, late_mine, late_other, *outs):
    mine = pl.program_id(0) == core_ref[0]
    columns = outs[0].shape[1] // LANES

    def write(early, late):
        for index in range(columns):
            outs[0][:, index * LANES : (index + 1) * LANES] = early[index].astype(F32)
        for part in (early, late):
            first = columns if part is early else 0
            pair = 0 if part is early else (early.shape[0] - columns) // 3
            for unit in range(first, part.shape[0]):
                at = pair + (unit - first) // 3
                outs[1 + (unit - first) % 3][:, at * LANES : (at + 1) * LANES] = part[unit].astype(F32)

    @pl.when(mine)
    def _():
        write(early_mine, late_mine)

    @pl.when(jnp.logical_not(mine))
    def _():
        write(early_other, late_other)


def assemble(core, early_mine, early_other, late_mine, late_other, width):
    args = [
        part.reshape(-1, width // 2, LANES)
        for part in (early_mine, early_other, late_mine, late_other)
    ]
    out = jax.ShapeDtypeStruct((width, width), F32)
    return pl.pallas_call(
        assemble_kernel,
        grid_spec=pltpu.PrefetchScalarGridSpec(
            num_scalar_prefetch=1,
            grid=(2,),
            in_specs=[const(*part.shape) for part in args],
            out_specs=[pl.BlockSpec((width // 2, width), lambda i, core: (i, 0))] * 4,
        ),
        out_shape=[out] * 4,
        cost_estimate=LIGHT,
        name="assemble",
    )(core, *args)


def swap(value, axis, bit):
    size = lax.axis_size(axis)
    return lax.ppermute(value, axis, [(i, i ^ bit) for i in range(size)])


def stages(axis, low, high):
    found = []
    bit = low
    while bit < min(high, lax.axis_size(axis)):
        found.append((axis, bit))
        bit *= 2
    return found


def bit_of(axis, bit):
    return (lax.axis_index(axis) // bit) % 2


def add_low(left, right):
    return (left.astype(F32) + right.astype(F32)).astype(BF16)


def add(left, right):
    return left + right


def halves(rows, stage):
    axis, bit = stage
    half = rows.shape[0] // 2
    mine = bit_of(axis, bit)
    return (
        lax.dynamic_slice_in_dim(rows, (1 - mine) * half, half, 0),
        lax.dynamic_slice_in_dim(rows, mine * half, half, 0),
    )


def joined(rows, other, stage):
    first = bit_of(*stage) == 0
    return jnp.concatenate([jnp.where(first, rows, other), jnp.where(first, other, rows)], axis=0)


def add_split_kernel(mine_ref, left_ref, right_ref, send_ref, keep_ref):
    value = add_low(left_ref[...], right_ref[...])

    @pl.when(pl.program_id(0) == 0)
    def _():
        send_ref[...] = value

    @pl.when(pl.program_id(0) == 1)
    def _():
        keep_ref[...] = value


def add_split(left, right, stage):
    half, width = left.shape[0] // 2, left.shape[1]
    if half % 8:
        return halves(add_low(left, right), stage)
    mine = bit_of(*stage).astype(jnp.int32)[None]
    block = pl.BlockSpec((half, width), lambda i, mine: (jnp.where(i == 0, 1 - mine[0], mine[0]), 0))
    out = pl.BlockSpec((half, width), lambda i, mine: (0, 0))
    shape = jax.ShapeDtypeStruct((half, width), BF16)
    return pl.pallas_call(
        add_split_kernel,
        grid_spec=pltpu.PrefetchScalarGridSpec(
            num_scalar_prefetch=1,
            grid=(2,),
            in_specs=[block, block],
            out_specs=[out, out],
        ),
        out_shape=[shape, shape],
        cost_estimate=LIGHT,
        name="add_split",
    )(mine, left, right)


def halves_sum(left, right, stage):
    width = left.shape[2]
    parts = add_split(left.reshape(-1, width), right.reshape(-1, width), stage)
    return [part.reshape(-1, *left.shape[1:]) for part in parts]


class Sum:
    def __init__(self, keep, send, stages, plus=add_low, split=True):
        self.keep, self.send, self.plus = keep, send, plus
        if split:
            self.steps = [("whole", stages[0])]
            self.steps += [("halve", stage) for stage in stages[1:-1]]
            self.steps += [("whole", stages[-1])]
            self.steps += [("join", stage) for stage in stages[-2:0:-1]]
        else:
            self.steps = [("whole", stage) for stage in stages]

    def start(self):
        return swap(self.send, *self.steps[0][1])

    def finish(self, got):
        kind, stage = self.steps.pop(0)
        if self.steps and self.steps[0][0] == "halve":
            self.send, self.keep = add_split(self.keep, got, self.steps[0][1])
        else:
            join = functools.partial(joined, stage=stage)
            self.keep = self.send = (join if kind == "join" else self.plus)(self.keep, got)


def advance(sums, *others):
    sums = [each for each in sums if each.steps]
    tied = tie((*(each.start() for each in sums), *others))
    for each, got in zip(sums, tied):
        each.finish(got)
    rest = tied[len(sums) :]
    return rest[0] if len(rest) == 1 else rest


def chip_stages(total):
    return [("dp", 2 << index) for index in range((total.shape[0]).bit_length() - 1)][::-1]


tie = lax.optimization_barrier


def exchange(rows):
    return lax.all_to_all(rows, "expert", split_axis=0, concat_axis=0, tiled=True)


def local(
    tokens,
    routing,
    query_weight,
    key_weight,
    value_weight,
    output_weight,
    first_gain,
    first_bias,
    second_gain,
    second_bias,
    centroids,
    expert_up,
    expert_down,
    cotangent,
):
    length, width = tokens.shape
    experts = centroids.shape[0]
    capacity = length // experts
    peers = lax.axis_size("expert")
    parts = lax.axis_size("dp")
    slots = experts * capacity
    core = (lax.axis_index("dp") % 2).astype(jnp.int32)[None]
    vectors = tie(jnp.stack([first_gain, first_bias, second_gain, second_bias]))
    first_gain, first_bias, second_gain, second_bias = (vectors[i : i + 1] for i in range(4))
    weights = (query_weight, key_weight, value_weight)

    cots, slot, wide = route(routing.reshape(1, length), cotangent, experts, capacity)
    cots, tokens = tie((cots, tokens))
    cots = exchange(cots.reshape(peers, -1, width)).reshape(slots, width)

    normed_turned, queries, keys, values = project(tokens, first_gain, first_bias, weights)
    mixed, probs = attention(queries, keys, values)
    mixed, cots = tie((mixed, cots))
    resid, gate, mixed_turned, rows = branch(
        mixed, tokens, output_weight, second_gain, second_bias, centroids, routing, slot, slots
    )

    rows = exchange(rows.reshape(peers, -1, width)).reshape(slots, width)
    own = centroids[lax.axis_index("expert")][None, :]
    produced, returned, grad_rows, hidden, grad_pre = expert(
        rows, cots, own, expert_up, expert_down
    )
    returned = exchange(returned.reshape(peers, -1, width))
    up_send, down_send, up_keep, down_keep = expert_weights(
        rows, grad_rows, hidden, grad_pre, parts, core
    )
    chips = chip_stages(up_send)
    up_send, up_keep = halves_sum(up_keep, swap(up_send, "dp", 1), chips[0])
    down_send, down_keep = halves_sum(down_keep, swap(down_send, "dp", 1), chips[0])
    returned, produced, up_send, up_keep, down_send, down_keep = tie(
        (returned, produced, up_send, up_keep, down_send, down_keep)
    )
    returned = returned.reshape(slots, width)
    up_got = swap(up_send, *chips[0])
    down_got = swap(down_send, *chips[0])
    produced = exchange(produced.reshape(peers, -1, width))

    pairs = width // LANES
    split = pairs // 2
    grad_resid, grad_mixed, second_sums, *units = second_back(
        core, wide, returned, resid, cotangent, second_gain, output_weight, mixed_turned,
        pairs + 3 * split,
    )

    cross = stages("expert", 1, 1 << 20)
    apart = stages("dp", 2, 1 << 20)
    back = functools.partial(
        attention_back, core, queries, keys, values, grad_mixed, mixed, normed_turned
    )
    left, send, keep = back(probs, 0, split, units)
    left, send, keep, up_got = tie((left, send, keep, up_got))
    early = Sum(keep.reshape(-1, LANES), send.reshape(-1, LANES), [("dp", 1)] + cross + apart)
    advance([early])
    early.send, *probs = tie((early.send, *probs))
    right, send, keep = back(probs, split, pairs - split, None)
    right, send, keep, produced = advance([early], right, send, keep, produced)
    produced = produced.reshape(slots, width)
    late = Sum(keep.reshape(-1, LANES), send.reshape(-1, LANES), [("dp", 1)] + apart + cross)
    layer_out = layer_output(wide, produced, resid, gate)
    layer_out, down_got = advance([early, late], layer_out, down_got)
    grad_tokens, first_sums = first_back(left, right, tokens, grad_resid, first_gain, weights)
    grad_tokens, first_sums = advance([early, late], grad_tokens, first_sums)
    grad_up = up_keep.astype(F32) + up_got.astype(F32)
    grad_down = down_keep.astype(F32) + down_got.astype(F32)
    for stage in chips[1:]:
        grad_up, grad_down = (
            keep.astype(F32) + swap(send, *stage).astype(F32)
            for send, keep in (halves(value.astype(BF16), stage) for value in (grad_up, grad_down))
        )
    grad_up, grad_down = (value.reshape(value.shape[1:])[None] for value in (grad_up, grad_down))
    small = jnp.concatenate([first_sums, second_sums], axis=0)
    small = Sum(small, small, stages("dp", 1, 1 << 20) + cross, plus=add, split=False)
    grad_up, grad_down = advance([early, late, small], grad_up, grad_down)
    while early.steps or late.steps or small.steps:
        advance([early, late, small])
    early, late, small = early.keep, late.keep, small.keep
    grad_output, grad_query, grad_key, grad_value = assemble(
        core, early, swap(early, "dp", 1), late, swap(late, "dp", 1), width
    )
    return (
        layer_out,
        grad_tokens,
        grad_query,
        grad_key,
        grad_value,
        grad_output,
        small[0],
        small[1],
        small[2],
        small[3],
        grad_up,
        grad_down,
    )


def solution(mesh):
    rows = P(("dp", "expert"), None)
    return jax.shard_map(
        local,
        mesh=mesh,
        in_specs=(rows, rows)
        + (P(),) * 9
        + (P("expert", None, None), P("expert", None, None), rows),
        out_specs=(rows, rows) + (P(),) * 8 + (P("expert", None, "dp"), P("expert", "dp", None)),
        check_vma=False,
    )
```

```python
import functools
import math

import jax
import jax.numpy as jnp
from jax import lax
from jax.experimental import pallas as pl
from jax.experimental.pallas import tpu as pltpu
from jax.sharding import PartitionSpec as P

HEADS = 12
HEAD = 64
LANES = 128
EPS = 1e-05
F32 = jnp.float32
BF16 = jnp.bfloat16
ROWS = 256

LIGHT = pl.CostEstimate(flops=1000000, bytes_accessed=100000, transcendentals=0)


def contract(left, right, left_dim, right_dim):
    return lax.dot_general(
        left, right, (((left_dim,), (right_dim,)), ((), ())), preferred_element_type=F32
    )


def normalize(values, gain, bias):
    centered = values - jnp.mean(values, axis=-1, keepdims=True)
    variance = jnp.mean(centered * centered, axis=-1, keepdims=True)
    scale = lax.rsqrt(variance + EPS)
    xhat = centered * scale
    return xhat * gain + bias, xhat, scale


def normalize_back(grad, xhat, scale, gain):
    scaled = grad * gain
    first = jnp.mean(scaled, axis=-1, keepdims=True)
    cross = jnp.mean(scaled * xhat, axis=-1, keepdims=True)
    return scale * (scaled - first - xhat * cross)


def head_mask(parity, value):
    lane = lax.broadcasted_iota(jnp.int32, (1, LANES), 1)
    return jnp.where(lane // HEAD == parity, value, 0.0).astype(BF16)


def causal_bias(bias_ref, keys_dim):
    @pl.when((pl.program_id(0) == 0) & (pl.program_id(1) == 0))
    def _():
        key = lax.broadcasted_iota(jnp.int32, bias_ref.shape, keys_dim)
        query = lax.broadcasted_iota(jnp.int32, bias_ref.shape, 1 - keys_dim)
        bias_ref[...] = jnp.where(key <= query, 0.0, -1e30)


def attention_kernel(q_ref, k_ref, v_ref, o_ref, *refs, block):
    *probs_refs, bias_ref = refs
    causal_bias(bias_ref, 0)
    parity = pl.program_id(1)
    queries = q_ref[...] * head_mask(parity, HEAD**-0.5)
    values = v_ref[...] * head_mask(parity, 1.0)
    outs = []
    for index, probs_ref in enumerate(probs_refs):
        first, finish = index * block, (index + 1) * block
        scores = contract(k_ref[:finish, :], queries[first:finish], 1, 1)
        diagonal = scores[first:] + bias_ref[...]
        if index:
            scores = jnp.concatenate([scores[:first], diagonal], axis=0)
        else:
            scores = diagonal
        shifted = jnp.exp(scores - jnp.max(scores, axis=0, keepdims=True))
        total = jnp.sum(shifted, axis=0, keepdims=True)
        probs = (shifted * (1.0 / total)).astype(BF16)
        probs_ref[0] = probs
        outs.append(contract(probs, values[:finish], 0, 0).astype(BF16))
    mixed = jnp.concatenate(outs, axis=0)

    @pl.when(parity == 0)
    def _():
        o_ref[...] = mixed

    @pl.when(parity == 1)
    def _():
        o_ref[...] = o_ref[...] + mixed


def attention(queries, keys, values):
    length, width = queries.shape
    pairs = width // LANES
    block = min(256, length)
    finishes = range(block, length + 1, block)
    spec = pl.BlockSpec((length, LANES), lambda pair, parity: (0, pair))
    mixed, *probs = pl.pallas_call(
        functools.partial(attention_kernel, block=block),
        grid=(pairs, 2),
        in_specs=[spec, spec, spec],
        out_specs=[spec]
        + [
            pl.BlockSpec((1, finish, block), lambda pair, parity: (pair * 2 + parity, 0, 0))
            for finish in finishes
        ],
        out_shape=[jax.ShapeDtypeStruct((length, width), BF16)]
        + [jax.ShapeDtypeStruct((2 * pairs, finish, block), BF16) for finish in finishes],
        scratch_shapes=[pltpu.VMEM((block, block), F32)],
        cost_estimate=LIGHT,
        name="attention",
    )(queries, keys, values)
    return mixed, probs


def attention_back_kernel(
    core_ref, q_ref, k_ref, v_ref, g_ref, o_ref, turned_ref, *refs, block, blocks
):
    probs_refs = refs[:blocks]
    grads_ref, send_ref, keep_ref, dk_sum, dv_sum = refs[-5:]
    parity = pl.program_id(1)
    scale_mask = head_mask(parity, HEAD**-0.5)
    queries = q_ref[...] * scale_mask
    grads = g_ref[...] * head_mask(parity, 1.0)
    keys_scaled = k_ref[...] * scale_mask
    dk_sum[...] = jnp.zeros_like(dk_sum)
    dv_sum[...] = jnp.zeros_like(dv_sum)
    dq_parts = []
    for index, probs_ref in enumerate(probs_refs):
        first, finish = index * block, (index + 1) * block
        probs = probs_ref[0]
        some = grads[first:finish]
        dv_sum[:finish, :] += contract(probs, some, 1, 0)
        grad_probs = contract(v_ref[:finish, :], some, 1, 1)
        shares = some.astype(F32) * o_ref[first:finish, :].astype(F32)
        delta = jnp.sum(jnp.transpose(shares), axis=0, keepdims=True)
        grad_scores = (probs.astype(F32) * (grad_probs - delta)).astype(BF16)
        dk_sum[:finish, :] += contract(grad_scores, queries[first:finish], 1, 0)
        dq_parts.append(contract(grad_scores, keys_scaled[:finish], 0, 0).astype(BF16))
    parts = (
        jnp.concatenate(dq_parts, axis=0),
        dk_sum[...].astype(BF16),
        dv_sum[...].astype(BF16),
    )

    @pl.when(parity == 0)
    def _():
        for index, part in enumerate(parts):
            grads_ref[index] = part

    @pl.when(parity == 1)
    def _():
        whole = [grads_ref[index] + part for index, part in enumerate(parts)]
        for index, part in enumerate(whole):
            grads_ref[index] = part
        weight_parts(core_ref, turned_ref[...], jnp.concatenate(whole, axis=1), send_ref, keep_ref)


def weight_parts(core_ref, turned, grads, send_ref, keep_ref):
    product = contract(turned, grads, 1, 0).astype(BF16)
    rows = send_ref.shape[1]

    def write(upper, lower):
        for index in range(grads.shape[1] // LANES):
            columns = slice(index * LANES, (index + 1) * LANES)
            upper[index] = product[:rows, columns]
            lower[index] = product[rows:, columns]

    @pl.when(core_ref[0] == 0)
    def _():
        write(keep_ref, send_ref)

    @pl.when(core_ref[0] != 0)
    def _():
        write(send_ref, keep_ref)


SCALAR = pl.BlockSpec(memory_space=pltpu.SMEM)


def attention_back(core, queries, keys, values, grads, mixed, turned, probs, start, pairs, units):
    length, width = queries.shape
    block = probs[0].shape[2]
    spec = pl.BlockSpec((length, LANES), lambda pair, parity: (0, start + pair))
    whole = pl.BlockSpec((width, length), lambda pair, parity: (0, 0))
    ahead = 0 if units is None else units[0].shape[0] // 3 - pairs
    shape = jax.ShapeDtypeStruct((3 * (ahead + pairs), width // 2, LANES), BF16)
    unit = pl.BlockSpec((3, width // 2, LANES), lambda pair, parity: (ahead + pair, 0, 0))
    args = [core, queries, keys, values, grads, mixed, turned, *probs]
    alias = {}
    if units is not None:
        alias = {len(args): 1, len(args) + 1: 2}
        args += units
    return pl.pallas_call(
        functools.partial(attention_back_kernel, block=block, blocks=len(probs)),
        grid=(pairs, 2),
        in_specs=[SCALAR, spec, spec, spec, spec, spec, whole]
        + [
            pl.BlockSpec(
                (1, *part.shape[1:]), lambda pair, parity: ((start + pair) * 2 + parity, 0, 0)
            )
            for part in probs
        ]
        + [pl.BlockSpec(memory_space=pl.ANY)] * len(alias),
        out_specs=[pl.BlockSpec((3, length, LANES), lambda pair, parity: (0, 0, pair)), unit, unit],
        out_shape=[jax.ShapeDtypeStruct((3, length, pairs * LANES), BF16), shape, shape],
        input_output_aliases=alias,
        scratch_shapes=[pltpu.VMEM((length, LANES), F32)] * 2,
        cost_estimate=LIGHT,
        name="attention_back",
    )(*args)


def gelu_parts(value):
    cdf = 0.5 + 0.5 * lax.erf(value * 0.5**0.5)
    density = jnp.exp2(value * value * (-0.5 / math.log(2.0)))
    return cdf, value * (density * (1.0 / math.sqrt(2.0 * math.pi)))


def expert_cots_kernel(c_ref, down_ref, out_ref):
    out_ref[...] = contract(c_ref[...], down_ref[0], 1, 1).astype(BF16)


def expert_cots(cots, down):
    count, width = cots.shape
    hidden = down.shape[1]
    tile = min(512, hidden)
    return pl.pallas_call(
        expert_cots_kernel,
        grid=(hidden // tile,),
        in_specs=[
            pl.BlockSpec((count, width), lambda f: (0, 0)),
            pl.BlockSpec((1, tile, width), lambda f: (0, f, 0)),
        ],
        out_specs=pl.BlockSpec((count, tile), lambda f: (0, f)),
        out_shape=jax.ShapeDtypeStruct((count, hidden), BF16),
        cost_estimate=LIGHT,
        name="expert_cots",
    )(cots, down)


def expert_kernel(
    x_ref, c_ref, cd_ref, cen_ref, up_ref, down_ref,
    y_ref, gs_ref, dy_ref, h_ref, dp_ref,
    y_sum, dx_sum, gate_ref,
):
    step = pl.program_id(0)

    @pl.when(step == 0)
    def _():
        logit = jnp.sum(x_ref[...].astype(F32) * cen_ref[...], axis=1, keepdims=True)
        gate = jax.nn.sigmoid(logit)
        gate_ref[...] = jnp.broadcast_to(gate, gate_ref.shape)
        dy_ref[...] = (c_ref[...].astype(F32) * gate).astype(BF16)
        y_sum[...] = jnp.zeros_like(y_sum)
        dx_sum[...] = jnp.zeros_like(dx_sum)

    pre = contract(x_ref[...], up_ref[0], 1, 0)
    cdf, weighted = gelu_parts(pre)
    hidden = (pre * cdf).astype(BF16)
    slope = cdf + weighted
    h_ref[...] = hidden
    y_sum[...] += contract(hidden, down_ref[0], 1, 0)
    grad_hidden = cd_ref[...].astype(F32) * gate_ref[:, 0:1]
    grad_pre = (grad_hidden * slope).astype(BF16)
    dp_ref[...] = grad_pre
    dx_sum[...] += contract(grad_pre, up_ref[0], 1, 1)

    @pl.when(step == pl.num_programs(0) - 1)
    def _():
        produced = y_sum[...].astype(BF16)
        y_ref[...] = produced
        gate = gate_ref[:, 0:1]
        dot = jnp.sum(c_ref[...].astype(F32) * produced.astype(F32), axis=1, keepdims=True)
        grad_logit = dot * gate * (1.0 - gate)
        back = dx_sum[...].astype(BF16).astype(F32) + grad_logit * cen_ref[...]
        gs_ref[...] = back.astype(BF16)


def expert(rows, cots, cots_down, centroid, up, down):
    count, width = rows.shape
    hidden = up.shape[2]
    tile = min(512, hidden)
    whole = pl.BlockSpec((count, width), lambda f: (0, 0))
    wide = jax.ShapeDtypeStruct((count, width), BF16)
    deep = jax.ShapeDtypeStruct((count, hidden), BF16)
    return pl.pallas_call(
        expert_kernel,
        grid=(hidden // tile,),
        in_specs=[
            whole,
            whole,
            pl.BlockSpec((count, tile), lambda f: (0, f)),
            pl.BlockSpec((1, width), lambda f: (0, 0)),
            pl.BlockSpec((1, width, tile), lambda f: (0, 0, f)),
            pl.BlockSpec((1, tile, width), lambda f: (0, f, 0)),
        ],
        out_specs=[whole, whole, whole]
        + [pl.BlockSpec((count, tile), lambda f: (0, f))] * 2,
        out_shape=[wide, wide, wide, deep, deep],
        scratch_shapes=[
            pltpu.VMEM((count, width), F32),
            pltpu.VMEM((count, width), F32),
            pltpu.VMEM((count, LANES), F32),
        ],
        cost_estimate=LIGHT,
        name="expert",
    )(rows, cots, cots_down, centroid, up, down)


def expert_weights_kernel(
    core_ref, x_ref, dy_ref, h_ref, dp_ref,
    up_send_ref, down_send_ref, up_keep_ref, down_keep_ref, xt_ref,
):
    @pl.when(pl.program_id(0) == 0)
    def _():
        xt_ref[...] = jnp.transpose(x_ref[...])

    up = contract(xt_ref[...], dp_ref[...], 1, 0).astype(BF16)
    down = contract(h_ref[...], dy_ref[...], 0, 0).astype(BF16)
    sending = pl.program_id(0) < pl.num_programs(0) // 2

    @pl.when(sending)
    def _():
        up_send_ref[0] = up
        down_send_ref[0] = down

    @pl.when(jnp.logical_not(sending))
    def _():
        up_keep_ref[0] = up
        down_keep_ref[0] = down


def expert_weights(rows, grads, hidden_rows, grad_pre, parts, core):
    count, width = rows.shape
    hidden = hidden_rows.shape[1]
    share = hidden // parts
    tile = min(384, share)
    each = share // tile
    half = hidden // tile // 2

    def column(f, core):
        step = f % half
        other = jnp.where(f < half, 1 - core[0], core[0])
        return ((step // each) * 2 + other) * each + step % each

    def send(f):
        return jnp.minimum(f, half - 1)

    def keep(f):
        return jnp.maximum(f - half, 0)

    whole = pl.BlockSpec((count, width), lambda f, core: (0, 0))
    deep = pl.BlockSpec((count, tile), lambda f, core: (0, column(f, core)))
    up = [
        pl.BlockSpec((1, width, tile), lambda f, core, at=at: (at(f) // each, 0, at(f) % each))
        for at in (send, keep)
    ]
    down = [
        pl.BlockSpec((1, tile, width), lambda f, core, at=at: (at(f) // each, at(f) % each, 0))
        for at in (send, keep)
    ]
    up_shape = jax.ShapeDtypeStruct((parts // 2, width, share), BF16)
    down_shape = jax.ShapeDtypeStruct((parts // 2, share, width), BF16)
    return pl.pallas_call(
        expert_weights_kernel,
        grid_spec=pltpu.PrefetchScalarGridSpec(
            num_scalar_prefetch=1,
            grid=(2 * half,),
            in_specs=[whole, whole, deep, deep],
            out_specs=[up[0], down[0], up[1], down[1]],
            scratch_shapes=[pltpu.VMEM((width, count), BF16)],
        ),
        out_shape=[up_shape, down_shape, up_shape, down_shape],
        cost_estimate=LIGHT,
        name="expert_weights",
    )(core, rows, grads, hidden_rows, grad_pre)


def one_hot(condition):
    return jnp.where(condition, 1.0, 0.0).astype(BF16)


def block_rows(step, count, length, dim):
    return step * count + lax.broadcasted_iota(jnp.int32, (count, length), dim)


def const(*shape):
    return pl.BlockSpec(shape, lambda *step: (0,) * len(shape))


def route_kernel(routing_ref, cot_ref, send_ref, slot_ref, wide_ref, *, experts, capacity):
    length = routing_ref.shape[1]
    step = pl.program_id(0)

    @pl.when(step == 0)
    def _():
        chosen = routing_ref[...]
        named = lax.broadcasted_iota(jnp.int32, (experts, length), 0) == chosen
        named = jnp.where(named, 1.0, 0.0)
        lane = lax.broadcasted_iota(jnp.int32, (experts, length), 1)
        count = named
        shift = 1
        while shift < length:
            count = count + jnp.where(lane >= shift, pltpu.roll(count, shift, 1), 0.0)
            shift *= 2
        position = jnp.sum(named * (count - named), axis=0, keepdims=True)
        slot = chosen.astype(F32) * capacity + position
        slot = jnp.where(position < capacity, slot, -1.0)
        slot_ref[...] = slot.astype(jnp.int32)
        wide_ref[...] = jnp.transpose(jnp.broadcast_to(slot, (LANES, length))).astype(jnp.int32)

    place = one_hot(block_rows(step, send_ref.shape[0], length, 0) == slot_ref[...])
    send_ref[...] = contract(place, cot_ref[...], 1, 0).astype(BF16)


def route(routing, cotangent, experts, capacity):
    length, width = cotangent.shape
    slots = experts * capacity
    return pl.pallas_call(
        functools.partial(route_kernel, experts=experts, capacity=capacity),
        grid=(slots // ROWS,),
        in_specs=[const(1, length), const(length, width)],
        out_specs=[
            pl.BlockSpec((ROWS, width), lambda i: (i, 0)),
            const(1, length),
            const(length, LANES),
        ],
        out_shape=[
            jax.ShapeDtypeStruct((slots, width), BF16),
            jax.ShapeDtypeStruct((1, length), jnp.int32),
            jax.ShapeDtypeStruct((length, LANES), jnp.int32),
        ],
        cost_estimate=LIGHT,
        name="route",
    )(routing, cotangent)


def project_kernel(
    tokens_ref, gain_ref, bias_ref, wq_ref, wk_ref, wv_ref, turned_ref, q_ref, k_ref, v_ref
):
    normed, _, _ = normalize(tokens_ref[...].astype(F32), gain_ref[...], bias_ref[...])
    normed = normed.astype(BF16)
    turned_ref[...] = jnp.transpose(normed)
    for weight, out in ((wq_ref, q_ref), (wk_ref, k_ref), (wv_ref, v_ref)):
        out[...] = contract(normed, weight[...], 1, 0).astype(BF16)


def project(tokens, gain, bias, weights):
    length, width = tokens.shape
    rows = pl.BlockSpec((ROWS, width), lambda i: (i, 0))
    out = jax.ShapeDtypeStruct((length, width), BF16)
    return pl.pallas_call(
        project_kernel,
        grid=(length // ROWS,),
        in_specs=[rows, const(1, width), const(1, width)] + [const(width, width)] * 3,
        out_specs=[pl.BlockSpec((width, ROWS), lambda i: (0, i))] + [rows] * 3,
        out_shape=[jax.ShapeDtypeStruct((width, length), BF16)] + [out] * 3,
        cost_estimate=LIGHT,
        name="project",
    )(tokens, gain, bias, *weights)


def branch_kernel(
    mixed_ref, tokens_ref, weight_ref, gain_ref, bias_ref, cen_ref, chosen_ref, slot_ref,
    resid_ref, gate_ref, turned_ref, send_ref, low_ref, *, blocks,
):
    step = pl.program_id(0)

    @pl.when(step < blocks)
    def _():
        mixed = mixed_ref[...]
        turned_ref[...] = jnp.transpose(mixed)
        resid = tokens_ref[...].astype(F32) + contract(mixed, weight_ref[...], 1, 0)
        second, _, _ = normalize(resid, gain_ref[...], bias_ref[...])
        resid_ref[...] = resid
        low_ref[pl.ds(pl.multiple_of(step * ROWS, ROWS), ROWS), :] = second.astype(BF16)
        centroid = jnp.zeros_like(second)
        for index in range(cen_ref.shape[0]):
            centroid = jnp.where(chosen_ref[...] == index, cen_ref[index : index + 1, :], centroid)
        gate_ref[...] = jax.nn.sigmoid(jnp.sum(second * centroid, axis=1, keepdims=True))

    @pl.when(step >= blocks)
    def _():
        place = one_hot(block_rows(step - blocks, ROWS, slot_ref.shape[1], 0) == slot_ref[...])
        send_ref[...] = contract(place, low_ref[...], 1, 0).astype(BF16)


def branch(mixed, tokens, weight, gain, bias, centroids, routing, slot, slots):
    length, width = mixed.shape
    blocks = length // ROWS

    def at(i):
        return jnp.minimum(i, blocks - 1)

    rows = pl.BlockSpec((ROWS, width), lambda i: (at(i), 0))
    thin = pl.BlockSpec((ROWS, 1), lambda i: (at(i), 0))
    return pl.pallas_call(
        functools.partial(branch_kernel, blocks=blocks),
        grid=(blocks + slots // ROWS,),
        in_specs=[
            rows,
            rows,
            const(width, width),
            const(1, width),
            const(1, width),
            const(*centroids.shape),
            thin,
            const(1, length),
        ],
        out_specs=[
            rows,
            thin,
            pl.BlockSpec((width, ROWS), lambda i: (0, at(i))),
            pl.BlockSpec((ROWS, width), lambda i: (jnp.maximum(i - blocks, 0), 0)),
        ],
        out_shape=[
            jax.ShapeDtypeStruct((length, width), F32),
            jax.ShapeDtypeStruct((length, 1), F32),
            jax.ShapeDtypeStruct((width, length), BF16),
            jax.ShapeDtypeStruct((slots, width), BF16),
        ],
        scratch_shapes=[pltpu.VMEM((length, width), BF16)],
        cost_estimate=LIGHT,
        name="branch",
    )(mixed, tokens, weight, gain, bias, centroids, routing, slot)


def gathered(wide_ref, rows_ref):
    slots = rows_ref.shape[0]
    count = wide_ref.shape[0]
    wide = jnp.concatenate([wide_ref[...]] * (slots // LANES), axis=1)
    place = one_hot(lax.broadcasted_iota(jnp.int32, (count, slots), 1) == wide)
    return contract(place, rows_ref[...], 1, 0)


def second_back_kernel(
    core_ref, wide_ref, back_ref, resid_ref, cot_ref, gain_ref, weight_ref, turned_ref,
    grad_ref, mixed_ref, sums_ref, send_ref, keep_ref, total_ref,
):
    grad = gathered(wide_ref, back_ref)
    _, xhat, scale = normalize(resid_ref[...], gain_ref[...], gain_ref[...])
    sums = jnp.concatenate(
        [jnp.sum(grad * xhat, axis=0, keepdims=True), jnp.sum(grad, axis=0, keepdims=True)], axis=0
    )

    @pl.when(pl.program_id(0) == 0)
    def _():
        sums_ref[...] = sums

    @pl.when(pl.program_id(0) > 0)
    def _():
        sums_ref[...] = sums_ref[...] + sums

    grad = cot_ref[...].astype(F32) + normalize_back(grad, xhat, scale, gain_ref[...])
    grad_ref[...] = grad
    low = grad.astype(BF16)
    mixed_ref[...] = contract(low, weight_ref[...], 1, 1).astype(BF16)
    product = contract(turned_ref[...], low, 1, 0)

    @pl.when(pl.program_id(0) == 0)
    def _():
        total_ref[...] = product

    @pl.when(pl.program_id(0) > 0)
    def _():
        total_ref[...] += product

    @pl.when(pl.program_id(0) == pl.num_programs(0) - 1)
    def _():
        rows = send_ref.shape[1]
        for index in range(send_ref.shape[0]):
            columns = slice(index * LANES, (index + 1) * LANES)
            for half, out in ((1 - core_ref[0], send_ref), (core_ref[0], keep_ref)):
                at = pl.ds(pl.multiple_of(half * rows, rows), rows)
                out[index] = total_ref[at, columns].astype(BF16)


def second_back(core, wide, back, resid, cotangent, gain, weight, turned, units):
    length, width = resid.shape
    rows = pl.BlockSpec((ROWS, width), lambda i: (i, 0))
    own = const(width // LANES, width // 2, LANES)
    shape = jax.ShapeDtypeStruct((units, width // 2, LANES), BF16)
    return pl.pallas_call(
        second_back_kernel,
        grid=(length // ROWS,),
        in_specs=[
            SCALAR,
            pl.BlockSpec((ROWS, LANES), lambda i: (i, 0)),
            const(*back.shape),
            rows,
            rows,
            const(1, width),
            const(width, width),
            pl.BlockSpec((width, ROWS), lambda i: (0, i)),
        ],
        out_specs=[rows, rows, const(2, width), own, own],
        out_shape=[
            jax.ShapeDtypeStruct((length, width), F32),
            jax.ShapeDtypeStruct((length, width), BF16),
            jax.ShapeDtypeStruct((2, width), F32),
            shape,
            shape,
        ],
        scratch_shapes=[pltpu.VMEM((width, width), F32)],
        cost_estimate=LIGHT,
        name="second_back",
    )(core, wide, back, resid, cotangent, gain, weight, turned)


def first_back_kernel(
    left_ref, right_ref, tokens_ref, resid_ref, gain_ref, wq_ref, wk_ref, wv_ref,
    grad_ref, sums_ref,
):
    side = left_ref.shape[2]
    grad = 0.0
    for index, weight in enumerate((wq_ref, wk_ref, wv_ref)):
        grad = grad + contract(left_ref[index], weight[:, :side], 1, 1)
        grad = grad + contract(right_ref[index], weight[:, side:], 1, 1)
    gain = gain_ref[...]
    _, xhat, scale = normalize(tokens_ref[...].astype(F32), gain, gain)
    sums = jnp.concatenate(
        [jnp.sum(grad * xhat, axis=0, keepdims=True), jnp.sum(grad, axis=0, keepdims=True)], axis=0
    )

    @pl.when(pl.program_id(0) == 0)
    def _():
        sums_ref[...] = sums

    @pl.when(pl.program_id(0) > 0)
    def _():
        sums_ref[...] = sums_ref[...] + sums

    grad_ref[...] = resid_ref[...] + normalize_back(grad, xhat, scale, gain)


def first_back(left, right, tokens, resid, gain, weights):
    length, width = tokens.shape
    rows = pl.BlockSpec((ROWS, width), lambda i: (i, 0))
    return pl.pallas_call(
        first_back_kernel,
        grid=(length // ROWS,),
        in_specs=[
            pl.BlockSpec((3, ROWS, part.shape[2]), lambda i: (0, i, 0)) for part in (left, right)
        ]
        + [rows, rows, const(1, width)]
        + [const(width, width)] * 3,
        out_specs=[rows, const(2, width)],
        out_shape=[
            jax.ShapeDtypeStruct((length, width), F32),
            jax.ShapeDtypeStruct((2, width), F32),
        ],
        cost_estimate=LIGHT,
        name="first_back",
    )(left, right, tokens, resid, gain, *weights)


def layer_out_kernel(wide_ref, rows_ref, resid_ref, gate_ref, out_ref):
    out_ref[...] = (resid_ref[...] + gate_ref[...] * gathered(wide_ref, rows_ref)).astype(BF16)


def layer_output(wide, produced, resid, gate):
    length, width = resid.shape
    rows = pl.BlockSpec((ROWS, width), lambda i: (i, 0))
    return pl.pallas_call(
        layer_out_kernel,
        grid=(length // ROWS,),
        in_specs=[
            pl.BlockSpec((ROWS, LANES), lambda i: (i, 0)),
            const(*produced.shape),
            rows,
            pl.BlockSpec((ROWS, 1), lambda i: (i, 0)),
        ],
        out_specs=rows,
        out_shape=jax.ShapeDtypeStruct((length, width), BF16),
        cost_estimate=LIGHT,
        name="layer_output",
    )(wide, produced, resid, gate)


def assemble_kernel(core_ref, mine_ref, other_ref, *outs, whole):
    outs = outs[-4:] if whole else outs[-3:]

    def write(parts):
        for unit in range(whole):
            outs[0][:, unit * LANES : (unit + 1) * LANES] = parts[unit].astype(F32)
        for unit in range(whole, parts.shape[0]):
            pair, matrix = divmod(unit - whole, 3)
            out = outs[matrix - 3]
            out[:, pair * LANES : (pair + 1) * LANES] = parts[unit].astype(F32)

    mine = pl.program_id(0) == core_ref[0]

    @pl.when(mine)
    def _():
        write(mine_ref)

    @pl.when(jnp.logical_not(mine))
    def _():
        write(other_ref)


def assemble(core, mine, other, width, outs):
    mine, other = (part.reshape(-1, width // 2, LANES) for part in (mine, other))
    whole = 0 if outs else width // LANES
    columns = (mine.shape[0] - whole) // 3 * LANES
    out = jax.ShapeDtypeStruct((width, width), F32)
    specs = [pl.BlockSpec((width // 2, columns), lambda i, core: (i, 1 if outs else 0))] * 3
    if whole:
        specs = [pl.BlockSpec((width // 2, width), lambda i, core: (i, 0))] + specs
    return pl.pallas_call(
        functools.partial(assemble_kernel, whole=whole),
        grid_spec=pltpu.PrefetchScalarGridSpec(
            num_scalar_prefetch=1,
            grid=(2,),
            in_specs=[const(*mine.shape)] * 2
            + [pl.BlockSpec(memory_space=pl.ANY)] * len(outs),
            out_specs=specs,
        ),
        out_shape=[out] * len(specs),
        input_output_aliases={3 + index: index for index in range(len(outs))},
        cost_estimate=LIGHT,
        name="assemble",
    )(core, mine, other, *outs)


def swap(value, axis, bit):
    size = lax.axis_size(axis)
    return lax.ppermute(value, axis, [(i, i ^ bit) for i in range(size)])


def stages(axis, low, high):
    found = []
    bit = low
    while bit < min(high, lax.axis_size(axis)):
        found.append((axis, bit))
        bit *= 2
    return found


def bit_of(axis, bit):
    return (lax.axis_index(axis) // bit) % 2


def add_low(left, right):
    return (left.astype(F32) + right.astype(F32)).astype(BF16)


def add(left, right):
    return left + right


def halves(rows, stage):
    axis, bit = stage
    half = rows.shape[0] // 2
    mine = bit_of(axis, bit)
    return (
        lax.dynamic_slice_in_dim(rows, (1 - mine) * half, half, 0),
        lax.dynamic_slice_in_dim(rows, mine * half, half, 0),
    )


def joined(rows, other, stage):
    first = bit_of(*stage) == 0
    return jnp.concatenate([jnp.where(first, rows, other), jnp.where(first, other, rows)], axis=0)


def add_split_kernel(mine_ref, left_ref, right_ref, send_ref, keep_ref):
    value = add_low(left_ref[...], right_ref[...])

    @pl.when(pl.program_id(0) == 0)
    def _():
        send_ref[...] = value

    @pl.when(pl.program_id(0) == 1)
    def _():
        keep_ref[...] = value


def add_split(left, right, stage):
    half, width = left.shape[0] // 2, left.shape[1]
    if half % 8:
        return halves(add_low(left, right), stage)
    mine = bit_of(*stage).astype(jnp.int32)[None]
    block = pl.BlockSpec((half, width), lambda i, mine: (jnp.where(i == 0, 1 - mine[0], mine[0]), 0))
    out = pl.BlockSpec((half, width), lambda i, mine: (0, 0))
    shape = jax.ShapeDtypeStruct((half, width), BF16)
    return pl.pallas_call(
        add_split_kernel,
        grid_spec=pltpu.PrefetchScalarGridSpec(
            num_scalar_prefetch=1,
            grid=(2,),
            in_specs=[block, block],
            out_specs=[out, out],
        ),
        out_shape=[shape, shape],
        cost_estimate=LIGHT,
        name="add_split",
    )(mine, left, right)


def halves_sum(left, right, stage):
    width = left.shape[2]
    parts = add_split(left.reshape(-1, width), right.reshape(-1, width), stage)
    return [part.reshape(-1, *left.shape[1:]) for part in parts]


class Sum:
    def __init__(self, keep, send, stages, plus=add_low, split=True):
        self.keep, self.send, self.plus = keep, send, plus
        if split:
            self.steps = [("whole", stages[0])]
            self.steps += [("halve", stage) for stage in stages[1:-1]]
            self.steps += [("whole", stages[-1])]
            self.steps += [("join", stage) for stage in stages[-2:0:-1]]
        else:
            self.steps = [("whole", stage) for stage in stages]

    def start(self):
        return swap(self.send, *self.steps[0][1])

    def finish(self, got):
        kind, stage = self.steps.pop(0)
        if self.steps and self.steps[0][0] == "halve":
            self.send, self.keep = add_split(self.keep, got, self.steps[0][1])
        else:
            join = functools.partial(joined, stage=stage)
            self.keep = self.send = (join if kind == "join" else self.plus)(self.keep, got)


def advance(sums, *others):
    sums = [each for each in sums if each.steps]
    tied = tie((*(each.start() for each in sums), *others))
    for each, got in zip(sums, tied):
        each.finish(got)
    rest = tied[len(sums) :]
    return rest[0] if len(rest) == 1 else rest


def chip_stages(total):
    return [("dp", 2 << index) for index in range((total.shape[0]).bit_length() - 1)][::-1]


tie = lax.optimization_barrier


def exchange(rows):
    return lax.all_to_all(rows, "expert", split_axis=0, concat_axis=0, tiled=True)


def local(
    tokens,
    routing,
    query_weight,
    key_weight,
    value_weight,
    output_weight,
    first_gain,
    first_bias,
    second_gain,
    second_bias,
    centroids,
    expert_up,
    expert_down,
    cotangent,
):
    length, width = tokens.shape
    experts = centroids.shape[0]
    capacity = length // experts
    peers = lax.axis_size("expert")
    parts = lax.axis_size("dp")
    slots = experts * capacity
    core = (lax.axis_index("dp") % 2).astype(jnp.int32)[None]
    vectors = tie(jnp.stack([first_gain, first_bias, second_gain, second_bias]))
    first_gain, first_bias, second_gain, second_bias = (vectors[i : i + 1] for i in range(4))
    weights = (query_weight, key_weight, value_weight)

    cots, slot, wide = route(routing.reshape(1, length), cotangent, experts, capacity)
    cots, tokens = tie((cots, tokens))
    cots = exchange(cots.reshape(peers, -1, width)).reshape(slots, width)

    normed_turned, queries, keys, values = project(tokens, first_gain, first_bias, weights)
    mixed, probs = attention(queries, keys, values)
    mixed, cots = tie((mixed, cots))
    resid, gate, mixed_turned, rows = branch(
        mixed, tokens, output_weight, second_gain, second_bias, centroids, routing, slot, slots
    )

    rows = exchange(rows.reshape(peers, -1, width))
    rows, cots_down = tie((rows, expert_cots(cots, expert_down)))
    rows = rows.reshape(slots, width)
    own = centroids[lax.axis_index("expert")][None, :]
    produced, returned, grad_rows, hidden, grad_pre = expert(
        rows, cots, cots_down, own, expert_up, expert_down
    )
    returned = exchange(returned.reshape(peers, -1, width))
    up_send, down_send, up_keep, down_keep = expert_weights(
        rows, grad_rows, hidden, grad_pre, parts, core
    )
    chips = chip_stages(up_send)
    up_send, up_keep = halves_sum(up_keep, swap(up_send, "dp", 1), chips[0])
    down_send, down_keep = halves_sum(down_keep, swap(down_send, "dp", 1), chips[0])
    returned, produced, up_send, up_keep, down_send, down_keep = tie(
        (returned, produced, up_send, up_keep, down_send, down_keep)
    )
    returned = returned.reshape(slots, width)
    up_got = swap(up_send, *chips[0])
    down_got = swap(down_send, *chips[0])
    produced = exchange(produced.reshape(peers, -1, width))

    pairs = width // LANES
    split = pairs // 2
    grad_resid, grad_mixed, second_sums, *units = second_back(
        core, wide, returned, resid, cotangent, second_gain, output_weight, mixed_turned,
        pairs + 3 * split,
    )

    cross = stages("expert", 1, 1 << 20)
    apart = stages("dp", 2, 1 << 20)
    back = functools.partial(
        attention_back, core, queries, keys, values, grad_mixed, mixed, normed_turned
    )
    left, send, keep = back(probs, 0, split, units)
    left, send, keep, up_got = tie((left, send, keep, up_got))
    early = Sum(keep.reshape(-1, LANES), send.reshape(-1, LANES), [("dp", 1)] + cross + apart)
    advance([early])
    early.send, *probs = tie((early.send, *probs))
    right, send, keep = back(probs, split, pairs - split, None)
    right, send, keep, produced = advance([early], right, send, keep, produced)
    produced = produced.reshape(slots, width)
    order = [("dp", 1)] + apart + cross[1:2] + cross[:1] + cross[2:]
    late = Sum(keep.reshape(-1, LANES), send.reshape(-1, LANES), order)
    layer_out = layer_output(wide, produced, resid, gate)
    layer_out, down_got = advance([early, late], layer_out, down_got)
    grad_tokens, first_sums = first_back(left, right, tokens, grad_resid, first_gain, weights)
    grad_tokens, first_sums = advance([early, late], grad_tokens, first_sums)
    grad_up = up_keep.astype(F32) + up_got.astype(F32)
    grad_down = down_keep.astype(F32) + down_got.astype(F32)
    for stage in chips[1:]:
        grad_up, grad_down = (
            keep.astype(F32) + swap(send, *stage).astype(F32)
            for send, keep in (halves(value.astype(BF16), stage) for value in (grad_up, grad_down))
        )
    grad_up, grad_down = (value.reshape(value.shape[1:])[None] for value in (grad_up, grad_down))
    small = jnp.concatenate([first_sums, second_sums], axis=0)
    small = Sum(small, small, stages("dp", 1, 1 << 20) + cross, plus=add, split=False)
    while len(early.steps) > 1:
        advance([early, late, small])
    got = early.start()
    grad_up, grad_down = advance([late, small], grad_up, grad_down)
    while len(late.steps) > 2:
        advance([late, small])
    early.finish(advance([late, small], got))
    outs = assemble(core, early.keep, swap(early.keep, "dp", 1), width, [])
    grad_output, *outs = advance([late, small], *outs)
    while small.steps:
        advance([small])
    grad_query, grad_key, grad_value = assemble(
        core, late.keep, swap(late.keep, "dp", 1), width, outs
    )
    small = small.keep
    return (
        layer_out,
        grad_tokens,
        grad_query,
        grad_key,
        grad_value,
        grad_output,
        small[0],
        small[1],
        small[2],
        small[3],
        grad_up,
        grad_down,
    )


def solution(mesh):
    rows = P(("dp", "expert"), None)
    return jax.shard_map(
        local,
        mesh=mesh,
        in_specs=(rows, rows)
        + (P(),) * 9
        + (P("expert", None, None), P("expert", None, None), rows),
        out_specs=(rows, rows) + (P(),) * 8 + (P("expert", None, "dp"), P("expert", "dp", None)),
        check_vma=False,
    )
```

```python
import functools
import math

import jax
import jax.numpy as jnp
from jax import lax
from jax.experimental import pallas as pl
from jax.experimental.pallas import tpu as pltpu
from jax.sharding import PartitionSpec as P

HEADS = 12
HEAD = 64
LANES = 128
EPS = 1e-05
F32 = jnp.float32
BF16 = jnp.bfloat16
ROWS = 256

LIGHT = pl.CostEstimate(flops=1000000, bytes_accessed=100000, transcendentals=0)


def contract(left, right, left_dim, right_dim):
    return lax.dot_general(
        left, right, (((left_dim,), (right_dim,)), ((), ())), preferred_element_type=F32
    )


def normalize(values, gain, bias):
    centered = values - jnp.mean(values, axis=-1, keepdims=True)
    variance = jnp.mean(centered * centered, axis=-1, keepdims=True)
    scale = lax.rsqrt(variance + EPS)
    xhat = centered * scale
    return xhat * gain + bias, xhat, scale


def normalize_back(grad, xhat, scale, gain):
    scaled = grad * gain
    first = jnp.mean(scaled, axis=-1, keepdims=True)
    cross = jnp.mean(scaled * xhat, axis=-1, keepdims=True)
    return scale * (scaled - first - xhat * cross)


def head_mask(parity, value):
    lane = lax.broadcasted_iota(jnp.int32, (1, LANES), 1)
    return jnp.where(lane // HEAD == parity, value, 0.0).astype(BF16)


def causal_bias(bias_ref, keys_dim):
    @pl.when((pl.program_id(0) == 0) & (pl.program_id(1) == 0))
    def _():
        key = lax.broadcasted_iota(jnp.int32, bias_ref.shape, keys_dim)
        query = lax.broadcasted_iota(jnp.int32, bias_ref.shape, 1 - keys_dim)
        bias_ref[...] = jnp.where(key <= query, 0.0, -1e30)


def attention_kernel(
    tokens_ref, gain_ref, shift_ref, wq_ref, wk_ref, wv_ref, q_ref, k_ref, v_ref, o_ref, *refs, block
):
    *probs_refs, normed_ref, bias_ref = refs
    causal_bias(bias_ref, 0)
    parity = pl.program_id(1)

    @pl.when((pl.program_id(0) == 0) & (parity == 0))
    def _():
        for index in range(len(probs_refs)):
            rows = slice(index * block, (index + 1) * block)
            normed, _, _ = normalize(tokens_ref[rows, :].astype(F32), gain_ref[...], shift_ref[...])
            normed_ref[rows, :] = normed.astype(BF16)

    @pl.when(parity == 0)
    def _():
        weights = jnp.concatenate([wq_ref[...], wk_ref[...], wv_ref[...]], axis=1)
        made = contract(normed_ref[...], weights, 1, 0).astype(BF16)
        for index, out in enumerate((q_ref, k_ref, v_ref)):
            out[...] = made[:, index * LANES : (index + 1) * LANES]

    queries = q_ref[...] * head_mask(parity, HEAD**-0.5)
    values = v_ref[...] * head_mask(parity, 1.0)
    outs = []
    for index, probs_ref in enumerate(probs_refs):
        first, finish = index * block, (index + 1) * block
        scores = contract(k_ref[:finish, :], queries[first:finish], 1, 1)
        diagonal = scores[first:] + bias_ref[...]
        if index:
            scores = jnp.concatenate([scores[:first], diagonal], axis=0)
        else:
            scores = diagonal
        shifted = jnp.exp(scores - jnp.max(scores, axis=0, keepdims=True))
        total = jnp.sum(shifted, axis=0, keepdims=True)
        probs = (shifted * (1.0 / total)).astype(BF16)
        probs_ref[0] = probs
        outs.append(contract(probs, values[:finish], 0, 0).astype(BF16))
    mixed = jnp.concatenate(outs, axis=0)

    @pl.when(parity == 0)
    def _():
        o_ref[...] = mixed

    @pl.when(parity == 1)
    def _():
        o_ref[...] = o_ref[...] + mixed


def attention(tokens, gain, shift, weights):
    length, width = tokens.shape
    pairs = width // LANES
    block = min(256, length)
    finishes = range(block, length + 1, block)
    spec = pl.BlockSpec((length, LANES), lambda pair, parity: (0, pair))
    weight = pl.BlockSpec((width, LANES), lambda pair, parity: (0, pair))
    wide = jax.ShapeDtypeStruct((length, width), BF16)
    queries, keys, values, mixed, *probs = pl.pallas_call(
        functools.partial(attention_kernel, block=block),
        grid=(pairs, 2),
        in_specs=[const(length, width), const(1, width), const(1, width)] + [weight] * 3,
        out_specs=[spec] * 4
        + [
            pl.BlockSpec((1, finish, block), lambda pair, parity: (pair * 2 + parity, 0, 0))
            for finish in finishes
        ],
        out_shape=[wide] * 4
        + [jax.ShapeDtypeStruct((2 * pairs, finish, block), BF16) for finish in finishes],
        scratch_shapes=[pltpu.VMEM((length, width), BF16), pltpu.VMEM((block, block), F32)],
        cost_estimate=LIGHT,
        name="attention",
    )(tokens, gain, shift, *weights)
    return queries, keys, values, mixed, probs


def attention_back_kernel(
    core_ref, q_ref, k_ref, v_ref, g_ref, o_ref, turned_ref, *refs, block, blocks
):
    probs_refs = refs[:blocks]
    grads_ref, send_ref, keep_ref, dk_sum, dv_sum = refs[-5:]
    parity = pl.program_id(1)
    scale_mask = head_mask(parity, HEAD**-0.5)
    queries = q_ref[...] * scale_mask
    grads = g_ref[...] * head_mask(parity, 1.0)
    keys_scaled = k_ref[...] * scale_mask
    dk_sum[...] = jnp.zeros_like(dk_sum)
    dv_sum[...] = jnp.zeros_like(dv_sum)
    dq_parts = []
    for index, probs_ref in enumerate(probs_refs):
        first, finish = index * block, (index + 1) * block
        probs = probs_ref[0]
        some = grads[first:finish]
        dv_sum[:finish, :] += contract(probs, some, 1, 0)
        grad_probs = contract(v_ref[:finish, :], some, 1, 1)
        shares = some.astype(F32) * o_ref[first:finish, :].astype(F32)
        delta = jnp.sum(jnp.transpose(shares), axis=0, keepdims=True)
        grad_scores = (probs.astype(F32) * (grad_probs - delta)).astype(BF16)
        dk_sum[:finish, :] += contract(grad_scores, queries[first:finish], 1, 0)
        dq_parts.append(contract(grad_scores, keys_scaled[:finish], 0, 0).astype(BF16))
    parts = (
        jnp.concatenate(dq_parts, axis=0),
        dk_sum[...].astype(BF16),
        dv_sum[...].astype(BF16),
    )

    @pl.when(parity == 0)
    def _():
        for index, part in enumerate(parts):
            grads_ref[index] = part

    @pl.when(parity == 1)
    def _():
        whole = [grads_ref[index] + part for index, part in enumerate(parts)]
        for index, part in enumerate(whole):
            grads_ref[index] = part
        weight_parts(core_ref, turned_ref[...], jnp.concatenate(whole, axis=1), send_ref, keep_ref)


def weight_parts(core_ref, turned, grads, send_ref, keep_ref):
    product = contract(turned, grads, 1, 0).astype(BF16)
    rows = send_ref.shape[1]

    def write(upper, lower):
        for index in range(grads.shape[1] // LANES):
            columns = slice(index * LANES, (index + 1) * LANES)
            upper[index] = product[:rows, columns]
            lower[index] = product[rows:, columns]

    @pl.when(core_ref[0] == 0)
    def _():
        write(keep_ref, send_ref)

    @pl.when(core_ref[0] != 0)
    def _():
        write(send_ref, keep_ref)


SCALAR = pl.BlockSpec(memory_space=pltpu.SMEM)


def attention_back(core, queries, keys, values, grads, mixed, turned, probs, start, pairs, units):
    length, width = queries.shape
    block = probs[0].shape[2]
    spec = pl.BlockSpec((length, LANES), lambda pair, parity: (0, start + pair))
    whole = pl.BlockSpec((width, length), lambda pair, parity: (0, 0))
    ahead = 0 if units is None else units[0].shape[0] // 3 - pairs
    shape = jax.ShapeDtypeStruct((3 * (ahead + pairs), width // 2, LANES), BF16)
    unit = pl.BlockSpec((3, width // 2, LANES), lambda pair, parity: (ahead + pair, 0, 0))
    args = [core, queries, keys, values, grads, mixed, turned, *probs]
    alias = {}
    if units is not None:
        alias = {len(args): 1, len(args) + 1: 2}
        args += units
    return pl.pallas_call(
        functools.partial(attention_back_kernel, block=block, blocks=len(probs)),
        grid=(pairs, 2),
        in_specs=[SCALAR, spec, spec, spec, spec, spec, whole]
        + [
            pl.BlockSpec(
                (1, *part.shape[1:]), lambda pair, parity: ((start + pair) * 2 + parity, 0, 0)
            )
            for part in probs
        ]
        + [pl.BlockSpec(memory_space=pl.ANY)] * len(alias),
        out_specs=[pl.BlockSpec((3, length, LANES), lambda pair, parity: (0, 0, pair)), unit, unit],
        out_shape=[jax.ShapeDtypeStruct((3, length, pairs * LANES), BF16), shape, shape],
        input_output_aliases=alias,
        scratch_shapes=[pltpu.VMEM((length, LANES), F32)] * 2,
        cost_estimate=LIGHT,
        name="attention_back",
    )(*args)


def gelu_parts(value):
    cdf = 0.5 + 0.5 * lax.erf(value * 0.5**0.5)
    density = jnp.exp2(value * value * (-0.5 / math.log(2.0)))
    return cdf, value * (density * (1.0 / math.sqrt(2.0 * math.pi)))


def expert_cots_kernel(c_ref, down_ref, out_ref):
    out_ref[...] = contract(c_ref[...], down_ref[0], 1, 1).astype(BF16)


def expert_cots(cots, down):
    count, width = cots.shape
    hidden = down.shape[1]
    tile = min(512, hidden)
    return pl.pallas_call(
        expert_cots_kernel,
        grid=(hidden // tile,),
        in_specs=[
            pl.BlockSpec((count, width), lambda f: (0, 0)),
            pl.BlockSpec((1, tile, width), lambda f: (0, f, 0)),
        ],
        out_specs=pl.BlockSpec((count, tile), lambda f: (0, f)),
        out_shape=jax.ShapeDtypeStruct((count, hidden), BF16),
        cost_estimate=LIGHT,
        name="expert_cots",
    )(cots, down)


def expert_kernel(
    x_ref, c_ref, cd_ref, cen_ref, up_ref, down_ref,
    y_ref, gs_ref, dy_ref, h_ref, dp_ref,
    y_sum, dx_sum, gate_ref,
):
    step = pl.program_id(0)

    @pl.when(step == 0)
    def _():
        logit = jnp.sum(x_ref[...].astype(F32) * cen_ref[...], axis=1, keepdims=True)
        gate = jax.nn.sigmoid(logit)
        gate_ref[...] = jnp.broadcast_to(gate, gate_ref.shape)
        dy_ref[...] = (c_ref[...].astype(F32) * gate).astype(BF16)
        y_sum[...] = jnp.zeros_like(y_sum)
        dx_sum[...] = jnp.zeros_like(dx_sum)

    pre = contract(x_ref[...], up_ref[0], 1, 0)
    cdf, weighted = gelu_parts(pre)
    hidden = (pre * cdf).astype(BF16)
    slope = cdf + weighted
    h_ref[...] = hidden
    y_sum[...] += contract(hidden, down_ref[0], 1, 0)
    grad_hidden = cd_ref[...].astype(F32) * gate_ref[:, 0:1]
    grad_pre = (grad_hidden * slope).astype(BF16)
    dp_ref[...] = grad_pre
    dx_sum[...] += contract(grad_pre, up_ref[0], 1, 1)

    @pl.when(step == pl.num_programs(0) - 1)
    def _():
        produced = y_sum[...].astype(BF16)
        y_ref[...] = produced
        gate = gate_ref[:, 0:1]
        dot = jnp.sum(c_ref[...].astype(F32) * produced.astype(F32), axis=1, keepdims=True)
        grad_logit = dot * gate * (1.0 - gate)
        back = dx_sum[...].astype(BF16).astype(F32) + grad_logit * cen_ref[...]
        gs_ref[...] = back.astype(BF16)


def expert(rows, cots, cots_down, centroid, up, down):
    count, width = rows.shape
    hidden = up.shape[2]
    tile = min(512, hidden)
    whole = pl.BlockSpec((count, width), lambda f: (0, 0))
    wide = jax.ShapeDtypeStruct((count, width), BF16)
    deep = jax.ShapeDtypeStruct((count, hidden), BF16)
    return pl.pallas_call(
        expert_kernel,
        grid=(hidden // tile,),
        in_specs=[
            whole,
            whole,
            pl.BlockSpec((count, tile), lambda f: (0, f)),
            pl.BlockSpec((1, width), lambda f: (0, 0)),
            pl.BlockSpec((1, width, tile), lambda f: (0, 0, f)),
            pl.BlockSpec((1, tile, width), lambda f: (0, f, 0)),
        ],
        out_specs=[whole, whole, whole]
        + [pl.BlockSpec((count, tile), lambda f: (0, f))] * 2,
        out_shape=[wide, wide, wide, deep, deep],
        scratch_shapes=[
            pltpu.VMEM((count, width), F32),
            pltpu.VMEM((count, width), F32),
            pltpu.VMEM((count, LANES), F32),
        ],
        cost_estimate=LIGHT,
        name="expert",
    )(rows, cots, cots_down, centroid, up, down)


def expert_weights_kernel(
    core_ref, x_ref, dy_ref, h_ref, dp_ref,
    up_send_ref, down_send_ref, up_keep_ref, down_keep_ref, xt_ref,
):
    @pl.when(pl.program_id(0) == 0)
    def _():
        xt_ref[...] = jnp.transpose(x_ref[...])

    up = contract(xt_ref[...], dp_ref[...], 1, 0).astype(BF16)
    down = contract(h_ref[...], dy_ref[...], 0, 0).astype(BF16)
    sending = pl.program_id(0) < pl.num_programs(0) // 2

    @pl.when(sending)
    def _():
        up_send_ref[0] = up
        down_send_ref[0] = down

    @pl.when(jnp.logical_not(sending))
    def _():
        up_keep_ref[0] = up
        down_keep_ref[0] = down


def expert_weights(rows, grads, hidden_rows, grad_pre, parts, core):
    count, width = rows.shape
    hidden = hidden_rows.shape[1]
    share = hidden // parts
    tile = min(384, share)
    each = share // tile
    half = hidden // tile // 2

    def column(f, core):
        step = f % half
        other = jnp.where(f < half, 1 - core[0], core[0])
        return ((step // each) * 2 + other) * each + step % each

    def send(f):
        return jnp.minimum(f, half - 1)

    def keep(f):
        return jnp.maximum(f - half, 0)

    whole = pl.BlockSpec((count, width), lambda f, core: (0, 0))
    deep = pl.BlockSpec((count, tile), lambda f, core: (0, column(f, core)))
    up = [
        pl.BlockSpec((1, width, tile), lambda f, core, at=at: (at(f) // each, 0, at(f) % each))
        for at in (send, keep)
    ]
    down = [
        pl.BlockSpec((1, tile, width), lambda f, core, at=at: (at(f) // each, at(f) % each, 0))
        for at in (send, keep)
    ]
    up_shape = jax.ShapeDtypeStruct((parts // 2, width, share), BF16)
    down_shape = jax.ShapeDtypeStruct((parts // 2, share, width), BF16)
    return pl.pallas_call(
        expert_weights_kernel,
        grid_spec=pltpu.PrefetchScalarGridSpec(
            num_scalar_prefetch=1,
            grid=(2 * half,),
            in_specs=[whole, whole, deep, deep],
            out_specs=[up[0], down[0], up[1], down[1]],
            scratch_shapes=[pltpu.VMEM((width, count), BF16)],
        ),
        out_shape=[up_shape, down_shape, up_shape, down_shape],
        cost_estimate=LIGHT,
        name="expert_weights",
    )(core, rows, grads, hidden_rows, grad_pre)


def one_hot(condition):
    return jnp.where(condition, 1.0, 0.0).astype(BF16)


def block_rows(step, count, length, dim):
    return step * count + lax.broadcasted_iota(jnp.int32, (count, length), dim)


def const(*shape):
    return pl.BlockSpec(shape, lambda *step: (0,) * len(shape))


def route_kernel(routing_ref, cot_ref, send_ref, slot_ref, wide_ref, *, experts, capacity):
    length = routing_ref.shape[1]
    step = pl.program_id(0)

    @pl.when(step == 0)
    def _():
        chosen = routing_ref[...]
        named = lax.broadcasted_iota(jnp.int32, (experts, length), 0) == chosen
        named = jnp.where(named, 1.0, 0.0)
        lane = lax.broadcasted_iota(jnp.int32, (experts, length), 1)
        count = named
        shift = 1
        while shift < length:
            count = count + jnp.where(lane >= shift, pltpu.roll(count, shift, 1), 0.0)
            shift *= 2
        position = jnp.sum(named * (count - named), axis=0, keepdims=True)
        slot = chosen.astype(F32) * capacity + position
        slot = jnp.where(position < capacity, slot, -1.0)
        slot_ref[...] = slot.astype(jnp.int32)
        wide_ref[...] = jnp.transpose(jnp.broadcast_to(slot, (LANES, length))).astype(jnp.int32)

    place = one_hot(block_rows(step, send_ref.shape[0], length, 0) == slot_ref[...])
    send_ref[...] = contract(place, cot_ref[...], 1, 0).astype(BF16)


def route(routing, cotangent, experts, capacity):
    length, width = cotangent.shape
    slots = experts * capacity
    return pl.pallas_call(
        functools.partial(route_kernel, experts=experts, capacity=capacity),
        grid=(slots // ROWS,),
        in_specs=[const(1, length), const(length, width)],
        out_specs=[
            pl.BlockSpec((ROWS, width), lambda i: (i, 0)),
            const(1, length),
            const(length, LANES),
        ],
        out_shape=[
            jax.ShapeDtypeStruct((slots, width), BF16),
            jax.ShapeDtypeStruct((1, length), jnp.int32),
            jax.ShapeDtypeStruct((length, LANES), jnp.int32),
        ],
        cost_estimate=LIGHT,
        name="route",
    )(routing, cotangent)


def settle_kernel(
    tokens_ref, first_gain_ref, first_bias_ref, mixed_ref, resid_ref, gain_ref, bias_ref,
    cen_ref, chosen_ref,
    normed_ref, turned_ref, xhat_ref, scale_ref, gate_ref,
):
    normed, _, _ = normalize(tokens_ref[...].astype(F32), first_gain_ref[...], first_bias_ref[...])
    normed_ref[...] = jnp.transpose(normed.astype(BF16))
    turned_ref[...] = jnp.transpose(mixed_ref[...])
    second, xhat, scale = normalize(resid_ref[...], gain_ref[...], bias_ref[...])
    xhat_ref[...] = xhat.astype(BF16)
    scale_ref[...] = scale
    centroid = jnp.zeros_like(second)
    for index in range(cen_ref.shape[0]):
        centroid = jnp.where(chosen_ref[...] == index, cen_ref[index : index + 1, :], centroid)
    gate_ref[...] = jax.nn.sigmoid(jnp.sum(second * centroid, axis=1, keepdims=True))


def settle(tokens, first_gain, first_bias, mixed, resid, gain, bias, centroids, routing):
    length, width = tokens.shape
    rows = pl.BlockSpec((ROWS, width), lambda i: (i, 0))
    thin = pl.BlockSpec((ROWS, 1), lambda i: (i, 0))
    turned = pl.BlockSpec((width, ROWS), lambda i: (0, i))
    vector = const(1, width)
    column = jax.ShapeDtypeStruct((length, 1), F32)
    return pl.pallas_call(
        settle_kernel,
        grid=(length // ROWS,),
        in_specs=[rows, vector, vector, rows, rows, vector, vector, const(*centroids.shape), thin],
        out_specs=[turned, turned, rows, thin, thin],
        out_shape=[jax.ShapeDtypeStruct((width, length), BF16)] * 2
        + [jax.ShapeDtypeStruct((length, width), BF16), column, column],
        cost_estimate=LIGHT,
        name="settle",
    )(tokens, first_gain, first_bias, mixed, resid, gain, bias, centroids, routing)


def branch_kernel(
    mixed_ref, tokens_ref, weight_ref, gain_ref, bias_ref, slot_ref,
    resid_ref, send_ref, low_ref, *, blocks,
):
    step = pl.program_id(0)

    @pl.when(step < blocks)
    def _():
        resid = tokens_ref[...].astype(F32) + contract(mixed_ref[...], weight_ref[...], 1, 0)
        second, _, _ = normalize(resid, gain_ref[...], bias_ref[...])
        resid_ref[...] = resid
        low_ref[pl.ds(pl.multiple_of(step * ROWS, ROWS), ROWS), :] = second.astype(BF16)

    @pl.when(step >= blocks)
    def _():
        place = one_hot(block_rows(step - blocks, ROWS, slot_ref.shape[1], 0) == slot_ref[...])
        send_ref[...] = contract(place, low_ref[...], 1, 0).astype(BF16)


def branch(mixed, tokens, weight, gain, bias, slot, slots):
    length, width = mixed.shape
    blocks = length // ROWS

    def at(i):
        return jnp.minimum(i, blocks - 1)

    rows = pl.BlockSpec((ROWS, width), lambda i: (at(i), 0))
    return pl.pallas_call(
        functools.partial(branch_kernel, blocks=blocks),
        grid=(blocks + slots // ROWS,),
        in_specs=[
            rows,
            rows,
            const(width, width),
            const(1, width),
            const(1, width),
            const(1, length),
        ],
        out_specs=[
            rows,
            pl.BlockSpec((ROWS, width), lambda i: (jnp.maximum(i - blocks, 0), 0)),
        ],
        out_shape=[
            jax.ShapeDtypeStruct((length, width), F32),
            jax.ShapeDtypeStruct((slots, width), BF16),
        ],
        scratch_shapes=[pltpu.VMEM((length, width), BF16)],
        cost_estimate=LIGHT,
        name="branch",
    )(mixed, tokens, weight, gain, bias, slot)


def gathered(wide_ref, rows_ref):
    slots = rows_ref.shape[0]
    count = wide_ref.shape[0]
    wide = jnp.concatenate([wide_ref[...]] * (slots // LANES), axis=1)
    place = one_hot(lax.broadcasted_iota(jnp.int32, (count, slots), 1) == wide)
    return contract(place, rows_ref[...], 1, 0)


def second_back_kernel(
    core_ref, wide_ref, back_ref, xhat_ref, scale_ref, cot_ref, gain_ref, weight_ref, turned_ref,
    grad_ref, mixed_ref, sums_ref, send_ref, keep_ref, total_ref,
):
    grad = gathered(wide_ref, back_ref)
    xhat, scale = xhat_ref[...].astype(F32), scale_ref[...]
    sums = jnp.concatenate(
        [jnp.sum(grad * xhat, axis=0, keepdims=True), jnp.sum(grad, axis=0, keepdims=True)], axis=0
    )

    @pl.when(pl.program_id(0) == 0)
    def _():
        sums_ref[...] = sums

    @pl.when(pl.program_id(0) > 0)
    def _():
        sums_ref[...] = sums_ref[...] + sums

    grad = cot_ref[...].astype(F32) + normalize_back(grad, xhat, scale, gain_ref[...])
    low = grad.astype(BF16)
    grad_ref[...] = low
    mixed_ref[...] = contract(low, weight_ref[...], 1, 1).astype(BF16)
    product = contract(turned_ref[...], low, 1, 0)

    @pl.when(pl.program_id(0) == 0)
    def _():
        total_ref[...] = product

    @pl.when(pl.program_id(0) > 0)
    def _():
        total_ref[...] += product

    @pl.when(pl.program_id(0) == pl.num_programs(0) - 1)
    def _():
        rows = send_ref.shape[1]
        for index in range(send_ref.shape[0]):
            columns = slice(index * LANES, (index + 1) * LANES)
            for half, out in ((1 - core_ref[0], send_ref), (core_ref[0], keep_ref)):
                at = pl.ds(pl.multiple_of(half * rows, rows), rows)
                out[index] = total_ref[at, columns].astype(BF16)


def second_back(core, wide, back, xhat, scale, cotangent, gain, weight, turned, units):
    length, width = xhat.shape
    rows = pl.BlockSpec((ROWS, width), lambda i: (i, 0))
    own = const(width // LANES, width // 2, LANES)
    shape = jax.ShapeDtypeStruct((units, width // 2, LANES), BF16)
    return pl.pallas_call(
        second_back_kernel,
        grid=(length // ROWS,),
        in_specs=[
            SCALAR,
            pl.BlockSpec((ROWS, LANES), lambda i: (i, 0)),
            const(*back.shape),
            rows,
            pl.BlockSpec((ROWS, 1), lambda i: (i, 0)),
            rows,
            const(1, width),
            const(width, width),
            pl.BlockSpec((width, ROWS), lambda i: (0, i)),
        ],
        out_specs=[rows, rows, const(2, width), own, own],
        out_shape=[
            jax.ShapeDtypeStruct((length, width), BF16),
            jax.ShapeDtypeStruct((length, width), BF16),
            jax.ShapeDtypeStruct((2, width), F32),
            shape,
            shape,
        ],
        scratch_shapes=[pltpu.VMEM((width, width), F32)],
        cost_estimate=LIGHT,
        name="second_back",
    )(core, wide, back, xhat, scale, cotangent, gain, weight, turned)


def first_back_kernel(
    left_ref, right_ref, tokens_ref, resid_ref, gain_ref, wq_ref, wk_ref, wv_ref,
    grad_ref, sums_ref,
):
    side = left_ref.shape[2]
    grad = 0.0
    for index, weight in enumerate((wq_ref, wk_ref, wv_ref)):
        grad = grad + contract(left_ref[index], weight[:, :side], 1, 1)
        grad = grad + contract(right_ref[index], weight[:, side:], 1, 1)
    gain = gain_ref[...]
    _, xhat, scale = normalize(tokens_ref[...].astype(F32), gain, gain)
    sums = jnp.concatenate(
        [jnp.sum(grad * xhat, axis=0, keepdims=True), jnp.sum(grad, axis=0, keepdims=True)], axis=0
    )

    @pl.when(pl.program_id(0) == 0)
    def _():
        sums_ref[...] = sums

    @pl.when(pl.program_id(0) > 0)
    def _():
        sums_ref[...] = sums_ref[...] + sums

    grad_ref[...] = resid_ref[...].astype(F32) + normalize_back(grad, xhat, scale, gain)


def first_back(left, right, tokens, resid, gain, weights):
    length, width = tokens.shape
    rows = pl.BlockSpec((ROWS, width), lambda i: (i, 0))
    return pl.pallas_call(
        first_back_kernel,
        grid=(length // ROWS,),
        in_specs=[
            pl.BlockSpec((3, ROWS, part.shape[2]), lambda i: (0, i, 0)) for part in (left, right)
        ]
        + [rows, rows, const(1, width)]
        + [const(width, width)] * 3,
        out_specs=[rows, const(2, width)],
        out_shape=[
            jax.ShapeDtypeStruct((length, width), F32),
            jax.ShapeDtypeStruct((2, width), F32),
        ],
        cost_estimate=LIGHT,
        name="first_back",
    )(left, right, tokens, resid, gain, *weights)


def layer_out_kernel(wide_ref, rows_ref, resid_ref, gate_ref, out_ref):
    out_ref[...] = (resid_ref[...] + gate_ref[...] * gathered(wide_ref, rows_ref)).astype(BF16)


def layer_output(wide, produced, resid, gate):
    length, width = resid.shape
    rows = pl.BlockSpec((ROWS, width), lambda i: (i, 0))
    return pl.pallas_call(
        layer_out_kernel,
        grid=(length // ROWS,),
        in_specs=[
            pl.BlockSpec((ROWS, LANES), lambda i: (i, 0)),
            const(*produced.shape),
            rows,
            pl.BlockSpec((ROWS, 1), lambda i: (i, 0)),
        ],
        out_specs=rows,
        out_shape=jax.ShapeDtypeStruct((length, width), BF16),
        cost_estimate=LIGHT,
        name="layer_output",
    )(wide, produced, resid, gate)


def assemble_kernel(core_ref, mine_ref, other_ref, *outs, whole):
    outs = outs[-4:] if whole else outs[-3:]

    def write(parts):
        for unit in range(whole):
            outs[0][:, unit * LANES : (unit + 1) * LANES] = parts[unit].astype(F32)
        for unit in range(whole, parts.shape[0]):
            pair, matrix = divmod(unit - whole, 3)
            out = outs[matrix - 3]
            out[:, pair * LANES : (pair + 1) * LANES] = parts[unit].astype(F32)

    mine = pl.program_id(0) == core_ref[0]

    @pl.when(mine)
    def _():
        write(mine_ref)

    @pl.when(jnp.logical_not(mine))
    def _():
        write(other_ref)


def assemble(core, mine, other, width, outs):
    mine, other = (part.reshape(-1, width // 2, LANES) for part in (mine, other))
    whole = 0 if outs else width // LANES
    columns = (mine.shape[0] - whole) // 3 * LANES
    out = jax.ShapeDtypeStruct((width, width), F32)
    specs = [pl.BlockSpec((width // 2, columns), lambda i, core: (i, 1 if outs else 0))] * 3
    if whole:
        specs = [pl.BlockSpec((width // 2, width), lambda i, core: (i, 0))] + specs
    return pl.pallas_call(
        functools.partial(assemble_kernel, whole=whole),
        grid_spec=pltpu.PrefetchScalarGridSpec(
            num_scalar_prefetch=1,
            grid=(2,),
            in_specs=[const(*mine.shape)] * 2
            + [pl.BlockSpec(memory_space=pl.ANY)] * len(outs),
            out_specs=specs,
        ),
        out_shape=[out] * len(specs),
        input_output_aliases={3 + index: index for index in range(len(outs))},
        cost_estimate=LIGHT,
        name="assemble",
    )(core, mine, other, *outs)


def swap(value, axis, bit):
    size = lax.axis_size(axis)
    return lax.ppermute(value, axis, [(i, i ^ bit) for i in range(size)])


def stages(axis, low, high):
    found = []
    bit = low
    while bit < min(high, lax.axis_size(axis)):
        found.append((axis, bit))
        bit *= 2
    return found


def bit_of(axis, bit):
    return (lax.axis_index(axis) // bit) % 2


def add_low(left, right):
    return (left.astype(F32) + right.astype(F32)).astype(BF16)


def add(left, right):
    return left + right


def halves(rows, stage):
    axis, bit = stage
    half = rows.shape[0] // 2
    mine = bit_of(axis, bit)
    return (
        lax.dynamic_slice_in_dim(rows, (1 - mine) * half, half, 0),
        lax.dynamic_slice_in_dim(rows, mine * half, half, 0),
    )


def joined(rows, other, stage):
    first = bit_of(*stage) == 0
    return jnp.concatenate([jnp.where(first, rows, other), jnp.where(first, other, rows)], axis=0)


def add_split_kernel(mine_ref, left_ref, right_ref, send_ref, keep_ref):
    value = add_low(left_ref[...], right_ref[...])

    @pl.when(pl.program_id(0) == 0)
    def _():
        send_ref[...] = value

    @pl.when(pl.program_id(0) == 1)
    def _():
        keep_ref[...] = value


def add_split(left, right, stage):
    half, width = left.shape[0] // 2, left.shape[1]
    if half % 8:
        return halves(add_low(left, right), stage)
    mine = bit_of(*stage).astype(jnp.int32)[None]
    block = pl.BlockSpec((half, width), lambda i, mine: (jnp.where(i == 0, 1 - mine[0], mine[0]), 0))
    out = pl.BlockSpec((half, width), lambda i, mine: (0, 0))
    shape = jax.ShapeDtypeStruct((half, width), BF16)
    return pl.pallas_call(
        add_split_kernel,
        grid_spec=pltpu.PrefetchScalarGridSpec(
            num_scalar_prefetch=1,
            grid=(2,),
            in_specs=[block, block],
            out_specs=[out, out],
        ),
        out_shape=[shape, shape],
        cost_estimate=LIGHT,
        name="add_split",
    )(mine, left, right)


def halves_sum(left, right, stage):
    width = left.shape[2]
    parts = add_split(left.reshape(-1, width), right.reshape(-1, width), stage)
    return [part.reshape(-1, *left.shape[1:]) for part in parts]


class Sum:
    def __init__(self, keep, send, stages, plus=add_low, split=True):
        self.keep, self.send, self.plus = keep, send, plus
        if split:
            self.steps = [("whole", stages[0])]
            self.steps += [("halve", stage) for stage in stages[1:-1]]
            self.steps += [("whole", stages[-1])]
            self.steps += [("join", stage) for stage in stages[-2:2:-1]]
            self.steps += [("both", stages[2:0:-1]), ("corner", stages[2:0:-1])]
        else:
            self.steps = [("whole", stage) for stage in stages]

    def start(self):
        kind, stage = self.steps[0]
        if kind == "both":
            return [swap(self.keep, *each) for each in stage]
        if kind == "corner":
            near, far = self.got
            half = near.shape[0] // 2
            return [swap(near[:half], *stage[1]), swap(far[half:], *stage[0])]
        return [swap(self.send, *stage)]

    def finish(self, got):
        kind, stage = self.steps.pop(0)
        if kind == "both":
            self.got = got
        elif kind == "corner":
            near, far = self.got
            mine = joined(self.keep, near, stage[0])
            other = joined(far, jnp.concatenate(got, axis=0), stage[0])
            self.keep = joined(mine, other, stage[1])
        elif self.steps and self.steps[0][0] == "halve":
            self.send, self.keep = add_split(self.keep, got[0], self.steps[0][1])
        else:
            join = functools.partial(joined, stage=stage)
            self.keep = self.send = (join if kind == "join" else self.plus)(self.keep, got[0])


def advance(sums, *others):
    sums = [each for each in sums if each.steps]
    got, others = tie(([each.start() for each in sums], others))
    for each, arrived in zip(sums, got):
        each.finish(arrived)
    return others[0] if len(others) == 1 else others


def chip_stages(total):
    return [("dp", 2 << index) for index in range((total.shape[0]).bit_length() - 1)][::-1]


tie = lax.optimization_barrier


def exchange(rows):
    return lax.all_to_all(rows, "expert", split_axis=0, concat_axis=0, tiled=True)


def local(
    tokens,
    routing,
    query_weight,
    key_weight,
    value_weight,
    output_weight,
    first_gain,
    first_bias,
    second_gain,
    second_bias,
    centroids,
    expert_up,
    expert_down,
    cotangent,
):
    length, width = tokens.shape
    experts = centroids.shape[0]
    capacity = length // experts
    peers = lax.axis_size("expert")
    parts = lax.axis_size("dp")
    slots = experts * capacity
    core = (lax.axis_index("dp") % 2).astype(jnp.int32)[None]
    vectors = tie(jnp.stack([first_gain, first_bias, second_gain, second_bias]))
    first_gain, first_bias, second_gain, second_bias = (vectors[i : i + 1] for i in range(4))
    weights = (query_weight, key_weight, value_weight)

    cots, slot, wide = route(routing.reshape(1, length), cotangent, experts, capacity)
    cots, tokens = tie((cots, tokens))
    cots = exchange(cots.reshape(peers, -1, width)).reshape(slots, width)

    queries, keys, values, mixed, probs = attention(tokens, first_gain, first_bias, weights)
    resid, rows = branch(mixed, tokens, output_weight, second_gain, second_bias, slot, slots)

    rows, cots = tie((rows, cots))
    rows = exchange(rows.reshape(peers, -1, width))
    cots_down = expert_cots(cots, expert_down)
    settled = settle(
        tokens, first_gain, first_bias, mixed, resid, second_gain, second_bias, centroids, routing
    )
    rows, cots_down, *settled = tie((rows, cots_down, *settled))
    normed_turned, mixed_turned, xhat, scale, gate = settled
    rows = rows.reshape(slots, width)
    own = centroids[lax.axis_index("expert")][None, :]
    produced, returned, grad_rows, hidden, grad_pre = expert(
        rows, cots, cots_down, own, expert_up, expert_down
    )
    returned = exchange(returned.reshape(peers, -1, width))
    up_send, down_send, up_keep, down_keep = expert_weights(
        rows, grad_rows, hidden, grad_pre, parts, core
    )
    chips = chip_stages(up_send)
    up_send, up_keep = halves_sum(up_keep, swap(up_send, "dp", 1), chips[0])
    down_send, down_keep = halves_sum(down_keep, swap(down_send, "dp", 1), chips[0])
    returned, produced, up_send, up_keep, down_send, down_keep = tie(
        (returned, produced, up_send, up_keep, down_send, down_keep)
    )
    returned = returned.reshape(slots, width)
    up_got = swap(up_send, *chips[0])
    down_got = swap(down_send, *chips[0])
    produced = exchange(produced.reshape(peers, -1, width))

    pairs = width // LANES
    split = pairs // 2
    grad_resid, grad_mixed, second_sums, *units = second_back(
        core, wide, returned, xhat, scale, cotangent, second_gain, output_weight, mixed_turned,
        pairs + 3 * split,
    )

    cross = stages("expert", 1, 1 << 20)
    apart = stages("dp", 2, 1 << 20)
    back = functools.partial(
        attention_back, core, queries, keys, values, grad_mixed, mixed, normed_turned
    )
    left, send, keep = back(probs, 0, split, units)
    left, send, keep, up_got = tie((left, send, keep, up_got))
    early = Sum(keep.reshape(-1, LANES), send.reshape(-1, LANES), [("dp", 1)] + cross + apart)
    advance([early])
    early.send, *probs = tie((early.send, *probs))
    right, send, keep = back(probs, split, pairs - split, None)
    right, send, keep, produced = advance([early], right, send, keep, produced)
    produced = produced.reshape(slots, width)
    order = [("dp", 1)] + apart + cross[1:2] + cross[:1] + cross[2:]
    late = Sum(keep.reshape(-1, LANES), send.reshape(-1, LANES), order)
    layer_out = layer_output(wide, produced, resid, gate)
    layer_out, down_got = advance([early, late], layer_out, down_got)
    grad_tokens, first_sums = first_back(left, right, tokens, grad_resid, first_gain, weights)
    grad_tokens, first_sums = advance([early, late], grad_tokens, first_sums)
    grad_up = up_keep.astype(F32) + up_got.astype(F32)
    grad_down = down_keep.astype(F32) + down_got.astype(F32)
    for stage in chips[1:]:
        grad_up, grad_down = (
            keep.astype(F32) + swap(send, *stage).astype(F32)
            for send, keep in (halves(value.astype(BF16), stage) for value in (grad_up, grad_down))
        )
    grad_up, grad_down = (value.reshape(value.shape[1:])[None] for value in (grad_up, grad_down))
    small = jnp.concatenate([first_sums, second_sums], axis=0)
    small = Sum(small, small, stages("dp", 1, 1 << 20) + cross, plus=add, split=False)
    while len(early.steps) > 2:
        advance([early, late, small])
    grad_up, grad_down = advance([early, late, small], grad_up, grad_down)
    while early.steps:
        advance([early, late, small])
    core_swap = swap(early.keep, "dp", 1)
    while len(late.steps) > 1:
        core_swap = advance([late, small], core_swap)
    outs = assemble(core, early.keep, core_swap, width, [])
    grad_output, *outs = advance([late, small], *outs)
    while small.steps:
        advance([small])
    grad_query, grad_key, grad_value = assemble(
        core, late.keep, swap(late.keep, "dp", 1), width, outs
    )
    small = small.keep
    return (
        layer_out,
        grad_tokens,
        grad_query,
        grad_key,
        grad_value,
        grad_output,
        small[0],
        small[1],
        small[2],
        small[3],
        grad_up,
        grad_down,
    )


def solution(mesh):
    rows = P(("dp", "expert"), None)
    return jax.shard_map(
        local,
        mesh=mesh,
        in_specs=(rows, rows)
        + (P(),) * 9
        + (P("expert", None, None), P("expert", None, None), rows),
        out_specs=(rows, rows) + (P(),) * 8 + (P("expert", None, "dp"), P("expert", "dp", None)),
        check_vma=False,
    )
```

```python
import functools
import math

import jax
import jax.numpy as jnp
from jax import lax
from jax.experimental import pallas as pl
from jax.experimental.pallas import tpu as pltpu
from jax.sharding import PartitionSpec as P

HEADS = 12
HEAD = 64
LANES = 128
EPS = 1e-05
F32 = jnp.float32
BF16 = jnp.bfloat16
ROWS = 256

LIGHT = pl.CostEstimate(flops=1000000, bytes_accessed=100000, transcendentals=0)


def contract(left, right, left_dim, right_dim):
    return lax.dot_general(
        left, right, (((left_dim,), (right_dim,)), ((), ())), preferred_element_type=F32
    )


def normalize(values, gain, bias):
    centered = values - jnp.mean(values, axis=-1, keepdims=True)
    variance = jnp.mean(centered * centered, axis=-1, keepdims=True)
    scale = lax.rsqrt(variance + EPS)
    xhat = centered * scale
    return xhat * gain + bias, xhat, scale


def normalize_back(grad, xhat, scale, gain):
    scaled = grad * gain
    first = jnp.mean(scaled, axis=-1, keepdims=True)
    cross = jnp.mean(scaled * xhat, axis=-1, keepdims=True)
    return scale * (scaled - first - xhat * cross)


def head_mask(parity, value):
    lane = lax.broadcasted_iota(jnp.int32, (1, LANES), 1)
    return jnp.where(lane // HEAD == parity, value, 0.0).astype(BF16)


def causal_bias(bias_ref, keys_dim):
    @pl.when((pl.program_id(0) == 0) & (pl.program_id(1) == 0))
    def _():
        key = lax.broadcasted_iota(jnp.int32, bias_ref.shape, keys_dim)
        query = lax.broadcasted_iota(jnp.int32, bias_ref.shape, 1 - keys_dim)
        bias_ref[...] = jnp.where(key <= query, 0.0, -1e30)


def attention_kernel(tokens_ref, gain_ref, shift_ref, *refs, block):
    first_weights, next_weights, (q_ref, k_ref, v_ref, o_ref) = refs[:3], refs[3:6], refs[6:10]
    *probs_refs, normed_ref, made_ref, bias_ref = refs[10:]
    causal_bias(bias_ref, 0)
    pair, parity = pl.program_id(0), pl.program_id(1)
    length = made_ref.shape[0]

    @pl.when((pair == 0) & (parity == 0))
    def _():
        weights = jnp.concatenate([weight[...] for weight in first_weights], axis=1)
        for index in range(len(probs_refs)):
            rows = slice(index * block, (index + 1) * block)
            normed, _, _ = normalize(tokens_ref[rows, :].astype(F32), gain_ref[...], shift_ref[...])
            normed = normed.astype(BF16)
            normed_ref[rows, :] = normed
            made_ref[rows, :] = contract(normed, weights, 1, 0).astype(BF16)

    @pl.when(parity == 0)
    def _():
        for index, out in enumerate((q_ref, k_ref, v_ref)):
            out[...] = made_ref[:, index * LANES : (index + 1) * LANES]

    weights = jnp.concatenate([weight[...] for weight in next_weights], axis=1)
    part = length // 2 // len(probs_refs)
    queries = q_ref[...] * head_mask(parity, HEAD**-0.5)
    values = v_ref[...] * head_mask(parity, 1.0)
    outs = []
    for index, probs_ref in enumerate(probs_refs):
        first, finish = index * block, (index + 1) * block
        scores = contract(k_ref[:finish, :], queries[first:finish], 1, 1)
        rows = pl.ds(pl.multiple_of(parity * (length // 2) + index * part, part), part)
        made_ref[rows, :] = contract(normed_ref[rows, :], weights, 1, 0).astype(BF16)
        diagonal = scores[first:] + bias_ref[...]
        if index:
            scores = jnp.concatenate([scores[:first], diagonal], axis=0)
        else:
            scores = diagonal
        shifted = jnp.exp(scores - jnp.max(scores, axis=0, keepdims=True))
        total = jnp.sum(shifted, axis=0, keepdims=True)
        probs = (shifted * (1.0 / total)).astype(BF16)
        probs_ref[0] = probs
        outs.append(contract(probs, values[:finish], 0, 0).astype(BF16))
    mixed = jnp.concatenate(outs, axis=0)

    @pl.when(parity == 0)
    def _():
        o_ref[...] = mixed

    @pl.when(parity == 1)
    def _():
        o_ref[...] = o_ref[...] + mixed


def attention(tokens, gain, shift, weights):
    length, width = tokens.shape
    pairs = width // LANES
    block = min(256, length)
    finishes = range(block, length + 1, block)
    spec = pl.BlockSpec((length, LANES), lambda pair, parity: (0, pair))
    ahead = pl.BlockSpec(
        (width, LANES), lambda pair, parity: (0, jnp.minimum(pair + 1, pairs - 1))
    )
    wide = jax.ShapeDtypeStruct((length, width), BF16)
    queries, keys, values, mixed, *probs = pl.pallas_call(
        functools.partial(attention_kernel, block=block),
        grid=(pairs, 2),
        in_specs=[const(length, width), const(1, width), const(1, width)]
        + [const(width, LANES)] * 3
        + [ahead] * 3,
        out_specs=[spec] * 4
        + [
            pl.BlockSpec((1, finish, block), lambda pair, parity: (pair * 2 + parity, 0, 0))
            for finish in finishes
        ],
        out_shape=[wide] * 4
        + [jax.ShapeDtypeStruct((2 * pairs, finish, block), BF16) for finish in finishes],
        scratch_shapes=[
            pltpu.VMEM((length, width), BF16),
            pltpu.VMEM((length, 3 * LANES), BF16),
            pltpu.VMEM((block, block), F32),
        ],
        cost_estimate=LIGHT,
        name="attention",
    )(tokens, gain, shift, *weights, *weights)
    return queries, keys, values, mixed, probs


def attention_back_kernel(
    core_ref, q_ref, k_ref, v_ref, g_ref, o_ref, turned_ref, *refs, block, blocks
):
    probs_refs = refs[:blocks]
    grads_ref, send_ref, keep_ref, dk_sum, dv_sum = refs[-5:]
    parity = pl.program_id(1)
    scale_mask = head_mask(parity, HEAD**-0.5)
    queries = q_ref[...] * scale_mask
    grads = g_ref[...] * head_mask(parity, 1.0)
    keys_scaled = k_ref[...] * scale_mask
    dk_sum[...] = jnp.zeros_like(dk_sum)
    dv_sum[...] = jnp.zeros_like(dv_sum)
    dq_parts = []
    for index, probs_ref in enumerate(probs_refs):
        first, finish = index * block, (index + 1) * block
        probs = probs_ref[0]
        some = grads[first:finish]
        dv_sum[:finish, :] += contract(probs, some, 1, 0)
        grad_probs = contract(v_ref[:finish, :], some, 1, 1)
        shares = some.astype(F32) * o_ref[first:finish, :].astype(F32)
        delta = jnp.sum(jnp.transpose(shares), axis=0, keepdims=True)
        grad_scores = (probs.astype(F32) * (grad_probs - delta)).astype(BF16)
        dk_sum[:finish, :] += contract(grad_scores, queries[first:finish], 1, 0)
        dq_parts.append(contract(grad_scores, keys_scaled[:finish], 0, 0).astype(BF16))
    parts = (
        jnp.concatenate(dq_parts, axis=0),
        dk_sum[...].astype(BF16),
        dv_sum[...].astype(BF16),
    )

    @pl.when(parity == 0)
    def _():
        for index, part in enumerate(parts):
            grads_ref[index] = part

    @pl.when(parity == 1)
    def _():
        whole = [grads_ref[index] + part for index, part in enumerate(parts)]
        for index, part in enumerate(whole):
            grads_ref[index] = part
        weight_parts(core_ref, turned_ref[...], jnp.concatenate(whole, axis=1), send_ref, keep_ref)


def weight_parts(core_ref, turned, grads, send_ref, keep_ref):
    product = contract(turned, grads, 1, 0).astype(BF16)
    rows = send_ref.shape[1]

    def write(upper, lower):
        for index in range(grads.shape[1] // LANES):
            columns = slice(index * LANES, (index + 1) * LANES)
            upper[index] = product[:rows, columns]
            lower[index] = product[rows:, columns]

    @pl.when(core_ref[0] == 0)
    def _():
        write(keep_ref, send_ref)

    @pl.when(core_ref[0] != 0)
    def _():
        write(send_ref, keep_ref)


SCALAR = pl.BlockSpec(memory_space=pltpu.SMEM)


def attention_back(core, queries, keys, values, grads, mixed, turned, probs, start, pairs, units):
    length, width = queries.shape
    block = probs[0].shape[2]
    spec = pl.BlockSpec((length, LANES), lambda pair, parity: (0, start + pair))
    whole = pl.BlockSpec((width, length), lambda pair, parity: (0, 0))
    ahead = 0 if units is None else units[0].shape[0] // 3 - pairs
    shape = jax.ShapeDtypeStruct((3 * (ahead + pairs), width // 2, LANES), BF16)
    unit = pl.BlockSpec((3, width // 2, LANES), lambda pair, parity: (ahead + pair, 0, 0))
    args = [core, queries, keys, values, grads, mixed, turned, *probs]
    alias = {}
    if units is not None:
        alias = {len(args): 1, len(args) + 1: 2}
        args += units
    return pl.pallas_call(
        functools.partial(attention_back_kernel, block=block, blocks=len(probs)),
        grid=(pairs, 2),
        in_specs=[SCALAR, spec, spec, spec, spec, spec, whole]
        + [
            pl.BlockSpec(
                (1, *part.shape[1:]), lambda pair, parity: ((start + pair) * 2 + parity, 0, 0)
            )
            for part in probs
        ]
        + [pl.BlockSpec(memory_space=pl.ANY)] * len(alias),
        out_specs=[pl.BlockSpec((3, length, LANES), lambda pair, parity: (0, 0, pair)), unit, unit],
        out_shape=[jax.ShapeDtypeStruct((3, length, pairs * LANES), BF16), shape, shape],
        input_output_aliases=alias,
        scratch_shapes=[pltpu.VMEM((length, LANES), F32)] * 2,
        cost_estimate=LIGHT,
        name="attention_back",
    )(*args)


def gelu_parts(value):
    cdf = 0.5 + 0.5 * lax.erf(value * 0.5**0.5)
    density = jnp.exp2(value * value * (-0.5 / math.log(2.0)))
    return cdf, value * (density * (1.0 / math.sqrt(2.0 * math.pi)))


def expert_cots_kernel(c_ref, down_ref, out_ref):
    out_ref[...] = contract(c_ref[...], down_ref[0], 1, 1).astype(BF16)


def expert_cots(cots, down):
    count, width = cots.shape
    hidden = down.shape[1]
    tile = min(512, hidden)
    return pl.pallas_call(
        expert_cots_kernel,
        grid=(hidden // tile,),
        in_specs=[
            pl.BlockSpec((count, width), lambda f: (0, 0)),
            pl.BlockSpec((1, tile, width), lambda f: (0, f, 0)),
        ],
        out_specs=pl.BlockSpec((count, tile), lambda f: (0, f)),
        out_shape=jax.ShapeDtypeStruct((count, hidden), BF16),
        cost_estimate=LIGHT,
        name="expert_cots",
    )(cots, down)


def expert_kernel(
    x_ref, c_ref, cd_ref, cen_ref, up_ref, down_ref,
    y_ref, gs_ref, dy_ref, h_ref, dp_ref,
    y_sum, dx_sum, gate_ref,
):
    step = pl.program_id(0)

    @pl.when(step == 0)
    def _():
        logit = jnp.sum(x_ref[...].astype(F32) * cen_ref[...], axis=1, keepdims=True)
        gate = jax.nn.sigmoid(logit)
        gate_ref[...] = jnp.broadcast_to(gate, gate_ref.shape)
        dy_ref[...] = (c_ref[...].astype(F32) * gate).astype(BF16)
        y_sum[...] = jnp.zeros_like(y_sum)
        dx_sum[...] = jnp.zeros_like(dx_sum)

    pre = contract(x_ref[...], up_ref[0], 1, 0)
    cdf, weighted = gelu_parts(pre)
    hidden = (pre * cdf).astype(BF16)
    slope = cdf + weighted
    h_ref[...] = hidden
    y_sum[...] += contract(hidden, down_ref[0], 1, 0)
    grad_hidden = cd_ref[...].astype(F32) * gate_ref[:, 0:1]
    grad_pre = (grad_hidden * slope).astype(BF16)
    dp_ref[...] = grad_pre
    dx_sum[...] += contract(grad_pre, up_ref[0], 1, 1)

    @pl.when(step == pl.num_programs(0) - 1)
    def _():
        produced = y_sum[...].astype(BF16)
        y_ref[...] = produced
        gate = gate_ref[:, 0:1]
        dot = jnp.sum(c_ref[...].astype(F32) * produced.astype(F32), axis=1, keepdims=True)
        grad_logit = dot * gate * (1.0 - gate)
        back = dx_sum[...].astype(BF16).astype(F32) + grad_logit * cen_ref[...]
        gs_ref[...] = back.astype(BF16)


def expert(rows, cots, cots_down, centroid, up, down):
    count, width = rows.shape
    hidden = up.shape[2]
    tile = min(512, hidden)
    whole = pl.BlockSpec((count, width), lambda f: (0, 0))
    wide = jax.ShapeDtypeStruct((count, width), BF16)
    deep = jax.ShapeDtypeStruct((count, hidden), BF16)
    return pl.pallas_call(
        expert_kernel,
        grid=(hidden // tile,),
        in_specs=[
            whole,
            whole,
            pl.BlockSpec((count, tile), lambda f: (0, f)),
            pl.BlockSpec((1, width), lambda f: (0, 0)),
            pl.BlockSpec((1, width, tile), lambda f: (0, 0, f)),
            pl.BlockSpec((1, tile, width), lambda f: (0, f, 0)),
        ],
        out_specs=[whole, whole, whole]
        + [pl.BlockSpec((count, tile), lambda f: (0, f))] * 2,
        out_shape=[wide, wide, wide, deep, deep],
        scratch_shapes=[
            pltpu.VMEM((count, width), F32),
            pltpu.VMEM((count, width), F32),
            pltpu.VMEM((count, LANES), F32),
        ],
        cost_estimate=LIGHT,
        name="expert",
    )(rows, cots, cots_down, centroid, up, down)


def expert_weights_kernel(
    core_ref, x_ref, dy_ref, h_ref, dp_ref,
    up_send_ref, down_send_ref, up_keep_ref, down_keep_ref, xt_ref,
):
    @pl.when(pl.program_id(0) == 0)
    def _():
        xt_ref[...] = jnp.transpose(x_ref[...])

    up = contract(xt_ref[...], dp_ref[...], 1, 0).astype(BF16)
    down = contract(h_ref[...], dy_ref[...], 0, 0).astype(BF16)
    sending = pl.program_id(0) < pl.num_programs(0) // 2

    @pl.when(sending)
    def _():
        up_send_ref[0] = up
        down_send_ref[0] = down

    @pl.when(jnp.logical_not(sending))
    def _():
        up_keep_ref[0] = up
        down_keep_ref[0] = down


def expert_weights(rows, grads, hidden_rows, grad_pre, parts, core):
    count, width = rows.shape
    hidden = hidden_rows.shape[1]
    share = hidden // parts
    tile = min(384, share)
    each = share // tile
    half = hidden // tile // 2

    def column(f, core):
        step = f % half
        other = jnp.where(f < half, 1 - core[0], core[0])
        return ((step // each) * 2 + other) * each + step % each

    def send(f):
        return jnp.minimum(f, half - 1)

    def keep(f):
        return jnp.maximum(f - half, 0)

    whole = pl.BlockSpec((count, width), lambda f, core: (0, 0))
    deep = pl.BlockSpec((count, tile), lambda f, core: (0, column(f, core)))
    up = [
        pl.BlockSpec((1, width, tile), lambda f, core, at=at: (at(f) // each, 0, at(f) % each))
        for at in (send, keep)
    ]
    down = [
        pl.BlockSpec((1, tile, width), lambda f, core, at=at: (at(f) // each, at(f) % each, 0))
        for at in (send, keep)
    ]
    up_shape = jax.ShapeDtypeStruct((parts // 2, width, share), BF16)
    down_shape = jax.ShapeDtypeStruct((parts // 2, share, width), BF16)
    return pl.pallas_call(
        expert_weights_kernel,
        grid_spec=pltpu.PrefetchScalarGridSpec(
            num_scalar_prefetch=1,
            grid=(2 * half,),
            in_specs=[whole, whole, deep, deep],
            out_specs=[up[0], down[0], up[1], down[1]],
            scratch_shapes=[pltpu.VMEM((width, count), BF16)],
        ),
        out_shape=[up_shape, down_shape, up_shape, down_shape],
        cost_estimate=LIGHT,
        name="expert_weights",
    )(core, rows, grads, hidden_rows, grad_pre)


def one_hot(condition):
    return jnp.where(condition, 1.0, 0.0).astype(BF16)


def block_rows(step, count, length, dim):
    return step * count + lax.broadcasted_iota(jnp.int32, (count, length), dim)


def const(*shape):
    return pl.BlockSpec(shape, lambda *step: (0,) * len(shape))


def route_kernel(routing_ref, cot_ref, send_ref, slot_ref, wide_ref, *, experts, capacity):
    length = routing_ref.shape[1]
    step = pl.program_id(0)

    @pl.when(step == 0)
    def _():
        chosen = routing_ref[...]
        named = lax.broadcasted_iota(jnp.int32, (experts, length), 0) == chosen
        named = jnp.where(named, 1.0, 0.0)
        lane = lax.broadcasted_iota(jnp.int32, (experts, length), 1)
        count = named
        shift = 1
        while shift < length:
            count = count + jnp.where(lane >= shift, pltpu.roll(count, shift, 1), 0.0)
            shift *= 2
        position = jnp.sum(named * (count - named), axis=0, keepdims=True)
        slot = chosen.astype(F32) * capacity + position
        slot = jnp.where(position < capacity, slot, -1.0)
        slot_ref[...] = slot.astype(jnp.int32)
        wide_ref[...] = jnp.transpose(jnp.broadcast_to(slot, (LANES, length))).astype(jnp.int32)

    place = one_hot(block_rows(step, send_ref.shape[0], length, 0) == slot_ref[...])
    send_ref[...] = contract(place, cot_ref[...], 1, 0).astype(BF16)


def route(routing, cotangent, experts, capacity):
    length, width = cotangent.shape
    slots = experts * capacity
    return pl.pallas_call(
        functools.partial(route_kernel, experts=experts, capacity=capacity),
        grid=(slots // ROWS,),
        in_specs=[const(1, length), const(length, width)],
        out_specs=[
            pl.BlockSpec((ROWS, width), lambda i: (i, 0)),
            const(1, length),
            const(length, LANES),
        ],
        out_shape=[
            jax.ShapeDtypeStruct((slots, width), BF16),
            jax.ShapeDtypeStruct((1, length), jnp.int32),
            jax.ShapeDtypeStruct((length, LANES), jnp.int32),
        ],
        cost_estimate=LIGHT,
        name="route",
    )(routing, cotangent)


def settle_kernel(
    tokens_ref, first_gain_ref, first_bias_ref, mixed_ref, resid_ref, gain_ref, bias_ref,
    cen_ref, chosen_ref,
    normed_ref, turned_ref, xhat_ref, scale_ref, gate_ref,
):
    normed, _, _ = normalize(tokens_ref[...].astype(F32), first_gain_ref[...], first_bias_ref[...])
    normed_ref[...] = jnp.transpose(normed.astype(BF16))
    turned_ref[...] = jnp.transpose(mixed_ref[...])
    second, xhat, scale = normalize(resid_ref[...], gain_ref[...], bias_ref[...])
    xhat_ref[...] = xhat.astype(BF16)
    scale_ref[...] = scale
    centroid = jnp.zeros_like(second)
    for index in range(cen_ref.shape[0]):
        centroid = jnp.where(chosen_ref[...] == index, cen_ref[index : index + 1, :], centroid)
    gate_ref[...] = jax.nn.sigmoid(jnp.sum(second * centroid, axis=1, keepdims=True))


def settle(tokens, first_gain, first_bias, mixed, resid, gain, bias, centroids, routing):
    length, width = tokens.shape
    rows = pl.BlockSpec((ROWS, width), lambda i: (i, 0))
    thin = pl.BlockSpec((ROWS, 1), lambda i: (i, 0))
    turned = pl.BlockSpec((width, ROWS), lambda i: (0, i))
    vector = const(1, width)
    column = jax.ShapeDtypeStruct((length, 1), F32)
    return pl.pallas_call(
        settle_kernel,
        grid=(length // ROWS,),
        in_specs=[rows, vector, vector, rows, rows, vector, vector, const(*centroids.shape), thin],
        out_specs=[turned, turned, rows, thin, thin],
        out_shape=[jax.ShapeDtypeStruct((width, length), BF16)] * 2
        + [jax.ShapeDtypeStruct((length, width), BF16), column, column],
        cost_estimate=LIGHT,
        name="settle",
    )(tokens, first_gain, first_bias, mixed, resid, gain, bias, centroids, routing)


def branch_kernel(
    mixed_ref, tokens_ref, weight_ref, gain_ref, bias_ref, slot_ref,
    resid_ref, send_ref, low_ref, *, blocks,
):
    step = pl.program_id(0)

    @pl.when(step < blocks)
    def _():
        resid = tokens_ref[...].astype(F32) + contract(mixed_ref[...], weight_ref[...], 1, 0)
        second, _, _ = normalize(resid, gain_ref[...], bias_ref[...])
        resid_ref[...] = resid
        low_ref[pl.ds(pl.multiple_of(step * ROWS, ROWS), ROWS), :] = second.astype(BF16)

    @pl.when(step >= blocks)
    def _():
        place = one_hot(block_rows(step - blocks, ROWS, slot_ref.shape[1], 0) == slot_ref[...])
        send_ref[...] = contract(place, low_ref[...], 1, 0).astype(BF16)


def branch(mixed, tokens, weight, gain, bias, slot, slots):
    length, width = mixed.shape
    blocks = length // ROWS

    def at(i):
        return jnp.minimum(i, blocks - 1)

    rows = pl.BlockSpec((ROWS, width), lambda i: (at(i), 0))
    return pl.pallas_call(
        functools.partial(branch_kernel, blocks=blocks),
        grid=(blocks + slots // ROWS,),
        in_specs=[
            rows,
            rows,
            const(width, width),
            const(1, width),
            const(1, width),
            const(1, length),
        ],
        out_specs=[
            rows,
            pl.BlockSpec((ROWS, width), lambda i: (jnp.maximum(i - blocks, 0), 0)),
        ],
        out_shape=[
            jax.ShapeDtypeStruct((length, width), F32),
            jax.ShapeDtypeStruct((slots, width), BF16),
        ],
        scratch_shapes=[pltpu.VMEM((length, width), BF16)],
        cost_estimate=LIGHT,
        name="branch",
    )(mixed, tokens, weight, gain, bias, slot)


def gathered(wide_ref, rows_ref):
    slots = rows_ref.shape[0]
    count = wide_ref.shape[0]
    wide = jnp.concatenate([wide_ref[...]] * (slots // LANES), axis=1)
    place = one_hot(lax.broadcasted_iota(jnp.int32, (count, slots), 1) == wide)
    return contract(place, rows_ref[...], 1, 0)


def second_back_kernel(
    core_ref, wide_ref, back_ref, xhat_ref, scale_ref, cot_ref, gain_ref, weight_ref, turned_ref,
    grad_ref, mixed_ref, sums_ref, send_ref, keep_ref, total_ref,
):
    grad = gathered(wide_ref, back_ref)
    xhat, scale = xhat_ref[...].astype(F32), scale_ref[...]
    sums = jnp.concatenate(
        [jnp.sum(grad * xhat, axis=0, keepdims=True), jnp.sum(grad, axis=0, keepdims=True)], axis=0
    )

    @pl.when(pl.program_id(0) == 0)
    def _():
        sums_ref[...] = sums

    @pl.when(pl.program_id(0) > 0)
    def _():
        sums_ref[...] = sums_ref[...] + sums

    grad = cot_ref[...].astype(F32) + normalize_back(grad, xhat, scale, gain_ref[...])
    low = grad.astype(BF16)
    grad_ref[...] = low
    mixed_ref[...] = contract(low, weight_ref[...], 1, 1).astype(BF16)
    product = contract(turned_ref[...], low, 1, 0)

    @pl.when(pl.program_id(0) == 0)
    def _():
        total_ref[...] = product

    @pl.when(pl.program_id(0) > 0)
    def _():
        total_ref[...] += product

    @pl.when(pl.program_id(0) == pl.num_programs(0) - 1)
    def _():
        rows = send_ref.shape[1]
        for index in range(send_ref.shape[0]):
            columns = slice(index * LANES, (index + 1) * LANES)
            for half, out in ((1 - core_ref[0], send_ref), (core_ref[0], keep_ref)):
                at = pl.ds(pl.multiple_of(half * rows, rows), rows)
                out[index] = total_ref[at, columns].astype(BF16)


def second_back(core, wide, back, xhat, scale, cotangent, gain, weight, turned, units):
    length, width = xhat.shape
    rows = pl.BlockSpec((ROWS, width), lambda i: (i, 0))
    own = const(width // LANES, width // 2, LANES)
    shape = jax.ShapeDtypeStruct((units, width // 2, LANES), BF16)
    return pl.pallas_call(
        second_back_kernel,
        grid=(length // ROWS,),
        in_specs=[
            SCALAR,
            pl.BlockSpec((ROWS, LANES), lambda i: (i, 0)),
            const(*back.shape),
            rows,
            pl.BlockSpec((ROWS, 1), lambda i: (i, 0)),
            rows,
            const(1, width),
            const(width, width),
            pl.BlockSpec((width, ROWS), lambda i: (0, i)),
        ],
        out_specs=[rows, rows, const(2, width), own, own],
        out_shape=[
            jax.ShapeDtypeStruct((length, width), BF16),
            jax.ShapeDtypeStruct((length, width), BF16),
            jax.ShapeDtypeStruct((2, width), F32),
            shape,
            shape,
        ],
        scratch_shapes=[pltpu.VMEM((width, width), F32)],
        cost_estimate=LIGHT,
        name="second_back",
    )(core, wide, back, xhat, scale, cotangent, gain, weight, turned)


def first_back_kernel(
    left_ref, right_ref, tokens_ref, resid_ref, gain_ref, wq_ref, wk_ref, wv_ref,
    grad_ref, sums_ref,
):
    side = left_ref.shape[2]
    grad = 0.0
    for index, weight in enumerate((wq_ref, wk_ref, wv_ref)):
        grad = grad + contract(left_ref[index], weight[:, :side], 1, 1)
        grad = grad + contract(right_ref[index], weight[:, side:], 1, 1)
    gain = gain_ref[...]
    _, xhat, scale = normalize(tokens_ref[...].astype(F32), gain, gain)
    sums = jnp.concatenate(
        [jnp.sum(grad * xhat, axis=0, keepdims=True), jnp.sum(grad, axis=0, keepdims=True)], axis=0
    )

    @pl.when(pl.program_id(0) == 0)
    def _():
        sums_ref[...] = sums

    @pl.when(pl.program_id(0) > 0)
    def _():
        sums_ref[...] = sums_ref[...] + sums

    grad_ref[...] = resid_ref[...].astype(F32) + normalize_back(grad, xhat, scale, gain)


def first_back(left, right, tokens, resid, gain, weights):
    length, width = tokens.shape
    rows = pl.BlockSpec((ROWS, width), lambda i: (i, 0))
    return pl.pallas_call(
        first_back_kernel,
        grid=(length // ROWS,),
        in_specs=[
            pl.BlockSpec((3, ROWS, part.shape[2]), lambda i: (0, i, 0)) for part in (left, right)
        ]
        + [rows, rows, const(1, width)]
        + [const(width, width)] * 3,
        out_specs=[rows, const(2, width)],
        out_shape=[
            jax.ShapeDtypeStruct((length, width), F32),
            jax.ShapeDtypeStruct((2, width), F32),
        ],
        cost_estimate=LIGHT,
        name="first_back",
    )(left, right, tokens, resid, gain, *weights)


def layer_out_kernel(wide_ref, rows_ref, resid_ref, gate_ref, out_ref):
    out_ref[...] = (resid_ref[...] + gate_ref[...] * gathered(wide_ref, rows_ref)).astype(BF16)


def layer_output(wide, produced, resid, gate):
    length, width = resid.shape
    rows = pl.BlockSpec((ROWS, width), lambda i: (i, 0))
    return pl.pallas_call(
        layer_out_kernel,
        grid=(length // ROWS,),
        in_specs=[
            pl.BlockSpec((ROWS, LANES), lambda i: (i, 0)),
            const(*produced.shape),
            rows,
            pl.BlockSpec((ROWS, 1), lambda i: (i, 0)),
        ],
        out_specs=rows,
        out_shape=jax.ShapeDtypeStruct((length, width), BF16),
        cost_estimate=LIGHT,
        name="layer_output",
    )(wide, produced, resid, gate)


def assemble_kernel(core_ref, mine_ref, other_ref, *outs, whole):
    outs = outs[-4:] if whole else outs[-3:]

    def write(parts):
        for unit in range(whole):
            outs[0][:, unit * LANES : (unit + 1) * LANES] = parts[unit].astype(F32)
        for unit in range(whole, parts.shape[0]):
            pair, matrix = divmod(unit - whole, 3)
            out = outs[matrix - 3]
            out[:, pair * LANES : (pair + 1) * LANES] = parts[unit].astype(F32)

    mine = pl.program_id(0) == core_ref[0]

    @pl.when(mine)
    def _():
        write(mine_ref)

    @pl.when(jnp.logical_not(mine))
    def _():
        write(other_ref)


def assemble(core, mine, other, width, outs):
    mine, other = (part.reshape(-1, width // 2, LANES) for part in (mine, other))
    whole = 0 if outs else width // LANES
    columns = (mine.shape[0] - whole) // 3 * LANES
    out = jax.ShapeDtypeStruct((width, width), F32)
    specs = [pl.BlockSpec((width // 2, columns), lambda i, core: (i, 1 if outs else 0))] * 3
    if whole:
        specs = [pl.BlockSpec((width // 2, width), lambda i, core: (i, 0))] + specs
    return pl.pallas_call(
        functools.partial(assemble_kernel, whole=whole),
        grid_spec=pltpu.PrefetchScalarGridSpec(
            num_scalar_prefetch=1,
            grid=(2,),
            in_specs=[const(*mine.shape)] * 2
            + [pl.BlockSpec(memory_space=pl.ANY)] * len(outs),
            out_specs=specs,
        ),
        out_shape=[out] * len(specs),
        input_output_aliases={3 + index: index for index in range(len(outs))},
        cost_estimate=LIGHT,
        name="assemble",
    )(core, mine, other, *outs)


def swap(value, axis, bit):
    size = lax.axis_size(axis)
    return lax.ppermute(value, axis, [(i, i ^ bit) for i in range(size)])


def stages(axis, low, high):
    found = []
    bit = low
    while bit < min(high, lax.axis_size(axis)):
        found.append((axis, bit))
        bit *= 2
    return found


def bit_of(axis, bit):
    return (lax.axis_index(axis) // bit) % 2


def add_low(left, right):
    return (left.astype(F32) + right.astype(F32)).astype(BF16)


def add(left, right):
    return left + right


def halves(rows, stage):
    axis, bit = stage
    half = rows.shape[0] // 2
    mine = bit_of(axis, bit)
    return (
        lax.dynamic_slice_in_dim(rows, (1 - mine) * half, half, 0),
        lax.dynamic_slice_in_dim(rows, mine * half, half, 0),
    )


def joined(rows, other, stage):
    first = bit_of(*stage) == 0
    return jnp.concatenate([jnp.where(first, rows, other), jnp.where(first, other, rows)], axis=0)


def add_split_kernel(mine_ref, left_ref, right_ref, send_ref, keep_ref):
    value = add_low(left_ref[...], right_ref[...])

    @pl.when(pl.program_id(0) == 0)
    def _():
        send_ref[...] = value

    @pl.when(pl.program_id(0) == 1)
    def _():
        keep_ref[...] = value


def add_split(left, right, stage):
    half, width = left.shape[0] // 2, left.shape[1]
    if half % 8:
        return halves(add_low(left, right), stage)
    mine = bit_of(*stage).astype(jnp.int32)[None]
    block = pl.BlockSpec((half, width), lambda i, mine: (jnp.where(i == 0, 1 - mine[0], mine[0]), 0))
    out = pl.BlockSpec((half, width), lambda i, mine: (0, 0))
    shape = jax.ShapeDtypeStruct((half, width), BF16)
    return pl.pallas_call(
        add_split_kernel,
        grid_spec=pltpu.PrefetchScalarGridSpec(
            num_scalar_prefetch=1,
            grid=(2,),
            in_specs=[block, block],
            out_specs=[out, out],
        ),
        out_shape=[shape, shape],
        cost_estimate=LIGHT,
        name="add_split",
    )(mine, left, right)


def halves_sum(left, right, stage):
    width = left.shape[2]
    parts = add_split(left.reshape(-1, width), right.reshape(-1, width), stage)
    return [part.reshape(-1, *left.shape[1:]) for part in parts]


class Sum:
    def __init__(self, keep, send, stages, plus=add_low, split=True, shared=True):
        self.keep, self.send, self.plus, self.shared = keep, send, plus, shared
        if split:
            self.steps = [("whole", stages[0])]
            self.steps += [("halve", stage) for stage in stages[1:-1]]
            self.steps += [("whole", stages[-1])]
            self.steps += [("join", stage) for stage in stages[-2:2:-1]]
            self.steps += [("both", stages[2:0:-1]), ("corner", stages[2:0:-1])]
        else:
            self.steps = [("whole", stage) for stage in stages]

    def start(self):
        kind, stage = self.steps[0]
        if kind == "both":
            return [swap(self.keep, *each) for each in stage]
        if kind == "corner":
            near, far = self.got
            if not self.shared:
                return [swap(near, *stage[1])]
            half = near.shape[0] // 2
            return [swap(near[:half], *stage[1]), swap(far[half:], *stage[0])]
        return [swap(self.send, *stage)]

    def finish(self, got):
        kind, stage = self.steps.pop(0)
        if kind == "both":
            self.got = got
        elif kind == "corner":
            near, far = self.got
            mine = joined(self.keep, near, stage[0])
            corner = jnp.concatenate(got, axis=0) if self.shared else got[0]
            other = joined(far, corner, stage[0])
            self.keep = joined(mine, other, stage[1])
        elif self.steps and self.steps[0][0] == "halve":
            self.send, self.keep = add_split(self.keep, got[0], self.steps[0][1])
        else:
            join = functools.partial(joined, stage=stage)
            self.keep = self.send = (join if kind == "join" else self.plus)(self.keep, got[0])


def advance(sums, *others):
    sums = [each for each in sums if each.steps]
    got, others = tie(([each.start() for each in sums], others))
    for each, arrived in zip(sums, got):
        each.finish(arrived)
    return others[0] if len(others) == 1 else others


def chip_stages(total):
    return [("dp", 2 << index) for index in range((total.shape[0]).bit_length() - 1)][::-1]


tie = lax.optimization_barrier


def exchange(rows):
    return lax.all_to_all(rows, "expert", split_axis=0, concat_axis=0, tiled=True)


def local(
    tokens,
    routing,
    query_weight,
    key_weight,
    value_weight,
    output_weight,
    first_gain,
    first_bias,
    second_gain,
    second_bias,
    centroids,
    expert_up,
    expert_down,
    cotangent,
):
    length, width = tokens.shape
    experts = centroids.shape[0]
    capacity = length // experts
    peers = lax.axis_size("expert")
    parts = lax.axis_size("dp")
    slots = experts * capacity
    core = (lax.axis_index("dp") % 2).astype(jnp.int32)[None]
    vectors = tie(jnp.stack([first_gain, first_bias, second_gain, second_bias]))
    first_gain, first_bias, second_gain, second_bias = (vectors[i : i + 1] for i in range(4))
    weights = (query_weight, key_weight, value_weight)

    cots, slot, wide = route(routing.reshape(1, length), cotangent, experts, capacity)
    cots, tokens = tie((cots, tokens))
    cots = exchange(cots.reshape(peers, -1, width)).reshape(slots, width)

    queries, keys, values, mixed, probs = attention(tokens, first_gain, first_bias, weights)
    resid, rows = branch(mixed, tokens, output_weight, second_gain, second_bias, slot, slots)

    rows, cots = tie((rows, cots))
    rows = exchange(rows.reshape(peers, -1, width))
    cots_down = expert_cots(cots, expert_down)
    settled = settle(
        tokens, first_gain, first_bias, mixed, resid, second_gain, second_bias, centroids, routing
    )
    rows, cots_down, *settled = tie((rows, cots_down, *settled))
    normed_turned, mixed_turned, xhat, scale, gate = settled
    rows = rows.reshape(slots, width)
    own = centroids[lax.axis_index("expert")][None, :]
    produced, returned, grad_rows, hidden, grad_pre = expert(
        rows, cots, cots_down, own, expert_up, expert_down
    )
    returned = exchange(returned.reshape(peers, -1, width))
    up_send, down_send, up_keep, down_keep = expert_weights(
        rows, grad_rows, hidden, grad_pre, parts, core
    )
    chips = chip_stages(up_send)
    up_send, up_keep = halves_sum(up_keep, swap(up_send, "dp", 1), chips[0])
    down_send, down_keep = halves_sum(down_keep, swap(down_send, "dp", 1), chips[0])
    returned, produced, up_send, up_keep, down_send, down_keep = tie(
        (returned, produced, up_send, up_keep, down_send, down_keep)
    )
    returned = returned.reshape(slots, width)
    up_got = swap(up_send, *chips[0])
    down_got = swap(down_send, *chips[0])
    produced = exchange(produced.reshape(peers, -1, width))

    pairs = width // LANES
    split = pairs // 2
    grad_resid, grad_mixed, second_sums, *units = second_back(
        core, wide, returned, xhat, scale, cotangent, second_gain, output_weight, mixed_turned,
        pairs + 3 * split,
    )

    cross = stages("expert", 1, 1 << 20)
    apart = stages("dp", 2, 1 << 20)
    back = functools.partial(
        attention_back, core, queries, keys, values, grad_mixed, mixed, normed_turned
    )
    left, send, keep = back(probs, 0, split, units)
    left, send, keep, up_got = tie((left, send, keep, up_got))
    early = Sum(keep.reshape(-1, LANES), send.reshape(-1, LANES), [("dp", 1)] + cross + apart)
    advance([early])
    early.send, *probs = tie((early.send, *probs))
    right, send, keep = back(probs, split, pairs - split, None)
    right, send, keep, produced = advance([early], right, send, keep, produced)
    produced = produced.reshape(slots, width)
    order = [("dp", 1)] + apart + cross[1:2] + cross[:1] + cross[2:]
    late = Sum(keep.reshape(-1, LANES), send.reshape(-1, LANES), order, shared=False)
    layer_out = layer_output(wide, produced, resid, gate)
    layer_out, down_got = advance([early, late], layer_out, down_got)
    grad_tokens, first_sums = first_back(left, right, tokens, grad_resid, first_gain, weights)
    grad_tokens, first_sums = advance([early, late], grad_tokens, first_sums)
    grad_up = up_keep.astype(F32) + up_got.astype(F32)
    grad_down = down_keep.astype(F32) + down_got.astype(F32)
    for stage in chips[1:]:
        grad_up, grad_down = (
            keep.astype(F32) + swap(send, *stage).astype(F32)
            for send, keep in (halves(value.astype(BF16), stage) for value in (grad_up, grad_down))
        )
    grad_up, grad_down = (value.reshape(value.shape[1:])[None] for value in (grad_up, grad_down))
    small = jnp.concatenate([first_sums, second_sums], axis=0)
    small = Sum(small, small, stages("dp", 1, 1 << 20) + cross, plus=add, split=False)
    while len(early.steps) > 2:
        advance([early, late, small])
    grad_up, grad_down = advance([early, late, small], grad_up, grad_down)
    while early.steps:
        advance([early, late, small])
    core_swap = swap(early.keep, "dp", 1)
    while len(late.steps) > 1:
        core_swap = advance([late, small], core_swap)
    outs = assemble(core, early.keep, core_swap, width, [])
    grad_output, *outs = advance([late, small], *outs)
    while small.steps:
        advance([small])
    grad_query, grad_key, grad_value = assemble(
        core, late.keep, swap(late.keep, "dp", 1), width, outs
    )
    small = small.keep
    return (
        layer_out,
        grad_tokens,
        grad_query,
        grad_key,
        grad_value,
        grad_output,
        small[0],
        small[1],
        small[2],
        small[3],
        grad_up,
        grad_down,
    )


def solution(mesh):
    rows = P(("dp", "expert"), None)
    return jax.shard_map(
        local,
        mesh=mesh,
        in_specs=(rows, rows)
        + (P(),) * 9
        + (P("expert", None, None), P("expert", None, None), rows),
        out_specs=(rows, rows) + (P(),) * 8 + (P("expert", None, "dp"), P("expert", "dp", None)),
        check_vma=False,
    )
```

```python
import functools
import math

import jax
import jax.numpy as jnp
from jax import lax
from jax.experimental import pallas as pl
from jax.experimental.pallas import tpu as pltpu
from jax.sharding import PartitionSpec as P

HEADS = 12
HEAD = 64
LANES = 128
EPS = 1e-05
F32 = jnp.float32
BF16 = jnp.bfloat16
ROWS = 256

LIGHT = pl.CostEstimate(flops=1000000, bytes_accessed=100000, transcendentals=0)


def contract(left, right, left_dim, right_dim):
    return lax.dot_general(
        left, right, (((left_dim,), (right_dim,)), ((), ())), preferred_element_type=F32
    )


def normalize(values, gain, bias):
    centered = values - jnp.mean(values, axis=-1, keepdims=True)
    variance = jnp.mean(centered * centered, axis=-1, keepdims=True)
    scale = lax.rsqrt(variance + EPS)
    xhat = centered * scale
    return xhat * gain + bias, xhat, scale


def normalize_back(grad, xhat, scale, gain):
    scaled = grad * gain
    first = jnp.mean(scaled, axis=-1, keepdims=True)
    cross = jnp.mean(scaled * xhat, axis=-1, keepdims=True)
    return scale * (scaled - first - xhat * cross)


def head_mask(parity, value):
    lane = lax.broadcasted_iota(jnp.int32, (1, LANES), 1)
    return jnp.where(lane // HEAD == parity, value, 0.0).astype(BF16)


def causal_bias(bias_ref, keys_dim):
    @pl.when((pl.program_id(0) == 0) & (pl.program_id(1) == 0))
    def _():
        key = lax.broadcasted_iota(jnp.int32, bias_ref.shape, keys_dim)
        query = lax.broadcasted_iota(jnp.int32, bias_ref.shape, 1 - keys_dim)
        bias_ref[...] = jnp.where(key <= query, 0.0, -1e30)


def attention_kernel(tokens_ref, gain_ref, shift_ref, *refs, block):
    first_weights, next_weights, (q_ref, k_ref, v_ref, o_ref) = refs[:3], refs[3:6], refs[6:10]
    *probs_refs, normed_ref, made_ref, bias_ref = refs[10:]
    causal_bias(bias_ref, 0)
    pair, parity = pl.program_id(0), pl.program_id(1)
    length = made_ref.shape[0]

    @pl.when((pair == 0) & (parity == 0))
    def _():
        weights = jnp.concatenate([weight[...] for weight in first_weights], axis=1)
        for index in range(len(probs_refs)):
            rows = slice(index * block, (index + 1) * block)
            normed, _, _ = normalize(tokens_ref[rows, :].astype(F32), gain_ref[...], shift_ref[...])
            normed = normed.astype(BF16)
            normed_ref[rows, :] = normed
            made_ref[rows, :] = contract(normed, weights, 1, 0).astype(BF16)

    @pl.when(parity == 0)
    def _():
        for index, out in enumerate((q_ref, k_ref, v_ref)):
            out[...] = made_ref[:, index * LANES : (index + 1) * LANES]

    weights = jnp.concatenate([weight[...] for weight in next_weights], axis=1)
    part = length // 2 // len(probs_refs)
    queries = q_ref[...] * head_mask(parity, HEAD**-0.5)
    values = jnp.transpose(v_ref[...] * head_mask(parity, 1.0))
    outs = []
    for index, probs_ref in enumerate(probs_refs):
        first, finish = index * block, (index + 1) * block
        scores = contract(k_ref[:finish, :], queries[first:finish], 1, 1)
        rows = pl.ds(pl.multiple_of(parity * (length // 2) + index * part, part), part)
        made_ref[rows, :] = contract(normed_ref[rows, :], weights, 1, 0).astype(BF16)
        diagonal = scores[first:] + bias_ref[...]
        if index:
            scores = jnp.concatenate([scores[:first], diagonal], axis=0)
        else:
            scores = diagonal
        shifted = jnp.exp(scores - jnp.max(scores, axis=0, keepdims=True))
        total = jnp.sum(shifted, axis=0, keepdims=True)
        probs = (shifted * (1.0 / total)).astype(BF16)
        probs_ref[0] = probs
        outs.append(jnp.transpose(contract(values[:, :finish], probs, 1, 0).astype(BF16)))
    mixed = jnp.concatenate(outs, axis=0)

    @pl.when(parity == 0)
    def _():
        o_ref[...] = mixed

    @pl.when(parity == 1)
    def _():
        o_ref[...] = o_ref[...] + mixed


def attention(tokens, gain, shift, weights):
    length, width = tokens.shape
    pairs = width // LANES
    block = min(256, length)
    finishes = range(block, length + 1, block)
    spec = pl.BlockSpec((length, LANES), lambda pair, parity: (0, pair))
    ahead = pl.BlockSpec(
        (width, LANES), lambda pair, parity: (0, jnp.minimum(pair + 1, pairs - 1))
    )
    wide = jax.ShapeDtypeStruct((length, width), BF16)
    queries, keys, values, mixed, *probs = pl.pallas_call(
        functools.partial(attention_kernel, block=block),
        grid=(pairs, 2),
        in_specs=[const(length, width), const(1, width), const(1, width)]
        + [const(width, LANES)] * 3
        + [ahead] * 3,
        out_specs=[spec] * 4
        + [
            pl.BlockSpec((1, finish, block), lambda pair, parity: (pair * 2 + parity, 0, 0))
            for finish in finishes
        ],
        out_shape=[wide] * 4
        + [jax.ShapeDtypeStruct((2 * pairs, finish, block), BF16) for finish in finishes],
        scratch_shapes=[
            pltpu.VMEM((length, width), BF16),
            pltpu.VMEM((length, 3 * LANES), BF16),
            pltpu.VMEM((block, block), F32),
        ],
        cost_estimate=LIGHT,
        name="attention",
    )(tokens, gain, shift, *weights, *weights)
    return queries, keys, values, mixed, probs


def attention_back_kernel(
    core_ref, q_ref, k_ref, v_ref, g_ref, o_ref, turned_ref, *refs, block, blocks
):
    probs_refs = refs[:blocks]
    grads_ref, send_ref, keep_ref, dk_sum, dv_sum = refs[-5:]
    parity = pl.program_id(1)
    scale_mask = head_mask(parity, HEAD**-0.5)
    queries = q_ref[...] * scale_mask
    grads = g_ref[...] * head_mask(parity, 1.0)
    keys_scaled = jnp.transpose(k_ref[...] * scale_mask)
    dk_sum[...] = jnp.zeros_like(dk_sum)
    dv_sum[...] = jnp.zeros_like(dv_sum)
    dq_parts = []
    for index, probs_ref in enumerate(probs_refs):
        first, finish = index * block, (index + 1) * block
        probs = probs_ref[0]
        some = grads[first:finish]
        dv_sum[:finish, :] += contract(probs, some, 1, 0)
        grad_probs = contract(v_ref[:finish, :], some, 1, 1)
        shares = some.astype(F32) * o_ref[first:finish, :].astype(F32)
        delta = jnp.sum(jnp.transpose(shares), axis=0, keepdims=True)
        grad_scores = (probs.astype(F32) * (grad_probs - delta)).astype(BF16)
        dk_sum[:finish, :] += contract(grad_scores, queries[first:finish], 1, 0)
        part = contract(keys_scaled[:, :finish], grad_scores, 1, 0).astype(BF16)
        dq_parts.append(jnp.transpose(part))
    parts = (
        jnp.concatenate(dq_parts, axis=0),
        dk_sum[...].astype(BF16),
        dv_sum[...].astype(BF16),
    )

    @pl.when(parity == 0)
    def _():
        for index, part in enumerate(parts):
            grads_ref[index] = part

    @pl.when(parity == 1)
    def _():
        whole = [grads_ref[index] + part for index, part in enumerate(parts)]
        for index, part in enumerate(whole):
            grads_ref[index] = part
        weight_parts(core_ref, turned_ref[...], jnp.concatenate(whole, axis=1), send_ref, keep_ref)


def weight_parts(core_ref, turned, grads, send_ref, keep_ref):
    product = contract(turned, grads, 1, 0).astype(BF16)
    rows = send_ref.shape[1]

    def write(upper, lower):
        for index in range(grads.shape[1] // LANES):
            columns = slice(index * LANES, (index + 1) * LANES)
            upper[index] = product[:rows, columns]
            lower[index] = product[rows:, columns]

    @pl.when(core_ref[0] == 0)
    def _():
        write(keep_ref, send_ref)

    @pl.when(core_ref[0] != 0)
    def _():
        write(send_ref, keep_ref)


SCALAR = pl.BlockSpec(memory_space=pltpu.SMEM)


def attention_back(core, queries, keys, values, grads, mixed, turned, probs, start, pairs, units):
    length, width = queries.shape
    block = probs[0].shape[2]
    spec = pl.BlockSpec((length, LANES), lambda pair, parity: (0, start + pair))
    whole = pl.BlockSpec((width, length), lambda pair, parity: (0, 0))
    ahead = 0 if units is None else units[0].shape[0] // 3 - pairs
    shape = jax.ShapeDtypeStruct((3 * (ahead + pairs), width // 2, LANES), BF16)
    unit = pl.BlockSpec((3, width // 2, LANES), lambda pair, parity: (ahead + pair, 0, 0))
    args = [core, queries, keys, values, grads, mixed, turned, *probs]
    alias = {}
    if units is not None:
        alias = {len(args): 1, len(args) + 1: 2}
        args += units
    return pl.pallas_call(
        functools.partial(attention_back_kernel, block=block, blocks=len(probs)),
        grid=(pairs, 2),
        in_specs=[SCALAR, spec, spec, spec, spec, spec, whole]
        + [
            pl.BlockSpec(
                (1, *part.shape[1:]), lambda pair, parity: ((start + pair) * 2 + parity, 0, 0)
            )
            for part in probs
        ]
        + [pl.BlockSpec(memory_space=pl.ANY)] * len(alias),
        out_specs=[pl.BlockSpec((3, length, LANES), lambda pair, parity: (0, 0, pair)), unit, unit],
        out_shape=[jax.ShapeDtypeStruct((3, length, pairs * LANES), BF16), shape, shape],
        input_output_aliases=alias,
        scratch_shapes=[pltpu.VMEM((length, LANES), F32)] * 2,
        cost_estimate=LIGHT,
        name="attention_back",
    )(*args)


def gelu_parts(value):
    cdf = 0.5 + 0.5 * lax.erf(value * 0.5**0.5)
    density = jnp.exp2(value * value * (-0.5 / math.log(2.0)))
    return cdf, value * (density * (1.0 / math.sqrt(2.0 * math.pi)))


def expert_cots_kernel(c_ref, down_ref, out_ref):
    out_ref[...] = contract(c_ref[...], down_ref[0], 1, 1).astype(BF16)


def expert_cots(cots, down):
    count, width = cots.shape
    hidden = down.shape[1]
    tile = min(512, hidden)
    return pl.pallas_call(
        expert_cots_kernel,
        grid=(hidden // tile,),
        in_specs=[
            pl.BlockSpec((count, width), lambda f: (0, 0)),
            pl.BlockSpec((1, tile, width), lambda f: (0, f, 0)),
        ],
        out_specs=pl.BlockSpec((count, tile), lambda f: (0, f)),
        out_shape=jax.ShapeDtypeStruct((count, hidden), BF16),
        cost_estimate=LIGHT,
        name="expert_cots",
    )(cots, down)


def expert_kernel(
    x_ref, c_ref, cd_ref, cen_ref, up_ref, down_ref,
    y_ref, gs_ref, dy_ref, h_ref, dp_ref,
    y_sum, dx_sum, gate_ref,
):
    step = pl.program_id(0)

    @pl.when(step == 0)
    def _():
        logit = jnp.sum(x_ref[...].astype(F32) * cen_ref[...], axis=1, keepdims=True)
        gate = jax.nn.sigmoid(logit)
        gate_ref[...] = jnp.broadcast_to(gate, gate_ref.shape)
        dy_ref[...] = (c_ref[...].astype(F32) * gate).astype(BF16)
        y_sum[...] = jnp.zeros_like(y_sum)
        dx_sum[...] = jnp.zeros_like(dx_sum)

    pre = contract(x_ref[...], up_ref[0], 1, 0)
    cdf, weighted = gelu_parts(pre)
    hidden = (pre * cdf).astype(BF16)
    slope = cdf + weighted
    h_ref[...] = hidden
    y_sum[...] += contract(hidden, down_ref[0], 1, 0)
    grad_hidden = cd_ref[...].astype(F32) * gate_ref[:, 0:1]
    grad_pre = (grad_hidden * slope).astype(BF16)
    dp_ref[...] = grad_pre
    dx_sum[...] += contract(grad_pre, up_ref[0], 1, 1)

    @pl.when(step == pl.num_programs(0) - 1)
    def _():
        produced = y_sum[...].astype(BF16)
        y_ref[...] = produced
        gate = gate_ref[:, 0:1]
        dot = jnp.sum(c_ref[...].astype(F32) * produced.astype(F32), axis=1, keepdims=True)
        grad_logit = dot * gate * (1.0 - gate)
        back = dx_sum[...].astype(BF16).astype(F32) + grad_logit * cen_ref[...]
        gs_ref[...] = back.astype(BF16)


def expert(rows, cots, cots_down, centroid, up, down):
    count, width = rows.shape
    hidden = up.shape[2]
    tile = min(512, hidden)
    whole = pl.BlockSpec((count, width), lambda f: (0, 0))
    wide = jax.ShapeDtypeStruct((count, width), BF16)
    deep = jax.ShapeDtypeStruct((count, hidden), BF16)
    return pl.pallas_call(
        expert_kernel,
        grid=(hidden // tile,),
        in_specs=[
            whole,
            whole,
            pl.BlockSpec((count, tile), lambda f: (0, f)),
            pl.BlockSpec((1, width), lambda f: (0, 0)),
            pl.BlockSpec((1, width, tile), lambda f: (0, 0, f)),
            pl.BlockSpec((1, tile, width), lambda f: (0, f, 0)),
        ],
        out_specs=[whole, whole, whole]
        + [pl.BlockSpec((count, tile), lambda f: (0, f))] * 2,
        out_shape=[wide, wide, wide, deep, deep],
        scratch_shapes=[
            pltpu.VMEM((count, width), F32),
            pltpu.VMEM((count, width), F32),
            pltpu.VMEM((count, LANES), F32),
        ],
        cost_estimate=LIGHT,
        name="expert",
    )(rows, cots, cots_down, centroid, up, down)


def expert_weights_kernel(
    core_ref, x_ref, dy_ref, h_ref, dp_ref,
    up_send_ref, down_send_ref, up_keep_ref, down_keep_ref, xt_ref,
):
    @pl.when(pl.program_id(0) == 0)
    def _():
        xt_ref[...] = jnp.transpose(x_ref[...])

    up = contract(xt_ref[...], dp_ref[...], 1, 0).astype(BF16)
    down = contract(h_ref[...], dy_ref[...], 0, 0).astype(BF16)
    sending = pl.program_id(0) < pl.num_programs(0) // 2

    @pl.when(sending)
    def _():
        up_send_ref[0] = up
        down_send_ref[0] = down

    @pl.when(jnp.logical_not(sending))
    def _():
        up_keep_ref[0] = up
        down_keep_ref[0] = down


def expert_weights(rows, grads, hidden_rows, grad_pre, parts, core):
    count, width = rows.shape
    hidden = hidden_rows.shape[1]
    share = hidden // parts
    tile = min(384, share)
    each = share // tile
    half = hidden // tile // 2

    def column(f, core):
        step = f % half
        other = jnp.where(f < half, 1 - core[0], core[0])
        return ((step // each) * 2 + other) * each + step % each

    def send(f):
        return jnp.minimum(f, half - 1)

    def keep(f):
        return jnp.maximum(f - half, 0)

    whole = pl.BlockSpec((count, width), lambda f, core: (0, 0))
    deep = pl.BlockSpec((count, tile), lambda f, core: (0, column(f, core)))
    up = [
        pl.BlockSpec((1, width, tile), lambda f, core, at=at: (at(f) // each, 0, at(f) % each))
        for at in (send, keep)
    ]
    down = [
        pl.BlockSpec((1, tile, width), lambda f, core, at=at: (at(f) // each, at(f) % each, 0))
        for at in (send, keep)
    ]
    up_shape = jax.ShapeDtypeStruct((parts // 2, width, share), BF16)
    down_shape = jax.ShapeDtypeStruct((parts // 2, share, width), BF16)
    return pl.pallas_call(
        expert_weights_kernel,
        grid_spec=pltpu.PrefetchScalarGridSpec(
            num_scalar_prefetch=1,
            grid=(2 * half,),
            in_specs=[whole, whole, deep, deep],
            out_specs=[up[0], down[0], up[1], down[1]],
            scratch_shapes=[pltpu.VMEM((width, count), BF16)],
        ),
        out_shape=[up_shape, down_shape, up_shape, down_shape],
        cost_estimate=LIGHT,
        name="expert_weights",
    )(core, rows, grads, hidden_rows, grad_pre)


def one_hot(condition):
    return jnp.where(condition, 1.0, 0.0).astype(BF16)


def block_rows(step, count, length, dim):
    return step * count + lax.broadcasted_iota(jnp.int32, (count, length), dim)


def const(*shape):
    return pl.BlockSpec(shape, lambda *step: (0,) * len(shape))


def route_kernel(routing_ref, cot_ref, send_ref, slot_ref, wide_ref, *, experts, capacity):
    length = routing_ref.shape[1]
    step = pl.program_id(0)

    @pl.when(step == 0)
    def _():
        chosen = routing_ref[...]
        named = lax.broadcasted_iota(jnp.int32, (experts, length), 0) == chosen
        named = jnp.where(named, 1.0, 0.0)
        lane = lax.broadcasted_iota(jnp.int32, (experts, length), 1)
        count = named
        shift = 1
        while shift < length:
            count = count + jnp.where(lane >= shift, pltpu.roll(count, shift, 1), 0.0)
            shift *= 2
        position = jnp.sum(named * (count - named), axis=0, keepdims=True)
        slot = chosen.astype(F32) * capacity + position
        slot = jnp.where(position < capacity, slot, -1.0)
        slot_ref[...] = slot.astype(jnp.int32)
        wide_ref[...] = jnp.transpose(jnp.broadcast_to(slot, (LANES, length))).astype(jnp.int32)

    place = one_hot(block_rows(step, send_ref.shape[0], length, 0) == slot_ref[...])
    send_ref[...] = contract(place, cot_ref[...], 1, 0).astype(BF16)


def route(routing, cotangent, experts, capacity):
    length, width = cotangent.shape
    slots = experts * capacity
    return pl.pallas_call(
        functools.partial(route_kernel, experts=experts, capacity=capacity),
        grid=(slots // ROWS,),
        in_specs=[const(1, length), const(length, width)],
        out_specs=[
            pl.BlockSpec((ROWS, width), lambda i: (i, 0)),
            const(1, length),
            const(length, LANES),
        ],
        out_shape=[
            jax.ShapeDtypeStruct((slots, width), BF16),
            jax.ShapeDtypeStruct((1, length), jnp.int32),
            jax.ShapeDtypeStruct((length, LANES), jnp.int32),
        ],
        cost_estimate=LIGHT,
        name="route",
    )(routing, cotangent)


def settle_kernel(
    tokens_ref, first_gain_ref, first_bias_ref, mixed_ref, resid_ref, gain_ref, bias_ref,
    cen_ref, chosen_ref,
    normed_ref, turned_ref, xhat_ref, scale_ref, gate_ref,
):
    normed, _, _ = normalize(tokens_ref[...].astype(F32), first_gain_ref[...], first_bias_ref[...])
    normed_ref[...] = jnp.transpose(normed.astype(BF16))
    turned_ref[...] = jnp.transpose(mixed_ref[...])
    second, xhat, scale = normalize(resid_ref[...], gain_ref[...], bias_ref[...])
    xhat_ref[...] = xhat.astype(BF16)
    scale_ref[...] = scale
    centroid = jnp.zeros_like(second)
    for index in range(cen_ref.shape[0]):
        centroid = jnp.where(chosen_ref[...] == index, cen_ref[index : index + 1, :], centroid)
    gate_ref[...] = jax.nn.sigmoid(jnp.sum(second * centroid, axis=1, keepdims=True))


def settle(tokens, first_gain, first_bias, mixed, resid, gain, bias, centroids, routing):
    length, width = tokens.shape
    rows = pl.BlockSpec((ROWS, width), lambda i: (i, 0))
    thin = pl.BlockSpec((ROWS, 1), lambda i: (i, 0))
    turned = pl.BlockSpec((width, ROWS), lambda i: (0, i))
    vector = const(1, width)
    column = jax.ShapeDtypeStruct((length, 1), F32)
    return pl.pallas_call(
        settle_kernel,
        grid=(length // ROWS,),
        in_specs=[rows, vector, vector, rows, rows, vector, vector, const(*centroids.shape), thin],
        out_specs=[turned, turned, rows, thin, thin],
        out_shape=[jax.ShapeDtypeStruct((width, length), BF16)] * 2
        + [jax.ShapeDtypeStruct((length, width), BF16), column, column],
        cost_estimate=LIGHT,
        name="settle",
    )(tokens, first_gain, first_bias, mixed, resid, gain, bias, centroids, routing)


def branch_kernel(
    mixed_ref, tokens_ref, weight_ref, gain_ref, bias_ref, slot_ref,
    resid_ref, send_ref, low_ref, *, blocks,
):
    step = pl.program_id(0)

    @pl.when(step < blocks)
    def _():
        resid = tokens_ref[...].astype(F32) + contract(mixed_ref[...], weight_ref[...], 1, 0)
        second, _, _ = normalize(resid, gain_ref[...], bias_ref[...])
        resid_ref[...] = resid
        low_ref[pl.ds(pl.multiple_of(step * ROWS, ROWS), ROWS), :] = second.astype(BF16)

    @pl.when(step >= blocks)
    def _():
        place = one_hot(block_rows(step - blocks, ROWS, slot_ref.shape[1], 0) == slot_ref[...])
        send_ref[...] = contract(place, low_ref[...], 1, 0).astype(BF16)


def branch(mixed, tokens, weight, gain, bias, slot, slots):
    length, width = mixed.shape
    blocks = length // ROWS

    def at(i):
        return jnp.minimum(i, blocks - 1)

    rows = pl.BlockSpec((ROWS, width), lambda i: (at(i), 0))
    return pl.pallas_call(
        functools.partial(branch_kernel, blocks=blocks),
        grid=(blocks + slots // ROWS,),
        in_specs=[
            rows,
            rows,
            const(width, width),
            const(1, width),
            const(1, width),
            const(1, length),
        ],
        out_specs=[
            rows,
            pl.BlockSpec((ROWS, width), lambda i: (jnp.maximum(i - blocks, 0), 0)),
        ],
        out_shape=[
            jax.ShapeDtypeStruct((length, width), F32),
            jax.ShapeDtypeStruct((slots, width), BF16),
        ],
        scratch_shapes=[pltpu.VMEM((length, width), BF16)],
        cost_estimate=LIGHT,
        name="branch",
    )(mixed, tokens, weight, gain, bias, slot)


def gathered(wide_ref, rows_ref):
    slots = rows_ref.shape[0]
    count = wide_ref.shape[0]
    wide = jnp.concatenate([wide_ref[...]] * (slots // LANES), axis=1)
    place = one_hot(lax.broadcasted_iota(jnp.int32, (count, slots), 1) == wide)
    return contract(place, rows_ref[...], 1, 0)


def second_back_kernel(
    core_ref, wide_ref, back_ref, xhat_ref, scale_ref, cot_ref, gain_ref, weight_ref, turned_ref,
    grad_ref, mixed_ref, sums_ref, send_ref, keep_ref, total_ref,
):
    grad = gathered(wide_ref, back_ref)
    xhat, scale = xhat_ref[...].astype(F32), scale_ref[...]
    sums = jnp.concatenate(
        [jnp.sum(grad * xhat, axis=0, keepdims=True), jnp.sum(grad, axis=0, keepdims=True)], axis=0
    )

    @pl.when(pl.program_id(0) == 0)
    def _():
        sums_ref[...] = sums

    @pl.when(pl.program_id(0) > 0)
    def _():
        sums_ref[...] = sums_ref[...] + sums

    grad = cot_ref[...].astype(F32) + normalize_back(grad, xhat, scale, gain_ref[...])
    low = grad.astype(BF16)
    grad_ref[...] = low
    mixed_ref[...] = contract(low, weight_ref[...], 1, 1).astype(BF16)
    product = contract(turned_ref[...], low, 1, 0)

    @pl.when(pl.program_id(0) == 0)
    def _():
        total_ref[...] = product

    @pl.when(pl.program_id(0) > 0)
    def _():
        total_ref[...] += product

    @pl.when(pl.program_id(0) == pl.num_programs(0) - 1)
    def _():
        rows = send_ref.shape[1]
        for index in range(send_ref.shape[0]):
            columns = slice(index * LANES, (index + 1) * LANES)
            for half, out in ((1 - core_ref[0], send_ref), (core_ref[0], keep_ref)):
                at = pl.ds(pl.multiple_of(half * rows, rows), rows)
                out[index] = total_ref[at, columns].astype(BF16)


def second_back(core, wide, back, xhat, scale, cotangent, gain, weight, turned, units):
    length, width = xhat.shape
    rows = pl.BlockSpec((ROWS, width), lambda i: (i, 0))
    own = const(width // LANES, width // 2, LANES)
    shape = jax.ShapeDtypeStruct((units, width // 2, LANES), BF16)
    return pl.pallas_call(
        second_back_kernel,
        grid=(length // ROWS,),
        in_specs=[
            SCALAR,
            pl.BlockSpec((ROWS, LANES), lambda i: (i, 0)),
            const(*back.shape),
            rows,
            pl.BlockSpec((ROWS, 1), lambda i: (i, 0)),
            rows,
            const(1, width),
            const(width, width),
            pl.BlockSpec((width, ROWS), lambda i: (0, i)),
        ],
        out_specs=[rows, rows, const(2, width), own, own],
        out_shape=[
            jax.ShapeDtypeStruct((length, width), BF16),
            jax.ShapeDtypeStruct((length, width), BF16),
            jax.ShapeDtypeStruct((2, width), F32),
            shape,
            shape,
        ],
        scratch_shapes=[pltpu.VMEM((width, width), F32)],
        cost_estimate=LIGHT,
        name="second_back",
    )(core, wide, back, xhat, scale, cotangent, gain, weight, turned)


def first_back_kernel(
    left_ref, right_ref, tokens_ref, resid_ref, gain_ref, wq_ref, wk_ref, wv_ref,
    grad_ref, sums_ref,
):
    side = left_ref.shape[2]
    grad = 0.0
    for index, weight in enumerate((wq_ref, wk_ref, wv_ref)):
        grad = grad + contract(left_ref[index], weight[:, :side], 1, 1)
        grad = grad + contract(right_ref[index], weight[:, side:], 1, 1)
    gain = gain_ref[...]
    _, xhat, scale = normalize(tokens_ref[...].astype(F32), gain, gain)
    sums = jnp.concatenate(
        [jnp.sum(grad * xhat, axis=0, keepdims=True), jnp.sum(grad, axis=0, keepdims=True)], axis=0
    )

    @pl.when(pl.program_id(0) == 0)
    def _():
        sums_ref[...] = sums

    @pl.when(pl.program_id(0) > 0)
    def _():
        sums_ref[...] = sums_ref[...] + sums

    grad_ref[...] = resid_ref[...].astype(F32) + normalize_back(grad, xhat, scale, gain)


def first_back(left, right, tokens, resid, gain, weights):
    length, width = tokens.shape
    rows = pl.BlockSpec((ROWS, width), lambda i: (i, 0))
    return pl.pallas_call(
        first_back_kernel,
        grid=(length // ROWS,),
        in_specs=[
            pl.BlockSpec((3, ROWS, part.shape[2]), lambda i: (0, i, 0)) for part in (left, right)
        ]
        + [rows, rows, const(1, width)]
        + [const(width, width)] * 3,
        out_specs=[rows, const(2, width)],
        out_shape=[
            jax.ShapeDtypeStruct((length, width), F32),
            jax.ShapeDtypeStruct((2, width), F32),
        ],
        cost_estimate=LIGHT,
        name="first_back",
    )(left, right, tokens, resid, gain, *weights)


def layer_out_kernel(wide_ref, rows_ref, resid_ref, gate_ref, out_ref):
    out_ref[...] = (resid_ref[...] + gate_ref[...] * gathered(wide_ref, rows_ref)).astype(BF16)


def layer_output(wide, produced, resid, gate):
    length, width = resid.shape
    rows = pl.BlockSpec((ROWS, width), lambda i: (i, 0))
    return pl.pallas_call(
        layer_out_kernel,
        grid=(length // ROWS,),
        in_specs=[
            pl.BlockSpec((ROWS, LANES), lambda i: (i, 0)),
            const(*produced.shape),
            rows,
            pl.BlockSpec((ROWS, 1), lambda i: (i, 0)),
        ],
        out_specs=rows,
        out_shape=jax.ShapeDtypeStruct((length, width), BF16),
        cost_estimate=LIGHT,
        name="layer_output",
    )(wide, produced, resid, gate)


def assemble_kernel(core_ref, mine_ref, other_ref, *outs, whole):
    outs = outs[-4:] if whole else outs[-3:]

    def write(parts):
        for unit in range(whole):
            outs[0][:, unit * LANES : (unit + 1) * LANES] = parts[unit].astype(F32)
        for unit in range(whole, parts.shape[0]):
            pair, matrix = divmod(unit - whole, 3)
            out = outs[matrix - 3]
            out[:, pair * LANES : (pair + 1) * LANES] = parts[unit].astype(F32)

    mine = pl.program_id(0) == core_ref[0]

    @pl.when(mine)
    def _():
        write(mine_ref)

    @pl.when(jnp.logical_not(mine))
    def _():
        write(other_ref)


def assemble(core, mine, other, width, outs):
    mine, other = (part.reshape(-1, width // 2, LANES) for part in (mine, other))
    whole = 0 if outs else width // LANES
    columns = (mine.shape[0] - whole) // 3 * LANES
    out = jax.ShapeDtypeStruct((width, width), F32)
    specs = [pl.BlockSpec((width // 2, columns), lambda i, core: (i, 1 if outs else 0))] * 3
    if whole:
        specs = [pl.BlockSpec((width // 2, width), lambda i, core: (i, 0))] + specs
    return pl.pallas_call(
        functools.partial(assemble_kernel, whole=whole),
        grid_spec=pltpu.PrefetchScalarGridSpec(
            num_scalar_prefetch=1,
            grid=(2,),
            in_specs=[const(*mine.shape)] * 2
            + [pl.BlockSpec(memory_space=pl.ANY)] * len(outs),
            out_specs=specs,
        ),
        out_shape=[out] * len(specs),
        input_output_aliases={3 + index: index for index in range(len(outs))},
        cost_estimate=LIGHT,
        name="assemble",
    )(core, mine, other, *outs)


def swap(value, axis, bit):
    size = lax.axis_size(axis)
    return lax.ppermute(value, axis, [(i, i ^ bit) for i in range(size)])


def stages(axis, low, high):
    found = []
    bit = low
    while bit < min(high, lax.axis_size(axis)):
        found.append((axis, bit))
        bit *= 2
    return found


def bit_of(axis, bit):
    return (lax.axis_index(axis) // bit) % 2


def add_low(left, right):
    return (left.astype(F32) + right.astype(F32)).astype(BF16)


def add(left, right):
    return left + right


def halves(rows, stage):
    axis, bit = stage
    half = rows.shape[0] // 2
    mine = bit_of(axis, bit)
    return (
        lax.dynamic_slice_in_dim(rows, (1 - mine) * half, half, 0),
        lax.dynamic_slice_in_dim(rows, mine * half, half, 0),
    )


def joined(rows, other, stage):
    first = bit_of(*stage) == 0
    return jnp.concatenate([jnp.where(first, rows, other), jnp.where(first, other, rows)], axis=0)


def add_split_kernel(mine_ref, left_ref, right_ref, send_ref, keep_ref):
    value = add_low(left_ref[...], right_ref[...])

    @pl.when(pl.program_id(0) == 0)
    def _():
        send_ref[...] = value

    @pl.when(pl.program_id(0) == 1)
    def _():
        keep_ref[...] = value


def add_split(left, right, stage):
    half, width = left.shape[0] // 2, left.shape[1]
    if half % 8:
        return halves(add_low(left, right), stage)
    mine = bit_of(*stage).astype(jnp.int32)[None]
    block = pl.BlockSpec((half, width), lambda i, mine: (jnp.where(i == 0, 1 - mine[0], mine[0]), 0))
    out = pl.BlockSpec((half, width), lambda i, mine: (0, 0))
    shape = jax.ShapeDtypeStruct((half, width), BF16)
    return pl.pallas_call(
        add_split_kernel,
        grid_spec=pltpu.PrefetchScalarGridSpec(
            num_scalar_prefetch=1,
            grid=(2,),
            in_specs=[block, block],
            out_specs=[out, out],
        ),
        out_shape=[shape, shape],
        cost_estimate=LIGHT,
        name="add_split",
    )(mine, left, right)


def halves_sum(left, right, stage):
    width = left.shape[2]
    parts = add_split(left.reshape(-1, width), right.reshape(-1, width), stage)
    return [part.reshape(-1, *left.shape[1:]) for part in parts]


class Sum:
    def __init__(self, keep, send, stages, plus=add_low, split=True, shared=True):
        self.keep, self.send, self.plus, self.shared = keep, send, plus, shared
        if split:
            self.steps = [("whole", stages[0])]
            self.steps += [("halve", stage) for stage in stages[1:-1]]
            self.steps += [("whole", stages[-1])]
            self.steps += [("join", stage) for stage in stages[-2:2:-1]]
            self.steps += [("both", stages[2:0:-1]), ("corner", stages[2:0:-1])]
        else:
            self.steps = [("whole", stage) for stage in stages]

    def start(self):
        kind, stage = self.steps[0]
        if kind == "both":
            return [swap(self.keep, *each) for each in stage]
        if kind == "corner":
            near, far = self.got
            if not self.shared:
                return [swap(near, *stage[1])]
            half = near.shape[0] // 2
            return [swap(near[:half], *stage[1]), swap(far[half:], *stage[0])]
        return [swap(self.send, *stage)]

    def finish(self, got):
        kind, stage = self.steps.pop(0)
        if kind == "both":
            self.got = got
        elif kind == "corner":
            near, far = self.got
            mine = joined(self.keep, near, stage[0])
            corner = jnp.concatenate(got, axis=0) if self.shared else got[0]
            other = joined(far, corner, stage[0])
            self.keep = joined(mine, other, stage[1])
        elif self.steps and self.steps[0][0] == "halve":
            self.send, self.keep = add_split(self.keep, got[0], self.steps[0][1])
        else:
            join = functools.partial(joined, stage=stage)
            self.keep = self.send = (join if kind == "join" else self.plus)(self.keep, got[0])


def advance(sums, *others):
    sums = [each for each in sums if each.steps]
    got, others = tie(([each.start() for each in sums], others))
    for each, arrived in zip(sums, got):
        each.finish(arrived)
    return others[0] if len(others) == 1 else others


def chip_stages(total):
    return [("dp", 2 << index) for index in range((total.shape[0]).bit_length() - 1)][::-1]


tie = lax.optimization_barrier


def exchange(rows):
    return lax.all_to_all(rows, "expert", split_axis=0, concat_axis=0, tiled=True)


def local(
    tokens,
    routing,
    query_weight,
    key_weight,
    value_weight,
    output_weight,
    first_gain,
    first_bias,
    second_gain,
    second_bias,
    centroids,
    expert_up,
    expert_down,
    cotangent,
):
    length, width = tokens.shape
    experts = centroids.shape[0]
    capacity = length // experts
    peers = lax.axis_size("expert")
    parts = lax.axis_size("dp")
    slots = experts * capacity
    core = (lax.axis_index("dp") % 2).astype(jnp.int32)[None]
    vectors = tie(jnp.stack([first_gain, first_bias, second_gain, second_bias]))
    first_gain, first_bias, second_gain, second_bias = (vectors[i : i + 1] for i in range(4))
    weights = (query_weight, key_weight, value_weight)

    cots, slot, wide = route(routing.reshape(1, length), cotangent, experts, capacity)
    cots, tokens = tie((cots, tokens))
    cots = exchange(cots.reshape(peers, -1, width)).reshape(slots, width)

    queries, keys, values, mixed, probs = attention(tokens, first_gain, first_bias, weights)
    resid, rows = branch(mixed, tokens, output_weight, second_gain, second_bias, slot, slots)

    rows, cots = tie((rows, cots))
    rows = exchange(rows.reshape(peers, -1, width))
    cots_down = expert_cots(cots, expert_down)
    settled = settle(
        tokens, first_gain, first_bias, mixed, resid, second_gain, second_bias, centroids, routing
    )
    rows, cots_down, *settled = tie((rows, cots_down, *settled))
    normed_turned, mixed_turned, xhat, scale, gate = settled
    rows = rows.reshape(slots, width)
    own = centroids[lax.axis_index("expert")][None, :]
    produced, returned, grad_rows, hidden, grad_pre = expert(
        rows, cots, cots_down, own, expert_up, expert_down
    )
    returned = exchange(returned.reshape(peers, -1, width))
    up_send, down_send, up_keep, down_keep = expert_weights(
        rows, grad_rows, hidden, grad_pre, parts, core
    )
    chips = chip_stages(up_send)
    up_send, up_keep = halves_sum(up_keep, swap(up_send, "dp", 1), chips[0])
    down_send, down_keep = halves_sum(down_keep, swap(down_send, "dp", 1), chips[0])
    returned, produced, up_send, up_keep, down_send, down_keep = tie(
        (returned, produced, up_send, up_keep, down_send, down_keep)
    )
    returned = returned.reshape(slots, width)
    up_got = swap(up_send, *chips[0])
    down_got = swap(down_send, *chips[0])
    produced = exchange(produced.reshape(peers, -1, width))

    pairs = width // LANES
    split = pairs // 2
    grad_resid, grad_mixed, second_sums, *units = second_back(
        core, wide, returned, xhat, scale, cotangent, second_gain, output_weight, mixed_turned,
        pairs + 3 * split,
    )

    cross = stages("expert", 1, 1 << 20)
    apart = stages("dp", 2, 1 << 20)
    back = functools.partial(
        attention_back, core, queries, keys, values, grad_mixed, mixed, normed_turned
    )
    left, send, keep = back(probs, 0, split, units)
    left, send, keep, up_got = tie((left, send, keep, up_got))
    early = Sum(keep.reshape(-1, LANES), send.reshape(-1, LANES), [("dp", 1)] + cross + apart)
    advance([early])
    early.send, *probs = tie((early.send, *probs))
    right, send, keep = back(probs, split, pairs - split, None)
    right, send, keep, produced = advance([early], right, send, keep, produced)
    produced = produced.reshape(slots, width)
    order = [("dp", 1)] + apart + cross[1:2] + cross[:1] + cross[2:]
    late = Sum(keep.reshape(-1, LANES), send.reshape(-1, LANES), order, shared=False)
    layer_out = layer_output(wide, produced, resid, gate)
    layer_out, down_got = advance([early, late], layer_out, down_got)
    grad_tokens, first_sums = first_back(left, right, tokens, grad_resid, first_gain, weights)
    grad_tokens, first_sums = advance([early, late], grad_tokens, first_sums)
    grad_up = up_keep.astype(F32) + up_got.astype(F32)
    grad_down = down_keep.astype(F32) + down_got.astype(F32)
    for stage in chips[1:]:
        grad_up, grad_down = (
            keep.astype(F32) + swap(send, *stage).astype(F32)
            for send, keep in (halves(value.astype(BF16), stage) for value in (grad_up, grad_down))
        )
    grad_up, grad_down = (value.reshape(value.shape[1:])[None] for value in (grad_up, grad_down))
    small = jnp.concatenate([first_sums, second_sums], axis=0)
    small = Sum(small, small, stages("dp", 1, 1 << 20) + cross, plus=add, split=False)
    while len(early.steps) > 2:
        advance([early, late, small])
    grad_up, grad_down = advance([early, late, small], grad_up, grad_down)
    while early.steps:
        advance([early, late, small])
    core_swap = swap(early.keep, "dp", 1)
    while len(late.steps) > 1:
        core_swap = advance([late, small], core_swap)
    outs = assemble(core, early.keep, core_swap, width, [])
    grad_output, *outs = advance([late, small], *outs)
    while small.steps:
        advance([small])
    grad_query, grad_key, grad_value = assemble(
        core, late.keep, swap(late.keep, "dp", 1), width, outs
    )
    small = small.keep
    return (
        layer_out,
        grad_tokens,
        grad_query,
        grad_key,
        grad_value,
        grad_output,
        small[0],
        small[1],
        small[2],
        small[3],
        grad_up,
        grad_down,
    )


def solution(mesh):
    rows = P(("dp", "expert"), None)
    return jax.shard_map(
        local,
        mesh=mesh,
        in_specs=(rows, rows)
        + (P(),) * 9
        + (P("expert", None, None), P("expert", None, None), rows),
        out_specs=(rows, rows) + (P(),) * 8 + (P("expert", None, "dp"), P("expert", "dp", None)),
        check_vma=False,
    )
```

```python
import functools
import math

import jax
import jax.numpy as jnp
from jax import lax
from jax.experimental import pallas as pl
from jax.experimental.pallas import tpu as pltpu
from jax.sharding import PartitionSpec as P

HEADS = 12
HEAD = 64
LANES = 128
EPS = 1e-05
F32 = jnp.float32
BF16 = jnp.bfloat16
ROWS = 256

LIGHT = pl.CostEstimate(flops=1000000, bytes_accessed=100000, transcendentals=0)


def contract(left, right, left_dim, right_dim):
    return lax.dot_general(
        left, right, (((left_dim,), (right_dim,)), ((), ())), preferred_element_type=F32
    )


def normalize(values, gain, bias):
    centered = values - jnp.mean(values, axis=-1, keepdims=True)
    variance = jnp.mean(centered * centered, axis=-1, keepdims=True)
    scale = lax.rsqrt(variance + EPS)
    xhat = centered * scale
    return xhat * gain + bias, xhat, scale


def normalize_back(grad, xhat, scale, gain):
    scaled = grad * gain
    first = jnp.mean(scaled, axis=-1, keepdims=True)
    cross = jnp.mean(scaled * xhat, axis=-1, keepdims=True)
    return scale * (scaled - first - xhat * cross)


def head_mask(parity, value):
    lane = lax.broadcasted_iota(jnp.int32, (1, LANES), 1)
    return jnp.where(lane // HEAD == parity, value, 0.0).astype(BF16)


def causal_bias(bias_ref, keys_dim):
    @pl.when((pl.program_id(0) == 0) & (pl.program_id(1) == 0))
    def _():
        key = lax.broadcasted_iota(jnp.int32, bias_ref.shape, keys_dim)
        query = lax.broadcasted_iota(jnp.int32, bias_ref.shape, 1 - keys_dim)
        bias_ref[...] = jnp.where(key <= query, 0.0, -1e30)


def attention_kernel(tokens_ref, gain_ref, shift_ref, *refs, block):
    first_weights, next_weights, (q_ref, k_ref, v_ref, o_ref) = refs[:3], refs[3:6], refs[6:10]
    *probs_refs, normed_ref, made_ref, bias_ref = refs[10:]
    causal_bias(bias_ref, 0)
    pair, parity = pl.program_id(0), pl.program_id(1)
    length = made_ref.shape[0]

    @pl.when((pair == 0) & (parity == 0))
    def _():
        weights = jnp.concatenate([weight[...] for weight in first_weights], axis=1)
        for index in range(len(probs_refs)):
            rows = slice(index * block, (index + 1) * block)
            normed, _, _ = normalize(tokens_ref[rows, :].astype(F32), gain_ref[...], shift_ref[...])
            normed = normed.astype(BF16)
            normed_ref[rows, :] = normed
            made_ref[rows, :] = contract(normed, weights, 1, 0).astype(BF16)

    @pl.when(parity == 0)
    def _():
        for index, out in enumerate((q_ref, k_ref, v_ref)):
            out[...] = made_ref[:, index * LANES : (index + 1) * LANES]

    weights = jnp.concatenate([weight[...] for weight in next_weights], axis=1)
    part = length // 2 // len(probs_refs)
    queries = q_ref[...] * head_mask(parity, HEAD**-0.5)
    values = jnp.transpose(v_ref[...] * head_mask(parity, 1.0))
    outs = []

    def product(index):
        finish = (index + 1) * block
        return contract(k_ref[:finish, :], queries[index * block : finish], 1, 1)

    ready = product(0)
    for index, probs_ref in enumerate(probs_refs):
        first, finish = index * block, (index + 1) * block
        scores = ready
        if index + 1 < len(probs_refs):
            ready = product(index + 1)
        rows = pl.ds(pl.multiple_of(parity * (length // 2) + index * part, part), part)
        made_ref[rows, :] = contract(normed_ref[rows, :], weights, 1, 0).astype(BF16)
        diagonal = scores[first:] + bias_ref[...]
        if index:
            scores = jnp.concatenate([scores[:first], diagonal], axis=0)
        else:
            scores = diagonal
        shifted = jnp.exp(scores - jnp.max(scores, axis=0, keepdims=True))
        total = jnp.sum(shifted, axis=0, keepdims=True)
        probs = (shifted * (1.0 / total)).astype(BF16)
        probs_ref[0] = probs
        outs.append(jnp.transpose(contract(values[:, :finish], probs, 1, 0).astype(BF16)))
    mixed = jnp.concatenate(outs, axis=0)

    @pl.when(parity == 0)
    def _():
        o_ref[...] = mixed

    @pl.when(parity == 1)
    def _():
        o_ref[...] = o_ref[...] + mixed


def attention(tokens, gain, shift, weights):
    length, width = tokens.shape
    pairs = width // LANES
    block = min(256, length)
    finishes = range(block, length + 1, block)
    spec = pl.BlockSpec((length, LANES), lambda pair, parity: (0, pair))
    ahead = pl.BlockSpec(
        (width, LANES), lambda pair, parity: (0, jnp.minimum(pair + 1, pairs - 1))
    )
    wide = jax.ShapeDtypeStruct((length, width), BF16)
    queries, keys, values, mixed, *probs = pl.pallas_call(
        functools.partial(attention_kernel, block=block),
        grid=(pairs, 2),
        in_specs=[const(length, width), const(1, width), const(1, width)]
        + [const(width, LANES)] * 3
        + [ahead] * 3,
        out_specs=[spec] * 4
        + [
            pl.BlockSpec((1, finish, block), lambda pair, parity: (pair * 2 + parity, 0, 0))
            for finish in finishes
        ],
        out_shape=[wide] * 4
        + [jax.ShapeDtypeStruct((2 * pairs, finish, block), BF16) for finish in finishes],
        scratch_shapes=[
            pltpu.VMEM((length, width), BF16),
            pltpu.VMEM((length, 3 * LANES), BF16),
            pltpu.VMEM((block, block), F32),
        ],
        cost_estimate=LIGHT,
        name="attention",
    )(tokens, gain, shift, *weights, *weights)
    return queries, keys, values, mixed, probs


def attention_back_kernel(
    core_ref, q_ref, k_ref, v_ref, g_ref, o_ref, turned_ref, *refs, block, blocks
):
    probs_refs = refs[:blocks]
    grads_ref, send_ref, keep_ref, dk_sum, dv_sum = refs[-5:]
    parity = pl.program_id(1)
    scale_mask = head_mask(parity, HEAD**-0.5)
    queries = q_ref[...] * scale_mask
    grads = g_ref[...] * head_mask(parity, 1.0)
    keys_scaled = jnp.transpose(k_ref[...] * scale_mask)
    dk_sum[...] = jnp.zeros_like(dk_sum)
    dv_sum[...] = jnp.zeros_like(dv_sum)
    dq_parts = []

    def product(index):
        finish = (index + 1) * block
        return contract(v_ref[:finish, :], grads[index * block : finish], 1, 1)

    ready = product(0)
    for index, probs_ref in enumerate(probs_refs):
        first, finish = index * block, (index + 1) * block
        probs = probs_ref[0]
        some = grads[first:finish]
        dv_sum[:finish, :] += contract(probs, some, 1, 0)
        grad_probs = ready
        if index + 1 < len(probs_refs):
            ready = product(index + 1)
        shares = some.astype(F32) * o_ref[first:finish, :].astype(F32)
        delta = jnp.sum(jnp.transpose(shares), axis=0, keepdims=True)
        grad_scores = (probs.astype(F32) * (grad_probs - delta)).astype(BF16)
        dk_sum[:finish, :] += contract(grad_scores, queries[first:finish], 1, 0)
        part = contract(keys_scaled[:, :finish], grad_scores, 1, 0).astype(BF16)
        dq_parts.append(jnp.transpose(part))
    parts = (
        jnp.concatenate(dq_parts, axis=0),
        dk_sum[...].astype(BF16),
        dv_sum[...].astype(BF16),
    )

    @pl.when(parity == 0)
    def _():
        for index, part in enumerate(parts):
            grads_ref[index] = part

    @pl.when(parity == 1)
    def _():
        whole = [grads_ref[index] + part for index, part in enumerate(parts)]
        for index, part in enumerate(whole):
            grads_ref[index] = part
        weight_parts(core_ref, turned_ref[...], jnp.concatenate(whole, axis=1), send_ref, keep_ref)


def weight_parts(core_ref, turned, grads, send_ref, keep_ref):
    product = contract(turned, grads, 1, 0).astype(BF16)
    rows = send_ref.shape[1]

    def write(upper, lower):
        for index in range(grads.shape[1] // LANES):
            columns = slice(index * LANES, (index + 1) * LANES)
            upper[index] = product[:rows, columns]
            lower[index] = product[rows:, columns]

    @pl.when(core_ref[0] == 0)
    def _():
        write(keep_ref, send_ref)

    @pl.when(core_ref[0] != 0)
    def _():
        write(send_ref, keep_ref)


SCALAR = pl.BlockSpec(memory_space=pltpu.SMEM)


def attention_back(core, queries, keys, values, grads, mixed, turned, probs, start, pairs, units):
    length, width = queries.shape
    block = probs[0].shape[2]
    spec = pl.BlockSpec((length, LANES), lambda pair, parity: (0, start + pair))
    whole = pl.BlockSpec((width, length), lambda pair, parity: (0, 0))
    ahead = 0 if units is None else units[0].shape[0] // 3 - pairs
    shape = jax.ShapeDtypeStruct((3 * (ahead + pairs), width // 2, LANES), BF16)
    unit = pl.BlockSpec((3, width // 2, LANES), lambda pair, parity: (ahead + pair, 0, 0))
    args = [core, queries, keys, values, grads, mixed, turned, *probs]
    alias = {}
    if units is not None:
        alias = {len(args): 1, len(args) + 1: 2}
        args += units
    return pl.pallas_call(
        functools.partial(attention_back_kernel, block=block, blocks=len(probs)),
        grid=(pairs, 2),
        in_specs=[SCALAR, spec, spec, spec, spec, spec, whole]
        + [
            pl.BlockSpec(
                (1, *part.shape[1:]), lambda pair, parity: ((start + pair) * 2 + parity, 0, 0)
            )
            for part in probs
        ]
        + [pl.BlockSpec(memory_space=pl.ANY)] * len(alias),
        out_specs=[pl.BlockSpec((3, length, LANES), lambda pair, parity: (0, 0, pair)), unit, unit],
        out_shape=[jax.ShapeDtypeStruct((3, length, pairs * LANES), BF16), shape, shape],
        input_output_aliases=alias,
        scratch_shapes=[pltpu.VMEM((length, LANES), F32)] * 2,
        cost_estimate=LIGHT,
        name="attention_back",
    )(*args)


def gelu_parts(value):
    cdf = 0.5 + 0.5 * lax.erf(value * 0.5**0.5)
    density = jnp.exp2(value * value * (-0.5 / math.log(2.0)))
    return cdf, value * (density * (1.0 / math.sqrt(2.0 * math.pi)))


def expert_cots_kernel(c_ref, down_ref, out_ref):
    out_ref[...] = contract(c_ref[...], down_ref[0], 1, 1).astype(BF16)


def expert_cots(cots, down):
    count, width = cots.shape
    hidden = down.shape[1]
    tile = min(512, hidden)
    return pl.pallas_call(
        expert_cots_kernel,
        grid=(hidden // tile,),
        in_specs=[
            pl.BlockSpec((count, width), lambda f: (0, 0)),
            pl.BlockSpec((1, tile, width), lambda f: (0, f, 0)),
        ],
        out_specs=pl.BlockSpec((count, tile), lambda f: (0, f)),
        out_shape=jax.ShapeDtypeStruct((count, hidden), BF16),
        cost_estimate=LIGHT,
        name="expert_cots",
    )(cots, down)


def expert_kernel(
    x_ref, c_ref, cd_ref, cen_ref, up_ref, down_ref,
    y_ref, gs_ref, dy_ref, h_ref, dp_ref,
    y_sum, dx_sum, gate_ref,
):
    step = pl.program_id(0)

    @pl.when(step == 0)
    def _():
        logit = jnp.sum(x_ref[...].astype(F32) * cen_ref[...], axis=1, keepdims=True)
        gate = jax.nn.sigmoid(logit)
        gate_ref[...] = jnp.broadcast_to(gate, gate_ref.shape)
        dy_ref[...] = (c_ref[...].astype(F32) * gate).astype(BF16)
        y_sum[...] = jnp.zeros_like(y_sum)
        dx_sum[...] = jnp.zeros_like(dx_sum)

    pre = contract(x_ref[...], up_ref[0], 1, 0)
    cdf, weighted = gelu_parts(pre)
    hidden = (pre * cdf).astype(BF16)
    slope = cdf + weighted
    h_ref[...] = hidden
    y_sum[...] += contract(hidden, down_ref[0], 1, 0)
    grad_hidden = cd_ref[...].astype(F32) * gate_ref[:, 0:1]
    grad_pre = (grad_hidden * slope).astype(BF16)
    dp_ref[...] = grad_pre
    dx_sum[...] += contract(grad_pre, up_ref[0], 1, 1)

    @pl.when(step == pl.num_programs(0) - 1)
    def _():
        produced = y_sum[...].astype(BF16)
        y_ref[...] = produced
        gate = gate_ref[:, 0:1]
        dot = jnp.sum(c_ref[...].astype(F32) * produced.astype(F32), axis=1, keepdims=True)
        grad_logit = dot * gate * (1.0 - gate)
        back = dx_sum[...].astype(BF16).astype(F32) + grad_logit * cen_ref[...]
        gs_ref[...] = back.astype(BF16)


def expert(rows, cots, cots_down, centroid, up, down):
    count, width = rows.shape
    hidden = up.shape[2]
    tile = min(512, hidden)
    whole = pl.BlockSpec((count, width), lambda f: (0, 0))
    wide = jax.ShapeDtypeStruct((count, width), BF16)
    deep = jax.ShapeDtypeStruct((count, hidden), BF16)
    return pl.pallas_call(
        expert_kernel,
        grid=(hidden // tile,),
        in_specs=[
            whole,
            whole,
            pl.BlockSpec((count, tile), lambda f: (0, f)),
            pl.BlockSpec((1, width), lambda f: (0, 0)),
            pl.BlockSpec((1, width, tile), lambda f: (0, 0, f)),
            pl.BlockSpec((1, tile, width), lambda f: (0, f, 0)),
        ],
        out_specs=[whole, whole, whole]
        + [pl.BlockSpec((count, tile), lambda f: (0, f))] * 2,
        out_shape=[wide, wide, wide, deep, deep],
        scratch_shapes=[
            pltpu.VMEM((count, width), F32),
            pltpu.VMEM((count, width), F32),
            pltpu.VMEM((count, LANES), F32),
        ],
        cost_estimate=LIGHT,
        name="expert",
    )(rows, cots, cots_down, centroid, up, down)


def expert_weights_kernel(
    core_ref, x_ref, dy_ref, h_ref, dp_ref,
    up_send_ref, down_send_ref, up_keep_ref, down_keep_ref, xt_ref,
):
    @pl.when(pl.program_id(0) == 0)
    def _():
        xt_ref[...] = jnp.transpose(x_ref[...])

    up = contract(xt_ref[...], dp_ref[...], 1, 0).astype(BF16)
    down = contract(h_ref[...], dy_ref[...], 0, 0).astype(BF16)
    sending = pl.program_id(0) < pl.num_programs(0) // 2

    @pl.when(sending)
    def _():
        up_send_ref[0] = up
        down_send_ref[0] = down

    @pl.when(jnp.logical_not(sending))
    def _():
        up_keep_ref[0] = up
        down_keep_ref[0] = down


def expert_weights(rows, grads, hidden_rows, grad_pre, parts, core):
    count, width = rows.shape
    hidden = hidden_rows.shape[1]
    share = hidden // parts
    tile = min(384, share)
    each = share // tile
    half = hidden // tile // 2

    def column(f, core):
        step = f % half
        other = jnp.where(f < half, 1 - core[0], core[0])
        return ((step // each) * 2 + other) * each + step % each

    def send(f):
        return jnp.minimum(f, half - 1)

    def keep(f):
        return jnp.maximum(f - half, 0)

    whole = pl.BlockSpec((count, width), lambda f, core: (0, 0))
    deep = pl.BlockSpec((count, tile), lambda f, core: (0, column(f, core)))
    up = [
        pl.BlockSpec((1, width, tile), lambda f, core, at=at: (at(f) // each, 0, at(f) % each))
        for at in (send, keep)
    ]
    down = [
        pl.BlockSpec((1, tile, width), lambda f, core, at=at: (at(f) // each, at(f) % each, 0))
        for at in (send, keep)
    ]
    up_shape = jax.ShapeDtypeStruct((parts // 2, width, share), BF16)
    down_shape = jax.ShapeDtypeStruct((parts // 2, share, width), BF16)
    return pl.pallas_call(
        expert_weights_kernel,
        grid_spec=pltpu.PrefetchScalarGridSpec(
            num_scalar_prefetch=1,
            grid=(2 * half,),
            in_specs=[whole, whole, deep, deep],
            out_specs=[up[0], down[0], up[1], down[1]],
            scratch_shapes=[pltpu.VMEM((width, count), BF16)],
        ),
        out_shape=[up_shape, down_shape, up_shape, down_shape],
        cost_estimate=LIGHT,
        name="expert_weights",
    )(core, rows, grads, hidden_rows, grad_pre)


def one_hot(condition):
    return jnp.where(condition, 1.0, 0.0).astype(BF16)


def block_rows(step, count, length, dim):
    return step * count + lax.broadcasted_iota(jnp.int32, (count, length), dim)


def const(*shape):
    return pl.BlockSpec(shape, lambda *step: (0,) * len(shape))


def route_kernel(routing_ref, cot_ref, send_ref, slot_ref, wide_ref, *, experts, capacity):
    length = routing_ref.shape[1]
    step = pl.program_id(0)

    @pl.when(step == 0)
    def _():
        chosen = routing_ref[...]
        named = lax.broadcasted_iota(jnp.int32, (experts, length), 0) == chosen
        named = jnp.where(named, 1.0, 0.0)
        lane = lax.broadcasted_iota(jnp.int32, (experts, length), 1)
        count = named
        shift = 1
        while shift < length:
            count = count + jnp.where(lane >= shift, pltpu.roll(count, shift, 1), 0.0)
            shift *= 2
        position = jnp.sum(named * (count - named), axis=0, keepdims=True)
        slot = chosen.astype(F32) * capacity + position
        slot = jnp.where(position < capacity, slot, -1.0)
        slot_ref[...] = slot.astype(jnp.int32)
        wide_ref[...] = jnp.transpose(jnp.broadcast_to(slot, (LANES, length))).astype(jnp.int32)

    place = one_hot(block_rows(step, send_ref.shape[0], length, 0) == slot_ref[...])
    send_ref[...] = contract(place, cot_ref[...], 1, 0).astype(BF16)


def route(routing, cotangent, experts, capacity):
    length, width = cotangent.shape
    slots = experts * capacity
    return pl.pallas_call(
        functools.partial(route_kernel, experts=experts, capacity=capacity),
        grid=(slots // ROWS,),
        in_specs=[const(1, length), const(length, width)],
        out_specs=[
            pl.BlockSpec((ROWS, width), lambda i: (i, 0)),
            const(1, length),
            const(length, LANES),
        ],
        out_shape=[
            jax.ShapeDtypeStruct((slots, width), BF16),
            jax.ShapeDtypeStruct((1, length), jnp.int32),
            jax.ShapeDtypeStruct((length, LANES), jnp.int32),
        ],
        cost_estimate=LIGHT,
        name="route",
    )(routing, cotangent)


def settle_kernel(
    tokens_ref, first_gain_ref, first_bias_ref, mixed_ref, resid_ref, gain_ref, bias_ref,
    cen_ref, chosen_ref,
    normed_ref, turned_ref, xhat_ref, scale_ref, gate_ref,
):
    normed, _, _ = normalize(tokens_ref[...].astype(F32), first_gain_ref[...], first_bias_ref[...])
    normed_ref[...] = jnp.transpose(normed.astype(BF16))
    turned_ref[...] = jnp.transpose(mixed_ref[...])
    second, xhat, scale = normalize(resid_ref[...], gain_ref[...], bias_ref[...])
    xhat_ref[...] = xhat.astype(BF16)
    scale_ref[...] = scale
    centroid = jnp.zeros_like(second)
    for index in range(cen_ref.shape[0]):
        centroid = jnp.where(chosen_ref[...] == index, cen_ref[index : index + 1, :], centroid)
    gate_ref[...] = jax.nn.sigmoid(jnp.sum(second * centroid, axis=1, keepdims=True))


def settle(tokens, first_gain, first_bias, mixed, resid, gain, bias, centroids, routing):
    length, width = tokens.shape
    rows = pl.BlockSpec((ROWS, width), lambda i: (i, 0))
    thin = pl.BlockSpec((ROWS, 1), lambda i: (i, 0))
    turned = pl.BlockSpec((width, ROWS), lambda i: (0, i))
    vector = const(1, width)
    column = jax.ShapeDtypeStruct((length, 1), F32)
    return pl.pallas_call(
        settle_kernel,
        grid=(length // ROWS,),
        in_specs=[rows, vector, vector, rows, rows, vector, vector, const(*centroids.shape), thin],
        out_specs=[turned, turned, rows, thin, thin],
        out_shape=[jax.ShapeDtypeStruct((width, length), BF16)] * 2
        + [jax.ShapeDtypeStruct((length, width), BF16), column, column],
        cost_estimate=LIGHT,
        name="settle",
    )(tokens, first_gain, first_bias, mixed, resid, gain, bias, centroids, routing)


def branch_kernel(
    mixed_ref, tokens_ref, weight_ref, gain_ref, bias_ref, slot_ref,
    resid_ref, send_ref, low_ref, *, blocks,
):
    step = pl.program_id(0)

    @pl.when(step < blocks)
    def _():
        resid = tokens_ref[...].astype(F32) + contract(mixed_ref[...], weight_ref[...], 1, 0)
        second, _, _ = normalize(resid, gain_ref[...], bias_ref[...])
        resid_ref[...] = resid
        low_ref[pl.ds(pl.multiple_of(step * ROWS, ROWS), ROWS), :] = second.astype(BF16)

    @pl.when(step >= blocks)
    def _():
        place = one_hot(block_rows(step - blocks, ROWS, slot_ref.shape[1], 0) == slot_ref[...])
        send_ref[...] = contract(place, low_ref[...], 1, 0).astype(BF16)


def branch(mixed, tokens, weight, gain, bias, slot, slots):
    length, width = mixed.shape
    blocks = length // ROWS

    def at(i):
        return jnp.minimum(i, blocks - 1)

    rows = pl.BlockSpec((ROWS, width), lambda i: (at(i), 0))
    return pl.pallas_call(
        functools.partial(branch_kernel, blocks=blocks),
        grid=(blocks + slots // ROWS,),
        in_specs=[
            rows,
            rows,
            const(width, width),
            const(1, width),
            const(1, width),
            const(1, length),
        ],
        out_specs=[
            rows,
            pl.BlockSpec((ROWS, width), lambda i: (jnp.maximum(i - blocks, 0), 0)),
        ],
        out_shape=[
            jax.ShapeDtypeStruct((length, width), F32),
            jax.ShapeDtypeStruct((slots, width), BF16),
        ],
        scratch_shapes=[pltpu.VMEM((length, width), BF16)],
        cost_estimate=LIGHT,
        name="branch",
    )(mixed, tokens, weight, gain, bias, slot)


def gathered(wide_ref, rows_ref):
    slots = rows_ref.shape[0]
    count = wide_ref.shape[0]
    wide = jnp.concatenate([wide_ref[...]] * (slots // LANES), axis=1)
    place = one_hot(lax.broadcasted_iota(jnp.int32, (count, slots), 1) == wide)
    return contract(place, rows_ref[...], 1, 0)


def second_back_kernel(
    core_ref, wide_ref, back_ref, xhat_ref, scale_ref, cot_ref, gain_ref, weight_ref, turned_ref,
    grad_ref, mixed_ref, sums_ref, send_ref, keep_ref, total_ref,
):
    grad = gathered(wide_ref, back_ref)
    xhat, scale = xhat_ref[...].astype(F32), scale_ref[...]
    sums = jnp.concatenate(
        [jnp.sum(grad * xhat, axis=0, keepdims=True), jnp.sum(grad, axis=0, keepdims=True)], axis=0
    )

    @pl.when(pl.program_id(0) == 0)
    def _():
        sums_ref[...] = sums

    @pl.when(pl.program_id(0) > 0)
    def _():
        sums_ref[...] = sums_ref[...] + sums

    grad = cot_ref[...].astype(F32) + normalize_back(grad, xhat, scale, gain_ref[...])
    low = grad.astype(BF16)
    grad_ref[...] = low
    mixed_ref[...] = contract(low, weight_ref[...], 1, 1).astype(BF16)
    product = contract(turned_ref[...], low, 1, 0)

    @pl.when(pl.program_id(0) == 0)
    def _():
        total_ref[...] = product

    @pl.when(pl.program_id(0) > 0)
    def _():
        total_ref[...] += product

    @pl.when(pl.program_id(0) == pl.num_programs(0) - 1)
    def _():
        rows = send_ref.shape[1]
        for index in range(send_ref.shape[0]):
            columns = slice(index * LANES, (index + 1) * LANES)
            for half, out in ((1 - core_ref[0], send_ref), (core_ref[0], keep_ref)):
                at = pl.ds(pl.multiple_of(half * rows, rows), rows)
                out[index] = total_ref[at, columns].astype(BF16)


def second_back(core, wide, back, xhat, scale, cotangent, gain, weight, turned, units):
    length, width = xhat.shape
    rows = pl.BlockSpec((ROWS, width), lambda i: (i, 0))
    own = const(width // LANES, width // 2, LANES)
    shape = jax.ShapeDtypeStruct((units, width // 2, LANES), BF16)
    return pl.pallas_call(
        second_back_kernel,
        grid=(length // ROWS,),
        in_specs=[
            SCALAR,
            pl.BlockSpec((ROWS, LANES), lambda i: (i, 0)),
            const(*back.shape),
            rows,
            pl.BlockSpec((ROWS, 1), lambda i: (i, 0)),
            rows,
            const(1, width),
            const(width, width),
            pl.BlockSpec((width, ROWS), lambda i: (0, i)),
        ],
        out_specs=[rows, rows, const(2, width), own, own],
        out_shape=[
            jax.ShapeDtypeStruct((length, width), BF16),
            jax.ShapeDtypeStruct((length, width), BF16),
            jax.ShapeDtypeStruct((2, width), F32),
            shape,
            shape,
        ],
        scratch_shapes=[pltpu.VMEM((width, width), F32)],
        cost_estimate=LIGHT,
        name="second_back",
    )(core, wide, back, xhat, scale, cotangent, gain, weight, turned)


def first_back_kernel(
    left_ref, right_ref, tokens_ref, resid_ref, gain_ref, wq_ref, wk_ref, wv_ref,
    grad_ref, sums_ref,
):
    side = left_ref.shape[2]
    grad = 0.0
    for index, weight in enumerate((wq_ref, wk_ref, wv_ref)):
        grad = grad + contract(left_ref[index], weight[:, :side], 1, 1)
        grad = grad + contract(right_ref[index], weight[:, side:], 1, 1)
    gain = gain_ref[...]
    _, xhat, scale = normalize(tokens_ref[...].astype(F32), gain, gain)
    sums = jnp.concatenate(
        [jnp.sum(grad * xhat, axis=0, keepdims=True), jnp.sum(grad, axis=0, keepdims=True)], axis=0
    )

    @pl.when(pl.program_id(0) == 0)
    def _():
        sums_ref[...] = sums

    @pl.when(pl.program_id(0) > 0)
    def _():
        sums_ref[...] = sums_ref[...] + sums

    grad_ref[...] = resid_ref[...].astype(F32) + normalize_back(grad, xhat, scale, gain)


def first_back(left, right, tokens, resid, gain, weights):
    length, width = tokens.shape
    rows = pl.BlockSpec((ROWS, width), lambda i: (i, 0))
    return pl.pallas_call(
        first_back_kernel,
        grid=(length // ROWS,),
        in_specs=[
            pl.BlockSpec((3, ROWS, part.shape[2]), lambda i: (0, i, 0)) for part in (left, right)
        ]
        + [rows, rows, const(1, width)]
        + [const(width, width)] * 3,
        out_specs=[rows, const(2, width)],
        out_shape=[
            jax.ShapeDtypeStruct((length, width), F32),
            jax.ShapeDtypeStruct((2, width), F32),
        ],
        cost_estimate=LIGHT,
        name="first_back",
    )(left, right, tokens, resid, gain, *weights)


def layer_out_kernel(wide_ref, rows_ref, resid_ref, gate_ref, out_ref):
    out_ref[...] = (resid_ref[...] + gate_ref[...] * gathered(wide_ref, rows_ref)).astype(BF16)


def layer_output(wide, produced, resid, gate):
    length, width = resid.shape
    rows = pl.BlockSpec((ROWS, width), lambda i: (i, 0))
    return pl.pallas_call(
        layer_out_kernel,
        grid=(length // ROWS,),
        in_specs=[
            pl.BlockSpec((ROWS, LANES), lambda i: (i, 0)),
            const(*produced.shape),
            rows,
            pl.BlockSpec((ROWS, 1), lambda i: (i, 0)),
        ],
        out_specs=rows,
        out_shape=jax.ShapeDtypeStruct((length, width), BF16),
        cost_estimate=LIGHT,
        name="layer_output",
    )(wide, produced, resid, gate)


def assemble_kernel(core_ref, mine_ref, other_ref, *outs, whole):
    outs = outs[-4:] if whole else outs[-3:]

    def write(parts):
        for unit in range(whole):
            outs[0][:, unit * LANES : (unit + 1) * LANES] = parts[unit].astype(F32)
        for unit in range(whole, parts.shape[0]):
            pair, matrix = divmod(unit - whole, 3)
            out = outs[matrix - 3]
            out[:, pair * LANES : (pair + 1) * LANES] = parts[unit].astype(F32)

    mine = pl.program_id(0) == core_ref[0]

    @pl.when(mine)
    def _():
        write(mine_ref)

    @pl.when(jnp.logical_not(mine))
    def _():
        write(other_ref)


def assemble(core, mine, other, width, outs):
    mine, other = (part.reshape(-1, width // 2, LANES) for part in (mine, other))
    whole = 0 if outs else width // LANES
    columns = (mine.shape[0] - whole) // 3 * LANES
    out = jax.ShapeDtypeStruct((width, width), F32)
    specs = [pl.BlockSpec((width // 2, columns), lambda i, core: (i, 1 if outs else 0))] * 3
    if whole:
        specs = [pl.BlockSpec((width // 2, width), lambda i, core: (i, 0))] + specs
    return pl.pallas_call(
        functools.partial(assemble_kernel, whole=whole),
        grid_spec=pltpu.PrefetchScalarGridSpec(
            num_scalar_prefetch=1,
            grid=(2,),
            in_specs=[const(*mine.shape)] * 2
            + [pl.BlockSpec(memory_space=pl.ANY)] * len(outs),
            out_specs=specs,
        ),
        out_shape=[out] * len(specs),
        input_output_aliases={3 + index: index for index in range(len(outs))},
        cost_estimate=LIGHT,
        name="assemble",
    )(core, mine, other, *outs)


def swap(value, axis, bit):
    size = lax.axis_size(axis)
    return lax.ppermute(value, axis, [(i, i ^ bit) for i in range(size)])


def stages(axis, low, high):
    found = []
    bit = low
    while bit < min(high, lax.axis_size(axis)):
        found.append((axis, bit))
        bit *= 2
    return found


def bit_of(axis, bit):
    return (lax.axis_index(axis) // bit) % 2


def add_low(left, right):
    return (left.astype(F32) + right.astype(F32)).astype(BF16)


def add(left, right):
    return left + right


def halves(rows, stage):
    axis, bit = stage
    half = rows.shape[0] // 2
    mine = bit_of(axis, bit)
    return (
        lax.dynamic_slice_in_dim(rows, (1 - mine) * half, half, 0),
        lax.dynamic_slice_in_dim(rows, mine * half, half, 0),
    )


def joined(rows, other, stage):
    first = bit_of(*stage) == 0
    return jnp.concatenate([jnp.where(first, rows, other), jnp.where(first, other, rows)], axis=0)


def add_split_kernel(mine_ref, left_ref, right_ref, send_ref, keep_ref):
    value = add_low(left_ref[...], right_ref[...])

    @pl.when(pl.program_id(0) == 0)
    def _():
        send_ref[...] = value

    @pl.when(pl.program_id(0) == 1)
    def _():
        keep_ref[...] = value


def add_split(left, right, stage):
    half, width = left.shape[0] // 2, left.shape[1]
    if half % 8:
        return halves(add_low(left, right), stage)
    mine = bit_of(*stage).astype(jnp.int32)[None]
    block = pl.BlockSpec((half, width), lambda i, mine: (jnp.where(i == 0, 1 - mine[0], mine[0]), 0))
    out = pl.BlockSpec((half, width), lambda i, mine: (0, 0))
    shape = jax.ShapeDtypeStruct((half, width), BF16)
    return pl.pallas_call(
        add_split_kernel,
        grid_spec=pltpu.PrefetchScalarGridSpec(
            num_scalar_prefetch=1,
            grid=(2,),
            in_specs=[block, block],
            out_specs=[out, out],
        ),
        out_shape=[shape, shape],
        cost_estimate=LIGHT,
        name="add_split",
    )(mine, left, right)


def halves_sum(left, right, stage):
    width = left.shape[2]
    parts = add_split(left.reshape(-1, width), right.reshape(-1, width), stage)
    return [part.reshape(-1, *left.shape[1:]) for part in parts]


class Sum:
    def __init__(self, keep, send, stages, plus=add_low, split=True, shared=True):
        self.keep, self.send, self.plus, self.shared = keep, send, plus, shared
        if split:
            self.steps = [("whole", stages[0])]
            self.steps += [("halve", stage) for stage in stages[1:-1]]
            self.steps += [("whole", stages[-1])]
            self.steps += [("join", stage) for stage in stages[-2:2:-1]]
            self.steps += [("both", stages[2:0:-1]), ("corner", stages[2:0:-1])]
        else:
            self.steps = [("whole", stage) for stage in stages]

    def start(self):
        kind, stage = self.steps[0]
        if kind == "both":
            return [swap(self.keep, *each) for each in stage]
        if kind == "corner":
            near, far = self.got
            if not self.shared:
                return [swap(near, *stage[1])]
            half = near.shape[0] // 2
            return [swap(near[:half], *stage[1]), swap(far[half:], *stage[0])]
        return [swap(self.send, *stage)]

    def finish(self, got):
        kind, stage = self.steps.pop(0)
        if kind == "both":
            self.got = got
        elif kind == "corner":
            near, far = self.got
            mine = joined(self.keep, near, stage[0])
            corner = jnp.concatenate(got, axis=0) if self.shared else got[0]
            other = joined(far, corner, stage[0])
            self.keep = joined(mine, other, stage[1])
        elif self.steps and self.steps[0][0] == "halve":
            self.send, self.keep = add_split(self.keep, got[0], self.steps[0][1])
        else:
            join = functools.partial(joined, stage=stage)
            self.keep = self.send = (join if kind == "join" else self.plus)(self.keep, got[0])


def advance(sums, *others):
    sums = [each for each in sums if each.steps]
    got, others = tie(([each.start() for each in sums], others))
    for each, arrived in zip(sums, got):
        each.finish(arrived)
    return others[0] if len(others) == 1 else others


def chip_stages(total):
    return [("dp", 2 << index) for index in range((total.shape[0]).bit_length() - 1)][::-1]


tie = lax.optimization_barrier


def exchange(rows):
    return lax.all_to_all(rows, "expert", split_axis=0, concat_axis=0, tiled=True)


def local(
    tokens,
    routing,
    query_weight,
    key_weight,
    value_weight,
    output_weight,
    first_gain,
    first_bias,
    second_gain,
    second_bias,
    centroids,
    expert_up,
    expert_down,
    cotangent,
):
    length, width = tokens.shape
    experts = centroids.shape[0]
    capacity = length // experts
    peers = lax.axis_size("expert")
    parts = lax.axis_size("dp")
    slots = experts * capacity
    core = (lax.axis_index("dp") % 2).astype(jnp.int32)[None]
    vectors = tie(jnp.stack([first_gain, first_bias, second_gain, second_bias]))
    first_gain, first_bias, second_gain, second_bias = (vectors[i : i + 1] for i in range(4))
    weights = (query_weight, key_weight, value_weight)

    cots, slot, wide = route(routing.reshape(1, length), cotangent, experts, capacity)
    cots, tokens = tie((cots, tokens))
    cots = exchange(cots.reshape(peers, -1, width)).reshape(slots, width)

    queries, keys, values, mixed, probs = attention(tokens, first_gain, first_bias, weights)
    resid, rows = branch(mixed, tokens, output_weight, second_gain, second_bias, slot, slots)

    rows, cots = tie((rows, cots))
    rows = exchange(rows.reshape(peers, -1, width))
    cots_down = expert_cots(cots, expert_down)
    settled = settle(
        tokens, first_gain, first_bias, mixed, resid, second_gain, second_bias, centroids, routing
    )
    rows, cots_down, *settled = tie((rows, cots_down, *settled))
    normed_turned, mixed_turned, xhat, scale, gate = settled
    rows = rows.reshape(slots, width)
    own = centroids[lax.axis_index("expert")][None, :]
    produced, returned, grad_rows, hidden, grad_pre = expert(
        rows, cots, cots_down, own, expert_up, expert_down
    )
    returned = exchange(returned.reshape(peers, -1, width))
    up_send, down_send, up_keep, down_keep = expert_weights(
        rows, grad_rows, hidden, grad_pre, parts, core
    )
    chips = chip_stages(up_send)
    up_send, up_keep = halves_sum(up_keep, swap(up_send, "dp", 1), chips[0])
    down_send, down_keep = halves_sum(down_keep, swap(down_send, "dp", 1), chips[0])
    returned, produced, up_send, up_keep, down_send, down_keep = tie(
        (returned, produced, up_send, up_keep, down_send, down_keep)
    )
    returned = returned.reshape(slots, width)
    up_got = swap(up_send, *chips[0])
    down_got = swap(down_send, *chips[0])
    produced = exchange(produced.reshape(peers, -1, width))

    pairs = width // LANES
    split = pairs // 2
    grad_resid, grad_mixed, second_sums, *units = second_back(
        core, wide, returned, xhat, scale, cotangent, second_gain, output_weight, mixed_turned,
        pairs + 3 * split,
    )

    cross = stages("expert", 1, 1 << 20)
    apart = stages("dp", 2, 1 << 20)
    back = functools.partial(
        attention_back, core, queries, keys, values, grad_mixed, mixed, normed_turned
    )
    left, send, keep = back(probs, 0, split, units)
    left, send, keep, up_got = tie((left, send, keep, up_got))
    early = Sum(keep.reshape(-1, LANES), send.reshape(-1, LANES), [("dp", 1)] + cross + apart)
    advance([early])
    early.send, *probs = tie((early.send, *probs))
    right, send, keep = back(probs, split, pairs - split, None)
    right, send, keep, produced = advance([early], right, send, keep, produced)
    produced = produced.reshape(slots, width)
    order = [("dp", 1)] + apart + cross[1:2] + cross[:1] + cross[2:]
    late = Sum(keep.reshape(-1, LANES), send.reshape(-1, LANES), order, shared=False)
    layer_out = layer_output(wide, produced, resid, gate)
    layer_out, down_got = advance([early, late], layer_out, down_got)
    grad_tokens, first_sums = first_back(left, right, tokens, grad_resid, first_gain, weights)
    grad_tokens, first_sums = advance([early, late], grad_tokens, first_sums)
    grad_up = up_keep.astype(F32) + up_got.astype(F32)
    grad_down = down_keep.astype(F32) + down_got.astype(F32)
    for stage in chips[1:]:
        grad_up, grad_down = (
            keep.astype(F32) + swap(send, *stage).astype(F32)
            for send, keep in (halves(value.astype(BF16), stage) for value in (grad_up, grad_down))
        )
    grad_up, grad_down = (value.reshape(value.shape[1:])[None] for value in (grad_up, grad_down))
    small = jnp.concatenate([first_sums, second_sums], axis=0)
    small = Sum(small, small, stages("dp", 1, 1 << 20) + cross, plus=add, split=False)
    while len(early.steps) > 2:
        advance([early, late, small])
    grad_up, grad_down = advance([early, late, small], grad_up, grad_down)
    while early.steps:
        advance([early, late, small])
    core_swap = swap(early.keep, "dp", 1)
    while len(late.steps) > 1:
        core_swap = advance([late, small], core_swap)
    outs = assemble(core, early.keep, core_swap, width, [])
    grad_output, *outs = advance([late, small], *outs)
    while small.steps:
        advance([small])
    grad_query, grad_key, grad_value = assemble(
        core, late.keep, swap(late.keep, "dp", 1), width, outs
    )
    small = small.keep
    return (
        layer_out,
        grad_tokens,
        grad_query,
        grad_key,
        grad_value,
        grad_output,
        small[0],
        small[1],
        small[2],
        small[3],
        grad_up,
        grad_down,
    )


def solution(mesh):
    rows = P(("dp", "expert"), None)
    return jax.shard_map(
        local,
        mesh=mesh,
        in_specs=(rows, rows)
        + (P(),) * 9
        + (P("expert", None, None), P("expert", None, None), rows),
        out_specs=(rows, rows) + (P(),) * 8 + (P("expert", None, "dp"), P("expert", "dp", None)),
        check_vma=False,
    )
```
